32 devices in a mesh: section: 2 (over core), dp: 16 (over z, y, x).
Axes of the slice: x: 2, y: 2, z: 4, core: 2. Of those that a mesh axis runs over, the one named last changes fastest.
Arguments:
- byte_states: bfloat16 [32768, 768], P('dp'), may hold values from -6 to 6
- lengths: int32 [32], P('dp'), may hold values from 512 to 1024, as said below
- patch_weight: bfloat16 [6144, 768], replicated, may hold values from -0.078125 to 0.078125
- qkv_weight: bfloat16 [2, 768, 2304], P('section'), may hold values from -0.21875 to 0.21875
- out_weight: bfloat16 [2, 768, 768], P('section'), may hold values from -0.875 to 0.875
- up_weight: bfloat16 [2, 768, 3072], P('section'), may hold values from -0.21875 to 0.21875
- down_weight: bfloat16 [2, 3072, 768], P('section'), may hold values from -0.109375 to 0.109375
- norm_gains: float32 [2, 2, 768], P('section'), may hold values from 0.25 to 1.75
- byte_cotangent: bfloat16 [32768, 768], P('dp'), may hold values from -6 to 6
Outputs:
- section_outputs: bfloat16 [2, 32768, 768], P('section', 'dp')
- input_grad: float32 [32768, 768], P('dp')
- patch_grad: float32 [6144, 768], P(('section', 'dp'))
- qkv_grad: float32 [2, 768, 2304], P('section', 'dp')
- proj_grad: float32 [2, 768, 768], P('section', 'dp')
- up_grad: float32 [2, 768, 3072], P('section', 'dp')
- down_grad: float32 [2, 3072, 768], P('section', 'dp')
- gain_grad: float32 [2, 2, 768], P('section', None, 'dp')
The draws below stay inside these ranges and needn't reach their ends.
Inputs may be any that keep to these rules, and one draw needn't show every extreme that they name: `lengths`: each a multiple of 8; some sequence has all 1024 bytes live in every draw.
All inputs are finite; a program needn't handle non-finite values.
Results may differ from the reference program's by a relative error of at most 0.02.
Values may be sent and summed in bfloat16 or wider, within the bound.
A program may use at most 384 MiB of HBM per device.

```python
import jax
import jax.numpy as jnp
from jax import lax

D = 768
HEADS = 12
HDIM = 64
FF = 3072
PATCH = 8
SEQ = 1024
SEQS = 32
TOKENS = 32768


def draw_lengths(key, part):
    first_key, second_key = jax.random.split(jax.random.fold_in(key, 11))
    base = jax.random.randint(first_key, (SEQS,), SEQ // (2 * PATCH), SEQ // PATCH + 1) * PATCH
    chosen = jax.random.randint(second_key, (), 0, SEQS)
    return jnp.where(jnp.arange(SEQS) == chosen, SEQ, base).astype(jnp.int32)


def steps_of(stream_key, dims, cuts, low, high):
    gain, own = 1.0, jax.random.fold_in(stream_key, 6)
    for position, blocks in cuts:
        heights = jnp.exp(jax.random.uniform(jax.random.fold_in(own, position), (blocks,), jnp.float32, low / len(cuts), high / len(cuts)))
        gain = gain * jnp.repeat(heights, dims[position] // blocks).reshape([-1 if axis == position else 1 for axis in range(len(dims))])
    return gain


def bell_draw(stream_key, shape, width, most, shards=(), kind=jnp.bfloat16):
    entries = width * jax.random.normal(stream_key, shape, jnp.float32)
    if shards:
        entries = entries * steps_of(stream_key, shape, shards, -0.22, 0.18)
    return jnp.clip(entries, -most, most).astype(kind)


def setup_inputs(seed: int = 0) -> dict:
    key_of = jax.random.split(jax.random.key(seed), 10)
    return {
        "byte_states": bell_draw(key_of[0], (TOKENS, D), 1.0, 6.0, ((0, 16),)),
        "lengths": draw_lengths(jax.random.fold_in(key_of[9], 71), 0),
        "patch_weight": bell_draw(key_of[2], (PATCH * D, D), (PATCH * D) ** -0.5, 0.078125),
        "qkv_weight": bell_draw(key_of[3], (2, D, 3 * D), D ** -0.5, 0.21875, ((0, 2),)),
        "out_weight": bell_draw(key_of[4], (2, D, D), (D // 16) ** -0.5, 0.875, ((0, 2),)),
        "up_weight": bell_draw(key_of[5], (2, D, FF), D ** -0.5, 0.21875, ((0, 2),)),
        "down_weight": bell_draw(key_of[6], (2, FF, D), FF ** -0.5, 0.109375, ((0, 2),)),
        "norm_gains": jnp.clip(1.0 + 0.15 * jax.random.normal(key_of[7], (2, 2, D), jnp.float32), 0.25, 1.75),
        "byte_cotangent": bell_draw(key_of[8], (TOKENS, D), 1.0, 6.0, ((0, 16),)),
    }


@jax.custom_vjp
def low(v):
    return lax.optimization_barrier(v.astype(jnp.bfloat16)).astype(jnp.float32)

@jax.custom_vjp
def low_back(v):
    return v

def low_keep(v):
    return (low(v), None)

def low_pass(kept, grad):
    return (grad,)

def back_keep(v):
    return (v, None)

def back_low(kept, grad):
    return (low(grad),)
low.defvjp(low_keep, low_pass)
low_back.defvjp(back_keep, back_low)

def dense(left, right):
    return jnp.dot(left, right, precision=lax.Precision.HIGHEST)

def normalize(hidden):
    row_mean = lax.optimization_barrier(jnp.mean(hidden, axis=-1, keepdims=True))
    centered = hidden - row_mean
    row_var = lax.optimization_barrier(jnp.mean(centered * centered, axis=-1, keepdims=True))
    return centered * lax.rsqrt(row_var + 1e-05)

def attend(query, keys, values):
    scores = jnp.einsum('blhe,bmhe->bhlm', query, keys, precision=lax.Precision.HIGHEST) * HDIM ** (-0.5)
    scores = low_back(scores)
    key_count = query.shape[1]
    allowed = jnp.arange(key_count)[:, None] >= jnp.arange(key_count)[None, :]
    weights = low(jax.nn.softmax(jnp.where(allowed, scores, -1e+30), axis=-1))
    return jnp.einsum('bhlm,bmhe->blhe', weights, values, precision=lax.Precision.HIGHEST)

def layer(hidden, w_qkv, w_out, w_up, w_down, gains, groups):
    row_count = hidden.shape[0]
    normed = low(normalize(hidden) * gains[0])
    qkv = low(low_back(dense(normed, w_qkv)))
    qkv = qkv.reshape(groups, row_count // groups, 3, HEADS, HDIM)
    attended = attend(qkv[:, :, 0], qkv[:, :, 1], qkv[:, :, 2]).reshape(row_count, D)
    attended = low(low_back(attended))
    middle = hidden + low_back(dense(attended, w_out))
    normed_two = low(normalize(middle) * gains[1])
    pre_act = low_back(dense(normed_two, w_up))
    branch = low_back(dense(low(jax.nn.gelu(pre_act, approximate=False)), w_down))
    return middle + branch

def reference(byte_states, lengths, patch_weight, qkv_weight, out_weight, up_weight, down_weight, norm_gains, byte_cotangent):
    inputs = byte_states.astype(jnp.float32).reshape(SEQS, SEQ, D)
    params = (patch_weight.astype(jnp.float32), qkv_weight.astype(jnp.float32), out_weight.astype(jnp.float32), up_weight.astype(jnp.float32), down_weight.astype(jnp.float32), norm_gains.astype(jnp.float32))

    def forward(inputs, params):
        w_patch, w_qkv, w_out, w_up, w_down, gains = params

        def single(item):
            seq_input, seq_length = item
            patches = seq_input.reshape(SEQ // PATCH, PATCH * D)
            projected = low_back(dense(patches, w_patch))
            shifted = jnp.concatenate([jnp.zeros((1, D), jnp.float32), projected[:-1]], axis=0)
            glob = layer(shifted, w_qkv[0], w_out[0], w_up[0], w_down[0], gains[0], 1)
            glob = low(low_back(glob))
            spread = jnp.repeat(glob, PATCH, axis=0)
            local = layer(seq_input + spread, w_qkv[1], w_out[1], w_up[1], w_down[1], gains[1], SEQ // PATCH)
            live = (jnp.arange(SEQ) < seq_length).astype(jnp.float32)[:, None]
            return (spread, local * live)
        return lax.map(jax.checkpoint(single), (inputs, lengths))
    outputs, pullback = jax.vjp(forward, inputs, params)
    spread_all, local_all = outputs
    cotangent = (jnp.zeros_like(spread_all), byte_cotangent.astype(jnp.float32).reshape(SEQS, SEQ, D))
    grad_inputs, grad_params = pullback(cotangent)
    section_outputs = jnp.stack([spread_all.reshape(TOKENS, D), local_all.reshape(TOKENS, D)]).astype(jnp.bfloat16)
    input_grad = grad_inputs.reshape(TOKENS, D)
    return (section_outputs, input_grad, grad_params[0], grad_params[1], grad_params[2], grad_params[3], grad_params[4], grad_params[5])
```

```python
import functools

import jax
import jax.numpy as jnp
from jax import lax
from jax.experimental import pallas as pl
from jax.experimental.pallas import tpu as pltpu
from jax.sharding import PartitionSpec as P

D = 768
HEADS = 12
HDIM = 64
FF = 3072
PATCH = 8
SEQ = 1024
PATCHES = SEQ // PATCH
TILE = 256
SUBS = TILE // 128
PAIRS = HEADS // 2
TILES = SEQ // TILE
MB = 2
XG = 3 * D + FF
F32 = jnp.float32
BF16 = jnp.bfloat16
ANY = pl.BlockSpec(memory_space=pl.ANY)
VLIMIT = 56 * 2**20


def sds(shape, dtype):
    return jax.ShapeDtypeStruct(shape, dtype)


def mm(a, b):
    return jnp.dot(a, b, preferred_element_type=F32)


def mm_nt(a, b):
    return lax.dot_general(a, b, (((1,), (1,)), ((), ())), preferred_element_type=F32)


def mm_tn(a, b):
    return lax.dot_general(a, b, (((0,), (0,)), ((), ())), preferred_element_type=F32)


def normalized(v):
    centered = v - jnp.mean(v, axis=-1, keepdims=True)
    scale = lax.rsqrt(jnp.mean(centered * centered, axis=-1, keepdims=True) + 1e-5)
    return centered * scale, scale


def norm_backward(grad, gain, hat, scale):
    scaled = grad * gain
    inner = scaled - jnp.mean(scaled, axis=-1, keepdims=True)
    inner = inner - hat * jnp.mean(scaled * hat, axis=-1, keepdims=True)
    return inner * scale, jnp.sum(grad * hat, axis=0, keepdims=True)


def gelu_pair(z):
    t = 1.0 / (1.0 + 0.3275911 * 0.7071067811865476 * jnp.abs(z))
    bell = jnp.exp(-0.5 * z * z)
    poly = 1.061405429 * t - 1.453152027
    poly = poly * t + 1.421413741
    poly = poly * t - 0.284496736
    poly = poly * t + 0.254829592
    half_tail = 0.5 * poly * t * bell
    cdf = jnp.where(z >= 0, 1.0 - half_tail, half_tail)
    return z * cdf, cdf + z * bell * 0.3989422804014327


def lane_masks():
    lane = lax.broadcasted_iota(jnp.int32, (128, 128), 1)
    first = jnp.where(lane < HDIM, 1.0, 0.0)
    return first.astype(BF16), (1.0 - first).astype(BF16), lane < HDIM


def split_heads(v, first, second):
    return jnp.concatenate([v * first, v * second], axis=0)


def attention_forward(qkv_ref, o_ref, p_ref, shift):
    first, second, _ = lane_masks()
    row = lax.broadcasted_iota(jnp.int32, (128, 256), 0)
    col = lax.broadcasted_iota(jnp.int32, (128, 256), 1) & 127
    allowed = (col <= row) & ((col >> shift) == (row >> shift))
    for sub in range(SUBS):
        rows = slice(sub * 128, sub * 128 + 128)
        for pair in range(PAIRS):
            lo = pair * 128
            q = qkv_ref[rows, lo : lo + 128]
            k2 = split_heads(qkv_ref[rows, D + lo : D + lo + 128], first, second)
            v2 = split_heads(qkv_ref[rows, 2 * D + lo : 2 * D + lo + 128], first, second)
            s = jnp.where(allowed, mm_nt(q, k2) * 0.125, -1e30)
            parts = []
            for half in range(2):
                sh = s[:, half * 128 : half * 128 + 128]
                e = jnp.exp(sh - jnp.max(sh, axis=-1, keepdims=True))
                parts.append(e / jnp.sum(e, axis=-1, keepdims=True))
            p = jnp.concatenate(parts, axis=1).astype(BF16)
            p_ref[sub, pair] = p
            o_ref[rows, lo : lo + 128] = mm(p, v2).astype(BF16)


def attention_backward(qkv_ref, p_ref, do_ref, dqkv_ref):
    first, second, is_first = lane_masks()
    for sub in range(SUBS):
        rows = slice(sub * 128, sub * 128 + 128)
        for pair in range(PAIRS):
            lo = pair * 128
            q = qkv_ref[rows, lo : lo + 128]
            k2 = split_heads(qkv_ref[rows, D + lo : D + lo + 128], first, second)
            v2 = split_heads(qkv_ref[rows, 2 * D + lo : 2 * D + lo + 128], first, second)
            do = do_ref[rows, lo : lo + 128]
            p = p_ref[sub, pair]
            dp = mm_nt(do, v2)
            pf = p.astype(F32)
            weighted = pf * dp
            parts = []
            for half in range(2):
                cols = slice(half * 128, half * 128 + 128)
                total = jnp.sum(weighted[:, cols], axis=-1, keepdims=True)
                parts.append(weighted[:, cols] - pf[:, cols] * total)
            ds = jnp.concatenate(parts, axis=1).astype(BF16)
            dq = mm(ds, k2) * 0.125
            dk2 = mm_tn(ds, q) * 0.125
            dv2 = mm_tn(p, do)
            dk = jnp.where(is_first, dk2[:128], dk2[128:])
            dv = jnp.where(is_first, dv2[:128], dv2[128:])
            dqkv_ref[rows, lo : lo + 128] = dq.astype(BF16)
            dqkv_ref[rows, D + lo : D + lo + 128] = dk.astype(BF16)
            dqkv_ref[rows, 2 * D + lo : 2 * D + lo + 128] = dv.astype(BF16)


def block_forward(h, gains, w, wait, shift, a_ref, qkv_ref, p_ref, o_ref, mid_ref, c_ref, u_ref, gp_ref):
    wq, wo, wu, wd = w
    a_ref[...] = (normalized(h)[0] * gains[0:1, :]).astype(BF16)
    wait(0)
    for part in range(3):
        cols = slice(part * D, part * D + D)
        qkv_ref[:, cols] = mm(a_ref[...], wq[:, cols]).astype(BF16)
    attention_forward(qkv_ref, o_ref, p_ref, shift)
    wait(1)
    mid = h + mm(o_ref[...], wo[...])
    mid_ref[...] = mid
    c_ref[...] = (normalized(mid)[0] * gains[1:2, :]).astype(BF16)
    wait(2)
    for part in range(FF // D):
        cols = slice(part * D, part * D + D)
        u, gp = gelu_pair(mm(c_ref[...], wu[:, cols]))
        u_ref[:, cols] = u.astype(BF16)
        gp_ref[:, cols] = gp.astype(BF16)
    wait(3)
    return mid_ref[...] + mm(u_ref[...], wd[...])


def block_backward(dout, h, gains, w, wait, dz_ref, mid_ref, qkv_ref, p_ref, do_ref, dr_ref, dqkv_ref):
    wq, wo, wu = w
    hat, scale = normalized(mid_ref[...])
    wait(2)
    dc = mm_nt(dz_ref[...], wu[...])
    back, dgain_two = norm_backward(dc, gains[1:2, :], hat, scale)
    dmid = dout + back
    dr_ref[...] = dmid.astype(BF16)
    wait(1)
    do_ref[...] = mm_nt(dr_ref[...], wo[...]).astype(BF16)
    attention_backward(qkv_ref, p_ref, do_ref, dqkv_ref)
    wait(0)
    da = mm_nt(dqkv_ref[...], wq[...])
    hat, scale = normalized(h)
    back, dgain_one = norm_backward(da, gains[0:1, :], hat, scale)
    return dmid + back, jnp.concatenate([dgain_one, dgain_two], axis=0)


LANES = D // 128


def fill_lanes(dst, src):
    for b in range(LANES):
        dst[b] = src[:, b * 128 : b * 128 + 128].astype(F32)


def strided_rows(ref, start, rows):
    picked = [ref[b, pl.ds(start, rows, stride=PATCH), :] for b in range(LANES)]
    return jnp.concatenate(picked, axis=1)


def spread_matrix():
    row = lax.broadcasted_iota(jnp.int32, (TILE, TILE // PATCH), 0) // PATCH
    col = lax.broadcasted_iota(jnp.int32, (TILE, TILE // PATCH), 1)
    return jnp.where(row == col, 1.0, 0.0).astype(BF16)


def cost(flops, nbytes):
    return pl.CostEstimate(flops=int(flops), bytes_accessed=int(nbytes), transcendentals=0)


WSCRATCH = {
    "q": pltpu.VMEM((D, 3 * D), BF16),
    "o": pltpu.VMEM((D, D), BF16),
    "u": pltpu.VMEM((D, FF), BF16),
    "d": pltpu.VMEM((FF, D), BF16),
}


def global_forward_kernel(
    scal, bytes_ref, gains_ref, wp_hbm, wq_hbm, wo_hbm, wu_hbm, wd_hbm,
    g_ref, x_ref, start_ref, qkv_ref, p_ref, mid_ref, gp_ref,
    bytes_f32, wp, wq, wo, wu, wd, psem, wsem,
):
    @pl.when(scal[0] == 0)
    def _():
        pcopies = [
            pltpu.make_async_copy(wp_hbm.at[pl.ds(j * D, D)], wp.at[pl.ds(j * D, D)], psem.at[j])
            for j in range(PATCH)
        ]
        wcopies = [
            pltpu.make_async_copy(src.at[0], dst, wsem.at[i])
            for i, (src, dst) in enumerate(((wq_hbm, wq), (wo_hbm, wo), (wu_hbm, wu), (wd_hbm, wd)))
        ]
        for copy in pcopies + wcopies:
            copy.start()
        fill_lanes(bytes_f32, bytes_ref)
        rows = MB * PATCHES
        acc = jnp.zeros((rows, D), F32)
        for j in range(PATCH):
            xj = strided_rows(bytes_f32, j, rows).astype(BF16)
            pcopies[j].wait()
            acc = acc + mm(xj, wp[j * D : j * D + D, :])
        moved = pltpu.roll(acc, 1, 0)
        row = lax.broadcasted_iota(jnp.int32, (rows, D), 0)
        start_ref[...] = jnp.where((row & (PATCHES - 1)) == 0, 0.0, moved)
        out = block_forward(
            start_ref[...], gains_ref[0], (wq, wo, wu, wd), lambda i: wcopies[i].wait(), 7,
            x_ref.at[:, 0:D], qkv_ref, p_ref, x_ref.at[:, D : 2 * D], mid_ref,
            x_ref.at[:, 2 * D : 3 * D], x_ref.at[:, 3 * D : 3 * D + FF], gp_ref,
        )
        g_ref[...] = out.astype(BF16)


def global_forward(scal, states, gains, patch_weight, weights):
    rows = MB * PATCHES
    full = lambda *shape: pl.BlockSpec(shape, lambda i, s: (0,) * len(shape), pipeline_mode=pl.Buffered(1))
    outs = (
        ((rows, D), BF16), ((rows, XG), BF16), ((rows, D), F32), ((rows, 3 * D), BF16),
        ((SUBS, PAIRS, 128, 256), BF16), ((rows, D), F32), ((rows, FF), BF16),
    )
    return pl.pallas_call(
        global_forward_kernel,
        name="global_forward",
        out_shape=[sds(*o) for o in outs],
        grid_spec=pltpu.PrefetchScalarGridSpec(
            num_scalar_prefetch=1,
            grid=(1,),
            in_specs=[full(MB * SEQ, D), full(1, 2, D)] + [ANY] * 5,
            out_specs=[full(*o[0]) for o in outs],
            scratch_shapes=[
                pltpu.VMEM((LANES, MB * SEQ, 128), F32), pltpu.VMEM((PATCH * D, D), BF16),
                WSCRATCH["q"], WSCRATCH["o"], WSCRATCH["u"], WSCRATCH["d"],
                pltpu.SemaphoreType.DMA((PATCH,)), pltpu.SemaphoreType.DMA((4,)),
            ],
        ),
        compiler_params=pltpu.CompilerParams(vmem_limit_bytes=VLIMIT),
        cost_estimate=cost(6e9, 32e6),
    )(scal, states, gains, patch_weight, *weights)


def global_backward_kernel(
    scal, dg0_ref, dg1_ref, start_ref, mid_ref, qkv_ref, p_ref, gp_ref, gains_ref, wq_hbm, wo_hbm, wu_hbm, wd_hbm,
    dpp_ref, keep_ref, send_ref, dgain_ref,
    dm_s, dz_s, do_s, dr_s, dqkv_s, wq, wo, wu, wd, wsem,
):
    @pl.when(scal[0] == 0)
    def _():
        rows = MB * PATCHES
        wcopies = [
            pltpu.make_async_copy(src.at[0], dst, wsem.at[i])
            for i, (src, dst) in enumerate(((wq_hbm, wq), (wo_hbm, wo), (wu_hbm, wu), (wd_hbm, wd)))
        ]
        for i in (3, 2, 1, 0):
            wcopies[i].start()
        dm_s[0:PATCHES, :] = dg0_ref[...]
        dm_s[PATCHES:, :] = dg1_ref[...]
        wcopies[3].wait()
        for part in range(FF // D):
            cols = slice(part * D, part * D + D)
            du = mm_nt(dm_s[...], wd[cols, :])
            dz_s[:, cols] = (du * gp_ref[:, cols].astype(F32)).astype(BF16)
        dh, dgain = block_backward(
            dm_s[...].astype(F32), start_ref[...], gains_ref[0], (wq, wo, wu), lambda i: wcopies[i].wait(),
            dz_s, mid_ref, qkv_ref, p_ref, do_s, dr_s, dqkv_s,
        )
        dgain_ref[...] = jnp.zeros_like(dgain_ref)
        dgain_ref[0:2, :] = dgain
        moved = pltpu.roll(dh, rows - 1, 0)
        row = lax.broadcasted_iota(jnp.int32, (rows, D), 0)
        dpp_ref[...] = jnp.where((row & (PATCHES - 1)) == PATCHES - 1, 0.0, moved).astype(BF16)
        for half in range(2):
            def fill(ref):
                lo = 0
                for src, width in ((dqkv_s, 3 * D // 2), (dr_s, D // 2), (dz_s, FF // 2), (dm_s, D // 2)):
                    ref[:, lo : lo + width] = src[:, half * width : half * width + width]
                    lo += width
            pl.when(scal[1] == half)(functools.partial(fill, keep_ref))
            pl.when(scal[1] != half)(functools.partial(fill, send_ref))

    @pl.when(scal[0] != 0)
    def _():
        dgain_ref[...] = jnp.zeros_like(dgain_ref)


def global_backward(scal, dgs, saved, gains, weights):
    rows = MB * PATCHES
    full = lambda *shape: pl.BlockSpec(shape, lambda i, s: (0,) * len(shape), pipeline_mode=pl.Buffered(1))
    width = (3 * D + D + FF + D) // 2
    outs = (((rows, D), BF16), ((rows, width), BF16), ((rows, width), BF16), ((8, D), F32))
    return pl.pallas_call(
        global_backward_kernel,
        name="global_backward",
        out_shape=[sds(*o) for o in outs],
        grid_spec=pltpu.PrefetchScalarGridSpec(
            num_scalar_prefetch=1,
            grid=(1,),
            in_specs=[full(PATCHES, D)] * 2 + [full(*v.shape) for v in saved] + [full(1, 2, D)] + [ANY] * 4,
            out_specs=[full(*o[0]) for o in outs],
            scratch_shapes=[
                pltpu.VMEM((rows, D), BF16), pltpu.VMEM((rows, FF), BF16), pltpu.VMEM((rows, D), BF16),
                pltpu.VMEM((rows, D), BF16), pltpu.VMEM((rows, 3 * D), BF16),
                WSCRATCH["q"], WSCRATCH["o"], WSCRATCH["u"], WSCRATCH["d"],
                pltpu.SemaphoreType.DMA((4,)),
            ],
        ),
        compiler_params=pltpu.CompilerParams(vmem_limit_bytes=VLIMIT),
        cost_estimate=cost(6e9, 24e6),
    )(scal, *dgs, *saved, gains, *weights)


def start_weights(scal, pairs, sems, order):
    step = pl.program_id(0)
    for i in order:
        own, recv, dst = pairs[i]

        @pl.when((step == 0) & (scal[0] == 1))
        def _(own=own, dst=dst, i=i):
            pltpu.make_async_copy(own.at[0], dst, sems.at[i]).start()

        @pl.when((step == 0) & (scal[0] == 0))
        def _(recv=recv, dst=dst, i=i):
            pltpu.make_async_copy(recv.at[0], dst, sems.at[i]).start()

    def wait(i):
        @pl.when(step == 0)
        def _():
            pltpu.make_async_copy(pairs[i][1].at[0], pairs[i][2], sems.at[i]).wait()

    return wait


def live_rows(scal):
    step = pl.program_id(0)
    row = lax.broadcasted_iota(jnp.int32, (TILE, D), 0) + step * TILE
    return row < scal[4]


def local_forward_kernel(
    scal, bytes_ref, cot_ref, g_ref, gains_ref, wq_a, wo_a, wu_a, wd_a, wq_b, wo_b, wu_b, wd_b, gains_b,
    y_ref, dm_ref, a_ref, qkv_ref, p_ref, o_ref, mid_ref, c_ref, u_ref, gp_ref,
    wq, wo, wu, wd, wsem,
):
    pairs = ((wq_a, wq_b, wq), (wo_a, wo_b, wo), (wu_a, wu_b, wu), (wd_a, wd_b, wd))
    wait = start_weights(scal, pairs, wsem, (0, 1, 2, 3))
    gains = jnp.where(scal[0] == 1, gains_ref[0], gains_b[0])
    h = bytes_ref[...].astype(F32) + mm(spread_matrix(), g_ref[...])
    out = block_forward(h, gains, (wq, wo, wu, wd), wait, 3, a_ref, qkv_ref, p_ref, o_ref, mid_ref, c_ref, u_ref, gp_ref)
    live = live_rows(scal)
    y_ref[...] = jnp.where(live, out, 0.0).astype(BF16)
    dm_ref[...] = jnp.where(live, cot_ref[...].astype(F32), 0.0).astype(BF16)


def row_block(*shape):
    return pl.BlockSpec(shape, lambda i, s: (i,) + (0,) * (len(shape) - 1))


def const_block(*shape):
    return pl.BlockSpec(shape, lambda i, s: (0,) * len(shape), pipeline_mode=pl.Buffered(1))


def seq_block():
    return pl.BlockSpec((TILE, D), lambda i, s: (s[0] * TILES + i, 0))


def local_forward(scal, states, cotangent, g_own, gains, weights, gains_b, weights_b):
    outs = (
        ((SEQ, D), BF16), ((SEQ, D), BF16), ((SEQ, D), BF16), ((SEQ, 3 * D), BF16),
        ((SEQ // 128, PAIRS, 128, 256), BF16), ((SEQ, D), BF16), ((SEQ, D), F32), ((SEQ, D), BF16),
        ((SEQ, FF), BF16), ((SEQ, FF), BF16),
    )
    return pl.pallas_call(
        local_forward_kernel,
        name="local_forward",
        out_shape=[sds(*o) for o in outs],
        grid_spec=pltpu.PrefetchScalarGridSpec(
            num_scalar_prefetch=1,
            grid=(TILES,),
            in_specs=[seq_block(), seq_block(), row_block(TILE // PATCH, D), const_block(1, 2, D)]
            + [ANY] * 8 + [const_block(1, 2, D)],
            out_specs=[row_block(o[0][0] // TILES, *o[0][1:]) for o in outs],
            scratch_shapes=[
                WSCRATCH["q"], WSCRATCH["o"], WSCRATCH["u"], WSCRATCH["d"], pltpu.SemaphoreType.DMA((4,)),
            ],
        ),
        compiler_params=pltpu.CompilerParams(vmem_limit_bytes=VLIMIT),
        cost_estimate=cost(14.5e9, 60e6),
    )(scal, states, cotangent, g_own, gains, *weights, *weights_b, gains_b)


def local_dz_kernel(scal, dm_ref, gp_ref, wd_a, wd_b, dz_ref, wd, wsem):
    wait = start_weights(scal, ((wd_a, wd_b, wd),), wsem, (0,))
    wait(0)
    for part in range(FF // D):
        cols = slice(part * D, part * D + D)
        du = mm_nt(dm_ref[...], wd[cols, :])
        dz_ref[:, cols] = (du * gp_ref[:, cols].astype(F32)).astype(BF16)


def local_dz(scal, dm, gp, wd_a, wd_b):
    return pl.pallas_call(
        local_dz_kernel,
        name="local_dz",
        out_shape=sds((SEQ, FF), BF16),
        grid_spec=pltpu.PrefetchScalarGridSpec(
            num_scalar_prefetch=1,
            grid=(TILES,),
            in_specs=[row_block(TILE, D), row_block(TILE, FF), ANY, ANY],
            out_specs=row_block(TILE, FF),
            scratch_shapes=[WSCRATCH["d"], pltpu.SemaphoreType.DMA((1,))],
        ),
        compiler_params=pltpu.CompilerParams(vmem_limit_bytes=VLIMIT),
        cost_estimate=cost(4.8e9, 18e6),
    )(scal, dm, gp, wd_a, wd_b)


def local_backward_kernel(
    scal, dz_ref, dm_ref, bytes_ref, g_ref, mid_ref, qkv_ref, p_ref, gains_ref,
    wq_a, wo_a, wu_a, wq_b, wo_b, wu_b, gains_b,
    dr_ref, dqkv_ref, dh_ref, dg_ref, dgain_ref,
    do_s, wq, wo, wu, wsem,
):
    pairs = ((wq_a, wq_b, wq), (wo_a, wo_b, wo), (wu_a, wu_b, wu))
    wait = start_weights(scal, pairs, wsem, (2, 1, 0))
    gains = jnp.where(scal[0] == 1, gains_ref[0], gains_b[0])
    h = bytes_ref[...].astype(F32) + mm(spread_matrix(), g_ref[...])
    dh, dgain = block_backward(
        dm_ref[...].astype(F32), h, gains, (wq, wo, wu), wait, dz_ref, mid_ref, qkv_ref, p_ref, do_s, dr_ref, dqkv_ref
    )
    dh_ref[...] = dh
    dg_ref[...] = jnp.sum(dh.reshape(TILE // PATCH, PATCH, D), axis=1).astype(BF16)

    @pl.when(pl.program_id(0) == 0)
    def _():
        dgain_ref[...] = jnp.zeros_like(dgain_ref)

    dgain_ref[0:2, :] += dgain


def local_backward(scal, dz, dm, states, g_own, mid, qkv, p, gains, weights, gains_b, weights_b):
    outs = (
        ((SEQ, D), BF16), ((SEQ, 3 * D), BF16), ((SEQ, D), F32), ((PATCHES, D), BF16), ((8, D), F32),
    )
    return pl.pallas_call(
        local_backward_kernel,
        name="local_backward",
        out_shape=[sds(*o) for o in outs],
        grid_spec=pltpu.PrefetchScalarGridSpec(
            num_scalar_prefetch=1,
            grid=(TILES,),
            in_specs=[
                row_block(TILE, FF), row_block(TILE, D), seq_block(), row_block(TILE // PATCH, D), row_block(TILE, D),
                row_block(TILE, 3 * D), row_block(SUBS, PAIRS, 128, 256), const_block(1, 2, D),
            ] + [ANY] * 6 + [const_block(1, 2, D)],
            out_specs=[row_block(o[0][0] // TILES, *o[0][1:]) for o in outs[:4]] + [const_block(8, D)],
            scratch_shapes=[
                pltpu.VMEM((TILE, D), BF16), WSCRATCH["q"], WSCRATCH["o"], WSCRATCH["u"], pltpu.SemaphoreType.DMA((3,)),
            ],
        ),
        compiler_params=pltpu.CompilerParams(vmem_limit_bytes=VLIMIT),
        cost_estimate=cost(10e9, 50e6),
    )(scal, dz, dm, states, g_own, mid, qkv, p, gains, *weights, *weights_b, gains_b)


def store_shards(scal, total, keep_ref, send_ref, add_refs, order, r, count, z):
    first, second = order
    position = {"x": scal[1], "y": scal[2]}
    for one in range(2):
        for two in range(2):
            at = {first: one ^ position[first], second: two ^ position[second]}
            for k in range(count // 4):
                level = (k ^ scal[3]) * 4 if count == 16 else 0
                shard = level + at["y"] * 2 + at["x"]
                value = total[pl.ds(pl.multiple_of(shard * r, 16), r), :]
                if add_refs is not None:
                    value = value + add_refs[one][two, k].astype(F32)
                (send_ref if one else keep_ref)[two, k] = value.astype(BF16)


def weight_grad_kernel(scal, *refs, parts, order, r, count, has_add, core_zero, shards):
    xs, dys, refs = refs[:parts], refs[parts : 2 * parts], refs[2 * parts :]
    adds = None
    if has_add:
        adds, refs = refs[:2], refs[2:]

    def work():
        value = mm_tn(xs[0][...], dys[0][...])
        for x, dy in zip(xs[1:], dys[1:]):
            value = value + mm_tn(x[...], dy[...])
        if not shards:
            refs[0][...] = value
            return
        keep_ref, send_ref, total = refs
        total[...] = value
        store_shards(scal, total, keep_ref, send_ref, adds, order, r, count, pl.program_id(0))

    if core_zero:
        pl.when(scal[0] == 0)(work)
    else:
        work()


def weight_grad(scal, xs, x_lo, dys, dy_lo, rows, cols, tn, order, add=None, half=None, core_zero=False, shards=True):
    mt, nt = rows // D, cols // tn
    r = rows // 16
    count = 16 if mt == 1 else 4
    depth = xs[0].shape[0]
    kz = 4 if mt == 1 else 1

    def dy_map(m, n, s):
        offset = 0 if half is None else (s[0] if half == "own" else 1 - s[0]) * nt
        return (0, dy_lo // tn + offset + n)

    shard_spec = pl.BlockSpec((2, kz, r, tn), lambda m, n, s: (0, 0 if mt == 1 else m ^ s[3], 0, n))
    if shards:
        out_shape = [sds((2, 4, r, cols), BF16)] * 2
        out_specs = [shard_spec] * 2
        scratch = [pltpu.VMEM((D, tn), F32)]
    else:
        out_shape = sds((rows, cols), F32)
        out_specs = pl.BlockSpec((D, tn), lambda m, n, s: (m, n))
        scratch = []
    return pl.pallas_call(
        functools.partial(
            weight_grad_kernel, parts=len(xs), order=order, r=r, count=count, has_add=add is not None,
            core_zero=core_zero, shards=shards,
        ),
        name="weight_grad",
        out_shape=out_shape,
        grid_spec=pltpu.PrefetchScalarGridSpec(
            num_scalar_prefetch=1,
            grid=(mt, nt),
            in_specs=[pl.BlockSpec((depth, D), lambda m, n, s: (0, x_lo // D + m))] * len(xs)
            + [pl.BlockSpec((depth, tn), dy_map)] * len(xs) + [shard_spec] * (0 if add is None else 2),
            out_specs=out_specs,
            scratch_shapes=scratch,
        ),
        compiler_params=pltpu.CompilerParams(vmem_limit_bytes=VLIMIT),
        cost_estimate=cost(2 * depth * len(xs) * rows * cols, 2 * (depth * (rows + cols) + rows * cols)),
    )(scal, *xs, *dys, *(add or ()))


def patch_grad_kernel(scal, bytes_ref, dpp_ref, *refs, order, shards):
    bytes_f32, total = refs[-2:]

    @pl.when(pl.program_id(0) == 0)
    def _():
        fill_lanes(bytes_f32, bytes_ref)

    byte = scal[0] * (PATCH // 2) + pl.program_id(0)
    x = strided_rows(bytes_f32, byte, MB * PATCHES).astype(BF16)
    value = mm_tn(x, dpp_ref[...])
    if not shards:
        refs[0][...] = value
        return
    total[...] = value
    store_shards(scal, total, refs[0], refs[1], None, order, 192, 4, pl.program_id(0))


def patch_weight_grad(scal, states, dpp, order, shards=True):
    if shards:
        out_shape = [sds((2, 4, 192, D), BF16)] * 2
        out_specs = [pl.BlockSpec((2, 1, 192, D), lambda i, s: (0, i ^ s[3], 0, 0))] * 2
    else:
        out_shape = [sds((PATCH // 2 * D, D), F32)]
        out_specs = [pl.BlockSpec((D, D), lambda i, s: (i, 0))]
    return pl.pallas_call(
        functools.partial(patch_grad_kernel, order=order, shards=shards),
        name="patch_weight_grad",
        out_shape=out_shape,
        grid_spec=pltpu.PrefetchScalarGridSpec(
            num_scalar_prefetch=1,
            grid=(PATCH // 2,),
            in_specs=[const_block(MB * SEQ, D), const_block(MB * PATCHES, D)],
            out_specs=out_specs,
            scratch_shapes=[pltpu.VMEM((LANES, MB * SEQ, 128), F32), pltpu.VMEM((D, D), F32)],
        ),
        compiler_params=pltpu.CompilerParams(vmem_limit_bytes=VLIMIT),
        cost_estimate=cost(1.2e9, 10e6),
    )(scal, states, dpp)


def input_grad_kernel(dpp_ref, dh_ref, wp_hbm, out_ref, acc, wp, psem):
    copies = [
        pltpu.make_async_copy(wp_hbm.at[pl.ds(j * D, D)], wp.at[pl.ds(j * D, D)], psem.at[j]) for j in range(PATCH)
    ]
    for copy in copies:
        copy.start()
    for j in range(PATCH):
        copies[j].wait()
        value = mm_nt(dpp_ref[...], wp[j * D : j * D + D, :])
        for b in range(LANES):
            acc[b, pl.ds(j, PATCHES, stride=PATCH), :] = value[:, b * 128 : b * 128 + 128]
    for b in range(LANES):
        cols = slice(b * 128, b * 128 + 128)
        out_ref[:, cols] = (dh_ref[:, cols] + acc[b]).astype(BF16)


def input_grad_part(dpp_own, dh, patch_weight):
    return pl.pallas_call(
        input_grad_kernel,
        name="input_grad",
        out_shape=sds((SEQ, D), BF16),
        in_specs=[pl.BlockSpec(memory_space=pltpu.VMEM)] * 2 + [ANY],
        out_specs=pl.BlockSpec(memory_space=pltpu.VMEM),
        scratch_shapes=[
            pltpu.VMEM((LANES, SEQ, 128), F32), pltpu.VMEM((PATCH * D, D), BF16), pltpu.SemaphoreType.DMA((PATCH,)),
        ],
        compiler_params=pltpu.CompilerParams(vmem_limit_bytes=VLIMIT),
        cost_estimate=cost(1.2e9, 15e6),
    )(dpp_own, dh, patch_weight)


def swap_core(value):
    return lax.ppermute(value, "section", [(0, 1), (1, 0)])


def hop(value, mask, cores):
    size = lax.axis_size("dp")
    if cores == (0, 1):
        return lax.ppermute(value, "dp", [(i, i ^ mask) for i in range(size)])
    pairs = [(c * size + i, c * size + (i ^ mask)) for c in cores for i in range(size)]
    return lax.ppermute(value, ("section", "dp"), pairs)


HOPS = {"x": 1, "y": 2}


def add_low(a, b):
    return (a.astype(F32) + b.astype(F32)).astype(BF16)


def z_sum(keep, recv, cores):
    total = keep[..., 0, :, :].astype(F32) + recv[..., 0, :, :].astype(F32)
    for k in (1, 2, 3):
        part = hop(add_low(keep[..., k, :, :], recv[..., k, :, :]), 4 * k, cores)
        total = total + part.astype(F32)
    return total


def reduce_shards(keep, send, order, cores=(0, 1)):
    recv = hop(send, HOPS[order[0]], cores)
    kept, sent = add_low(keep[0], recv[0]), add_low(keep[1], recv[1])
    return z_sum(kept, hop(sent, HOPS[order[1]], cores), cores)


def local_weight_grads(scal, x, dy, rows, cols, tn, order):
    half = cols // 2
    peer = weight_grad(scal, [x], 0, [dy], 0, rows, half, tn, order, half="peer")
    return weight_grad(
        scal, [x], 0, [dy], 0, rows, half, tn, order, add=[swap_core(v) for v in peer], half="own"
    )


def body(states, lengths, patch_weight, w_qkv, w_out, w_up, w_down, gains, cotangent):
    size = lax.axis_size("dp")
    fast = size == 16
    core = lax.axis_index("section")
    at = lax.axis_index("dp")
    mx, my, mz = at % 2, (at // 2) % 2, (at // 4) % 4
    length = jnp.where(core == 0, lengths[0], lengths[1])
    scal = jnp.stack([core, mx, my, mz, length]).astype(jnp.int32)
    weights = (w_qkv, w_out, w_up, w_down)
    other = tuple(swap_core(w) for w in weights)
    gains_other = swap_core(gains)

    g_all, xg, start, qkv_g, p_g, mid_g, gp_g = global_forward(scal, states, gains, patch_weight, weights)
    g_recv = swap_core(g_all[PATCHES:])
    g_own = jnp.where(core == 0, g_all[:PATCHES], g_recv)
    if fast:
        xg_next = hop(xg, 1, (0,))

    y, dm, a, qkv, p, o, mid, c, u, gp = local_forward(
        scal, states, cotangent, g_own, gains, weights, gains_other, other
    )
    y_recv = swap_core(y)
    g_rows = jnp.broadcast_to(g_all[:, None, :], (MB * PATCHES, PATCH, D)).reshape(MB * SEQ, D)
    section_outputs = jnp.where(core == 0, g_rows, jnp.concatenate([y_recv, y], axis=0))[None]

    if fast:
        down_l = reduce_shards(*local_weight_grads(scal, u, dm, FF, D, 384, "xy"), "xy")
    dz = local_dz(scal, dm, gp, w_down, other[3])
    if fast:
        up_l = reduce_shards(*local_weight_grads(scal, c, dz, D, FF, 384, "yx"), "yx")
    dr, dqkv, dh, dg, dgain_l = local_backward(
        scal, dz, dm, states, g_own, mid, qkv, p, gains, weights[:3], gains_other, other[:3]
    )
    dg_recv = swap_core(dg)
    dpp, dy_keep, dy_send, dgain_g = global_backward(
        scal, (dg, dg_recv), (start, mid_g, qkv_g, p_g, gp_g), gains, weights
    )
    dpp_recv = swap_core(dpp)
    dpp = jnp.where(core == 0, dpp, dpp_recv)
    dpp_own = jnp.where(core == 0, dpp[:PATCHES], dpp[PATCHES:])
    own_grad = input_grad_part(dpp_own, dh, patch_weight)
    peer_grad = swap_core(own_grad)
    input_grad = jnp.where(
        core == 0, jnp.concatenate([own_grad, peer_grad]), jnp.concatenate([peer_grad, own_grad])
    ).astype(F32)

    blocks = jnp.stack([jnp.where(core == 0, dgain_g[:2], 0.0), dgain_l[:2]])
    blocks = lax.psum(blocks, ("section", "dp"))
    own_gains = jnp.where(core == 0, blocks[0], blocks[1])
    share = D // size
    gain_grad = lax.dynamic_slice(own_gains, (0, at * share), (2, share))

    if fast:
        proj_l = reduce_shards(*local_weight_grads(scal, o, dr, D, D, 384, "xy"), "xy")
        qkv_l = reduce_shards(*local_weight_grads(scal, a, dqkv, D, 3 * D, 384, "xy"), "xy")
        dy_next = hop(dy_send, 1, (0,))
        keep, send = patch_weight_grad(scal, states, dpp, "yx")
        patch_grad = reduce_shards(keep, send, "yx")

        def global_grad(x_lo, dy_lo, rows, cols):
            keep, send = weight_grad(
                scal, [xg, xg_next], x_lo, [dy_keep, dy_next], dy_lo, rows, cols, 384, "yx", core_zero=True
            )
            both = z_sum(keep, hop(send, 2, (0,)), (0,))
            swapped = hop(both[1].astype(BF16), 1, (0,)).astype(F32)
            mine = both[0]
            return jnp.where(
                mx == 0, jnp.concatenate([mine, swapped], axis=1), jnp.concatenate([swapped, mine], axis=1)
            )

        half = D // 2
        up_g = global_grad(2 * D, 4 * half, D, FF // 2)
        down_g = global_grad(3 * D, 8 * half, FF, half)
        proj_g = global_grad(D, 3 * half, D, half)
        qkv_g = global_grad(0, 0, D, 3 * half)

        def place(whole, part):
            other_part = swap_core(part)
            return jnp.where(core == 0, whole, jnp.concatenate([other_part, part], axis=1))[None]

        outs = (place(qkv_g, qkv_l), place(proj_g, proj_l), place(up_g, up_l), place(down_g, down_l))
    else:
        (patch_half,) = patch_weight_grad(scal, states, dpp, "xy", shards=False)
        patch_grad = lax.psum_scatter(patch_half, "dp", scatter_dimension=0, tiled=True)
        half = D // 2
        swap_halves = lambda keep, send, lo, width: jnp.where(
            mx == 0,
            jnp.concatenate([keep[:, lo : lo + width], send[:, lo : lo + width]], axis=1),
            jnp.concatenate([send[:, lo : lo + width], keep[:, lo : lo + width]], axis=1),
        )

        def whole_grad(x_lo, dy_lo, x, dy, rows, cols):
            dy_g = swap_halves(dy_keep, dy_send, dy_lo, cols // 2)
            glob = weight_grad(scal, [xg], x_lo, [dy_g], 0, rows, cols, 384, "xy", shards=False)
            loc = weight_grad(scal, [x], 0, [dy], 0, rows, cols, 384, "xy", shards=False)
            total = jnp.where(core == 0, glob, loc + swap_core(loc))
            return lax.psum_scatter(total, "dp", scatter_dimension=0, tiled=True)[None]

        outs = (
            whole_grad(0, 0, a, dqkv, D, 3 * D),
            whole_grad(D, 3 * half, o, dr, D, D),
            whole_grad(2 * D, 4 * half, c, dz, D, FF),
            whole_grad(3 * D, 8 * half, u, dm, FF, D),
        )
    return (section_outputs, input_grad, patch_grad, *outs, gain_grad[None])


def solution(mesh):
    return jax.shard_map(
        body,
        mesh=mesh,
        in_specs=(
            P("dp", None), P("dp"), P(), P("section", None, None), P("section", None, None),
            P("section", None, None), P("section", None, None), P("section", None, None), P("dp", None),
        ),
        out_specs=(
            P("section", "dp", None), P("dp", None), P(("section", "dp"), None), P("section", "dp", None),
            P("section", "dp", None), P("section", "dp", None), P("section", "dp", None), P("section", None, "dp"),
        ),
        check_vma=False,
    )
```

```python
import functools

import jax
import jax.numpy as jnp
from jax import lax
from jax.experimental import pallas as pl
from jax.experimental.pallas import tpu as pltpu
from jax.sharding import PartitionSpec as P

D = 768
HEADS = 12
HDIM = 64
FF = 3072
PATCH = 8
SEQ = 1024
PATCHES = SEQ // PATCH
TILE = 256
SUBS = TILE // 128
PAIRS = HEADS // 2
TILES = SEQ // TILE
MB = 2
XG = 3 * D + FF
F32 = jnp.float32
BF16 = jnp.bfloat16
ANY = pl.BlockSpec(memory_space=pl.ANY)
VLIMIT = 56 * 2**20


def sds(shape, dtype):
    return jax.ShapeDtypeStruct(shape, dtype)


def mm(a, b):
    return jnp.dot(a, b, preferred_element_type=F32)


def mm_nt(a, b):
    return lax.dot_general(a, b, (((1,), (1,)), ((), ())), preferred_element_type=F32)


def mm_tn(a, b):
    return lax.dot_general(a, b, (((0,), (0,)), ((), ())), preferred_element_type=F32)


def normalized(v):
    centered = v - jnp.mean(v, axis=-1, keepdims=True)
    scale = lax.rsqrt(jnp.mean(centered * centered, axis=-1, keepdims=True) + 1e-5)
    return centered * scale, scale


def norm_backward(grad, gain, hat, scale):
    scaled = grad * gain
    inner = scaled - jnp.mean(scaled, axis=-1, keepdims=True)
    inner = inner - hat * jnp.mean(scaled * hat, axis=-1, keepdims=True)
    return inner * scale, jnp.sum(grad * hat, axis=0, keepdims=True)


def gelu_pair(z):
    t = 1.0 / (1.0 + 0.3275911 * 0.7071067811865476 * jnp.abs(z))
    bell = jnp.exp(-0.5 * z * z)
    poly = 1.061405429 * t - 1.453152027
    poly = poly * t + 1.421413741
    poly = poly * t - 0.284496736
    poly = poly * t + 0.254829592
    half_tail = 0.5 * poly * t * bell
    cdf = jnp.where(z >= 0, 1.0 - half_tail, half_tail)
    return z * cdf, cdf + z * bell * 0.3989422804014327


def lane_masks():
    lane = lax.broadcasted_iota(jnp.int32, (128, 128), 1)
    first = jnp.where(lane < HDIM, 1.0, 0.0)
    return first.astype(BF16), (1.0 - first).astype(BF16), lane < HDIM


def split_heads(v, first, second):
    return jnp.concatenate([v * first, v * second], axis=0)


def attention_forward(qkv_ref, o_ref, p_ref, shift):
    first, second, _ = lane_masks()
    row = lax.broadcasted_iota(jnp.int32, (128, 256), 0)
    col = lax.broadcasted_iota(jnp.int32, (128, 256), 1) & 127
    allowed = (col <= row) & ((col >> shift) == (row >> shift))
    for sub in range(SUBS):
        rows = slice(sub * 128, sub * 128 + 128)
        for pair in range(PAIRS):
            lo = pair * 128
            q = qkv_ref[rows, lo : lo + 128]
            k2 = split_heads(qkv_ref[rows, D + lo : D + lo + 128], first, second)
            v2 = split_heads(qkv_ref[rows, 2 * D + lo : 2 * D + lo + 128], first, second)
            s = jnp.where(allowed, mm_nt(q, k2) * 0.125, -1e30)
            parts = []
            for half in range(2):
                sh = s[:, half * 128 : half * 128 + 128]
                e = jnp.exp(sh - jnp.max(sh, axis=-1, keepdims=True))
                parts.append(e / jnp.sum(e, axis=-1, keepdims=True))
            p = jnp.concatenate(parts, axis=1).astype(BF16)
            p_ref[sub, pair] = p
            o_ref[rows, lo : lo + 128] = mm(p, v2).astype(BF16)


def attention_backward(qkv_ref, p_ref, do_ref, dqkv_ref):
    first, second, is_first = lane_masks()
    for sub in range(SUBS):
        rows = slice(sub * 128, sub * 128 + 128)
        for pair in range(PAIRS):
            lo = pair * 128
            q = qkv_ref[rows, lo : lo + 128]
            k2 = split_heads(qkv_ref[rows, D + lo : D + lo + 128], first, second)
            v2 = split_heads(qkv_ref[rows, 2 * D + lo : 2 * D + lo + 128], first, second)
            do = do_ref[rows, lo : lo + 128]
            p = p_ref[sub, pair]
            dp = mm_nt(do, v2)
            pf = p.astype(F32)
            weighted = pf * dp
            parts = []
            for half in range(2):
                cols = slice(half * 128, half * 128 + 128)
                total = jnp.sum(weighted[:, cols], axis=-1, keepdims=True)
                parts.append(weighted[:, cols] - pf[:, cols] * total)
            ds = jnp.concatenate(parts, axis=1).astype(BF16)
            dq = mm(ds, k2) * 0.125
            dk2 = mm_tn(ds, q) * 0.125
            dv2 = mm_tn(p, do)
            dk = jnp.where(is_first, dk2[:128], dk2[128:])
            dv = jnp.where(is_first, dv2[:128], dv2[128:])
            dqkv_ref[rows, lo : lo + 128] = dq.astype(BF16)
            dqkv_ref[rows, D + lo : D + lo + 128] = dk.astype(BF16)
            dqkv_ref[rows, 2 * D + lo : 2 * D + lo + 128] = dv.astype(BF16)


def block_forward(h, gains, w, wait, shift, a_ref, qkv_ref, p_ref, o_ref, mid_ref, c_ref, u_ref, gp_ref):
    wq, wo, wu, wd = w
    a_ref[...] = (normalized(h)[0] * gains[0:1, :]).astype(BF16)
    wait(0)
    for part in range(3):
        cols = slice(part * D, part * D + D)
        qkv_ref[:, cols] = mm(a_ref[...], wq[:, cols]).astype(BF16)
    attention_forward(qkv_ref, o_ref, p_ref, shift)
    wait(1)
    mid = h + mm(o_ref[...], wo[...])
    mid_ref[...] = mid
    c_ref[...] = (normalized(mid)[0] * gains[1:2, :]).astype(BF16)
    wait(2)
    for part in range(FF // D):
        cols = slice(part * D, part * D + D)
        u, gp = gelu_pair(mm(c_ref[...], wu[:, cols]))
        u_ref[:, cols] = u.astype(BF16)
        gp_ref[:, cols] = gp.astype(BF16)
    wait(3)
    return mid_ref[...] + mm(u_ref[...], wd[...])


def block_backward(dout, h, gains, w, wait, dz_ref, mid_ref, qkv_ref, p_ref, do_ref, dr_ref, dqkv_ref):
    wq, wo, wu = w
    hat, scale = normalized(mid_ref[...])
    wait(2)
    dc = mm_nt(dz_ref[...], wu[...])
    back, dgain_two = norm_backward(dc, gains[1:2, :], hat, scale)
    dmid = dout + back
    dr_ref[...] = dmid.astype(BF16)
    wait(1)
    do_ref[...] = mm_nt(dr_ref[...], wo[...]).astype(BF16)
    attention_backward(qkv_ref, p_ref, do_ref, dqkv_ref)
    wait(0)
    da = mm_nt(dqkv_ref[...], wq[...])
    hat, scale = normalized(h)
    back, dgain_one = norm_backward(da, gains[0:1, :], hat, scale)
    return dmid + back, jnp.concatenate([dgain_one, dgain_two], axis=0)


LANES = D // 128


def fill_lanes(dst, src):
    for b in range(LANES):
        dst[b] = src[:, b * 128 : b * 128 + 128].astype(F32)


def strided_rows(ref, start, rows):
    picked = [ref[b, pl.ds(start, rows, stride=PATCH), :] for b in range(LANES)]
    return jnp.concatenate(picked, axis=1)


def spread_matrix():
    row = lax.broadcasted_iota(jnp.int32, (TILE, TILE // PATCH), 0) // PATCH
    col = lax.broadcasted_iota(jnp.int32, (TILE, TILE // PATCH), 1)
    return jnp.where(row == col, 1.0, 0.0).astype(BF16)


def add_low(a, b):
    return (a.astype(F32) + b.astype(F32)).astype(BF16)


def cost(flops, nbytes):
    return pl.CostEstimate(flops=int(flops), bytes_accessed=int(nbytes), transcendentals=0)


WSCRATCH = {
    "q": pltpu.VMEM((D, 3 * D), BF16),
    "o": pltpu.VMEM((D, D), BF16),
    "u": pltpu.VMEM((D, FF), BF16),
    "d": pltpu.VMEM((FF, D), BF16),
}


def global_forward_kernel(
    scal, bytes_ref, gains_ref, wp_hbm, wq_hbm, wo_hbm, wu_hbm, wd_hbm,
    g_ref, x_ref, start_ref, qkv_ref, p_ref, mid_ref, gp_ref, pat_ref,
    bytes_f32, wp, wq, wo, wu, wd, psem, wsem,
):
    rows = MB * PATCHES
    fill_lanes(bytes_f32, bytes_ref)

    def share_out(j, t):
        xj = strided_rows(bytes_f32, j, rows).astype(BF16)
        for piece in range(4):
            relative = (piece % 2) ^ scal[1] | (((piece // 2) ^ scal[2]) << 1)
            pat_ref[relative, :, t * 192 : t * 192 + 192] = xj[:, piece * 192 : piece * 192 + 192]
        return xj

    @pl.when(scal[0] == 1)
    def _():
        for t in range(PATCH // 2):
            share_out(PATCH // 2 + t, t)

    @pl.when(scal[0] == 0)
    def _():
        pcopies = [
            pltpu.make_async_copy(wp_hbm.at[pl.ds(j * D, D)], wp.at[pl.ds(j * D, D)], psem.at[j])
            for j in range(PATCH)
        ]
        wcopies = [
            pltpu.make_async_copy(src.at[0], dst, wsem.at[i])
            for i, (src, dst) in enumerate(((wq_hbm, wq), (wo_hbm, wo), (wu_hbm, wu), (wd_hbm, wd)))
        ]
        for copy in pcopies + wcopies:
            copy.start()
        acc = jnp.zeros((rows, D), F32)
        for j in range(PATCH):
            pcopies[j].wait()
            xj = share_out(j, j) if j < PATCH // 2 else strided_rows(bytes_f32, j, rows).astype(BF16)
            acc = acc + mm(xj, wp[j * D : j * D + D, :])
        moved = pltpu.roll(acc, 1, 0)
        row = lax.broadcasted_iota(jnp.int32, (rows, D), 0)
        start_ref[...] = jnp.where((row & (PATCHES - 1)) == 0, 0.0, moved)
        out = block_forward(
            start_ref[...], gains_ref[0], (wq, wo, wu, wd), lambda i: wcopies[i].wait(), 7,
            x_ref.at[:, 0:D], qkv_ref, p_ref, x_ref.at[:, D : 2 * D], mid_ref,
            x_ref.at[:, 2 * D : 3 * D], x_ref.at[:, 3 * D : 3 * D + FF], gp_ref,
        )
        g_ref[...] = out.astype(BF16)


def global_forward(scal, states, gains, patch_weight, weights):
    rows = MB * PATCHES
    full = lambda *shape: pl.BlockSpec(shape, lambda i, s: (0,) * len(shape), pipeline_mode=pl.Buffered(1))
    outs = (
        ((rows, D), BF16), ((rows, XG), BF16), ((rows, D), F32), ((rows, 3 * D), BF16),
        ((SUBS, PAIRS, 128, 256), BF16), ((rows, D), F32), ((rows, FF), BF16),
        ((4, rows, D), BF16),
    )
    return pl.pallas_call(
        global_forward_kernel,
        name="global_forward",
        out_shape=[sds(*o) for o in outs],
        grid_spec=pltpu.PrefetchScalarGridSpec(
            num_scalar_prefetch=1,
            grid=(1,),
            in_specs=[full(MB * SEQ, D), full(1, 2, D)] + [ANY] * 5,
            out_specs=[full(*o[0]) for o in outs],
            scratch_shapes=[
                pltpu.VMEM((LANES, MB * SEQ, 128), F32), pltpu.VMEM((PATCH * D, D), BF16),
                WSCRATCH["q"], WSCRATCH["o"], WSCRATCH["u"], WSCRATCH["d"],
                pltpu.SemaphoreType.DMA((PATCH,)), pltpu.SemaphoreType.DMA((4,)),
            ],
        ),
        compiler_params=pltpu.CompilerParams(vmem_limit_bytes=VLIMIT),
        cost_estimate=cost(6e9, 32e6),
    )(scal, states, gains, patch_weight, *weights)


def global_backward_kernel(
    scal, dg0_ref, dg1_ref, start_ref, mid_ref, qkv_ref, p_ref, gp_ref, gains_ref, wq_hbm, wo_hbm, wu_hbm, wd_hbm,
    dpp_ref, keep_ref, send_ref, dgain_ref,
    dm_s, dz_s, do_s, dr_s, dqkv_s, wq, wo, wu, wd, wsem,
):
    @pl.when(scal[0] == 0)
    def _():
        rows = MB * PATCHES
        wcopies = [
            pltpu.make_async_copy(src.at[0], dst, wsem.at[i])
            for i, (src, dst) in enumerate(((wq_hbm, wq), (wo_hbm, wo), (wu_hbm, wu), (wd_hbm, wd)))
        ]
        for i in (3, 2, 1, 0):
            wcopies[i].start()
        dm_s[0:PATCHES, :] = dg0_ref[...]
        dm_s[PATCHES:, :] = dg1_ref[...]
        wcopies[3].wait()
        for part in range(FF // D):
            cols = slice(part * D, part * D + D)
            du = mm_nt(dm_s[...], wd[cols, :])
            dz_s[:, cols] = (du * gp_ref[:, cols].astype(F32)).astype(BF16)
        dh, dgain = block_backward(
            dm_s[...].astype(F32), start_ref[...], gains_ref[0], (wq, wo, wu), lambda i: wcopies[i].wait(),
            dz_s, mid_ref, qkv_ref, p_ref, do_s, dr_s, dqkv_s,
        )
        dgain_ref[...] = jnp.zeros_like(dgain_ref)
        dgain_ref[0:2, :] = dgain
        moved = pltpu.roll(dh, rows - 1, 0)
        row = lax.broadcasted_iota(jnp.int32, (rows, D), 0)
        dpp_ref[...] = jnp.where((row & (PATCHES - 1)) == PATCHES - 1, 0.0, moved).astype(BF16)
        for half in range(2):
            def fill(ref):
                lo = 0
                for src, width in ((dqkv_s, 3 * D // 2), (dr_s, D // 2), (dz_s, FF // 2), (dm_s, D // 2)):
                    ref[:, lo : lo + width] = src[:, half * width : half * width + width]
                    lo += width
            pl.when(scal[1] == half)(functools.partial(fill, keep_ref))
            pl.when(scal[1] != half)(functools.partial(fill, send_ref))

    @pl.when(scal[0] != 0)
    def _():
        dgain_ref[...] = jnp.zeros_like(dgain_ref)


def global_backward(scal, dgs, saved, gains, weights):
    rows = MB * PATCHES
    full = lambda *shape: pl.BlockSpec(shape, lambda i, s: (0,) * len(shape), pipeline_mode=pl.Buffered(1))
    width = (3 * D + D + FF + D) // 2
    outs = (((rows, D), BF16), ((rows, width), BF16), ((rows, width), BF16), ((8, D), F32))
    return pl.pallas_call(
        global_backward_kernel,
        name="global_backward",
        out_shape=[sds(*o) for o in outs],
        grid_spec=pltpu.PrefetchScalarGridSpec(
            num_scalar_prefetch=1,
            grid=(1,),
            in_specs=[full(PATCHES, D)] * 2 + [full(*v.shape) for v in saved] + [full(1, 2, D)] + [ANY] * 4,
            out_specs=[full(*o[0]) for o in outs],
            scratch_shapes=[
                pltpu.VMEM((rows, D), BF16), pltpu.VMEM((rows, FF), BF16), pltpu.VMEM((rows, D), BF16),
                pltpu.VMEM((rows, D), BF16), pltpu.VMEM((rows, 3 * D), BF16),
                WSCRATCH["q"], WSCRATCH["o"], WSCRATCH["u"], WSCRATCH["d"],
                pltpu.SemaphoreType.DMA((4,)),
            ],
        ),
        compiler_params=pltpu.CompilerParams(vmem_limit_bytes=VLIMIT),
        cost_estimate=cost(6e9, 24e6),
    )(scal, *dgs, *saved, gains, *weights)


def start_weights(scal, pairs, sems, order):
    step = pl.program_id(0)
    for i in order:
        own, recv, dst = pairs[i]

        @pl.when((step == 0) & (scal[0] == 1))
        def _(own=own, dst=dst, i=i):
            pltpu.make_async_copy(own.at[0], dst, sems.at[i]).start()

        @pl.when((step == 0) & (scal[0] == 0))
        def _(recv=recv, dst=dst, i=i):
            pltpu.make_async_copy(recv.at[0], dst, sems.at[i]).start()

    def wait(i):
        @pl.when(step == 0)
        def _():
            pltpu.make_async_copy(pairs[i][1].at[0], pairs[i][2], sems.at[i]).wait()

    return wait


def live_rows(scal):
    step = pl.program_id(0)
    row = lax.broadcasted_iota(jnp.int32, (TILE, D), 0) + step * TILE
    return row < scal[4]


def local_forward_kernel(
    scal, bytes_ref, cot_ref, g_ref, gains_ref, wq_a, wo_a, wu_a, wd_a, wq_b, wo_b, wu_b, wd_b, gains_b,
    y_ref, dm_ref, a_ref, qkv_ref, p_ref, o_ref, mid_ref, c_ref, u_ref, gp_ref,
    wq, wo, wu, wd, wsem,
):
    pairs = ((wq_a, wq_b, wq), (wo_a, wo_b, wo), (wu_a, wu_b, wu), (wd_a, wd_b, wd))
    wait = start_weights(scal, pairs, wsem, (0, 1, 2, 3))
    gains = jnp.where(scal[0] == 1, gains_ref[0], gains_b[0])
    h = bytes_ref[...].astype(F32) + mm(spread_matrix(), g_ref[...])
    out = block_forward(h, gains, (wq, wo, wu, wd), wait, 3, a_ref, qkv_ref, p_ref, o_ref, mid_ref, c_ref, u_ref, gp_ref)
    live = live_rows(scal)
    y_ref[...] = jnp.where(live, out, 0.0).astype(BF16)
    dm_ref[...] = jnp.where(live, cot_ref[...].astype(F32), 0.0).astype(BF16)


def row_block(*shape):
    return pl.BlockSpec(shape, lambda i, s: (i,) + (0,) * (len(shape) - 1))


def const_block(*shape):
    return pl.BlockSpec(shape, lambda i, s: (0,) * len(shape), pipeline_mode=pl.Buffered(1))


def seq_block():
    return pl.BlockSpec((TILE, D), lambda i, s: (s[0] * TILES + i, 0))


def local_forward(scal, states, cotangent, g_own, gains, weights, gains_b, weights_b):
    outs = (
        ((SEQ, D), BF16), ((SEQ, D), BF16), ((SEQ, D), BF16), ((SEQ, 3 * D), BF16),
        ((SEQ // 128, PAIRS, 128, 256), BF16), ((SEQ, D), BF16), ((SEQ, D), F32), ((SEQ, D), BF16),
        ((SEQ, FF), BF16), ((SEQ, FF), BF16),
    )
    return pl.pallas_call(
        local_forward_kernel,
        name="local_forward",
        out_shape=[sds(*o) for o in outs],
        grid_spec=pltpu.PrefetchScalarGridSpec(
            num_scalar_prefetch=1,
            grid=(TILES,),
            in_specs=[seq_block(), seq_block(), row_block(TILE // PATCH, D), const_block(1, 2, D)]
            + [ANY] * 8 + [const_block(1, 2, D)],
            out_specs=[row_block(o[0][0] // TILES, *o[0][1:]) for o in outs],
            scratch_shapes=[
                WSCRATCH["q"], WSCRATCH["o"], WSCRATCH["u"], WSCRATCH["d"], pltpu.SemaphoreType.DMA((4,)),
            ],
        ),
        compiler_params=pltpu.CompilerParams(vmem_limit_bytes=VLIMIT),
        cost_estimate=cost(14.5e9, 60e6),
    )(scal, states, cotangent, g_own, gains, *weights, *weights_b, gains_b)


def local_dz_kernel(scal, dm_ref, gp_ref, wd_a, wd_b, dz_ref, wd, wsem):
    wait = start_weights(scal, ((wd_a, wd_b, wd),), wsem, (0,))
    wait(0)
    for part in range(FF // D):
        cols = slice(part * D, part * D + D)
        du = mm_nt(dm_ref[...], wd[cols, :])
        dz_ref[:, cols] = (du * gp_ref[:, cols].astype(F32)).astype(BF16)


def local_dz(scal, dm, gp, wd_a, wd_b):
    return pl.pallas_call(
        local_dz_kernel,
        name="local_dz",
        out_shape=sds((SEQ, FF), BF16),
        grid_spec=pltpu.PrefetchScalarGridSpec(
            num_scalar_prefetch=1,
            grid=(TILES,),
            in_specs=[row_block(TILE, D), row_block(TILE, FF), ANY, ANY],
            out_specs=row_block(TILE, FF),
            scratch_shapes=[WSCRATCH["d"], pltpu.SemaphoreType.DMA((1,))],
        ),
        compiler_params=pltpu.CompilerParams(vmem_limit_bytes=VLIMIT),
        cost_estimate=cost(4.8e9, 18e6),
    )(scal, dm, gp, wd_a, wd_b)


def local_backward_kernel(
    scal, dz_ref, dm_ref, bytes_ref, g_ref, mid_ref, qkv_ref, p_ref, gains_ref,
    wq_a, wo_a, wu_a, wq_b, wo_b, wu_b, gains_b,
    dr_ref, dqkv_ref, dh_ref, dg_ref, dgain_ref,
    do_s, wq, wo, wu, wsem,
):
    pairs = ((wq_a, wq_b, wq), (wo_a, wo_b, wo), (wu_a, wu_b, wu))
    wait = start_weights(scal, pairs, wsem, (2, 1, 0))
    gains = jnp.where(scal[0] == 1, gains_ref[0], gains_b[0])
    h = bytes_ref[...].astype(F32) + mm(spread_matrix(), g_ref[...])
    dh, dgain = block_backward(
        dm_ref[...].astype(F32), h, gains, (wq, wo, wu), wait, dz_ref, mid_ref, qkv_ref, p_ref, do_s, dr_ref, dqkv_ref
    )
    dh_ref[...] = dh
    dg_ref[...] = jnp.sum(dh.reshape(TILE // PATCH, PATCH, D), axis=1).astype(BF16)

    @pl.when(pl.program_id(0) == 0)
    def _():
        dgain_ref[...] = jnp.zeros_like(dgain_ref)

    dgain_ref[0:2, :] += dgain


def local_backward(scal, dz, dm, states, g_own, mid, qkv, p, gains, weights, gains_b, weights_b):
    outs = (
        ((SEQ, D), BF16), ((SEQ, 3 * D), BF16), ((SEQ, D), F32), ((PATCHES, D), BF16), ((8, D), F32),
    )
    return pl.pallas_call(
        local_backward_kernel,
        name="local_backward",
        out_shape=[sds(*o) for o in outs],
        grid_spec=pltpu.PrefetchScalarGridSpec(
            num_scalar_prefetch=1,
            grid=(TILES,),
            in_specs=[
                row_block(TILE, FF), row_block(TILE, D), seq_block(), row_block(TILE // PATCH, D), row_block(TILE, D),
                row_block(TILE, 3 * D), row_block(SUBS, PAIRS, 128, 256), const_block(1, 2, D),
            ] + [ANY] * 6 + [const_block(1, 2, D)],
            out_specs=[row_block(o[0][0] // TILES, *o[0][1:]) for o in outs[:4]] + [const_block(8, D)],
            scratch_shapes=[
                pltpu.VMEM((TILE, D), BF16), WSCRATCH["q"], WSCRATCH["o"], WSCRATCH["u"], pltpu.SemaphoreType.DMA((3,)),
            ],
        ),
        compiler_params=pltpu.CompilerParams(vmem_limit_bytes=VLIMIT),
        cost_estimate=cost(10e9, 50e6),
    )(scal, dz, dm, states, g_own, mid, qkv, p, gains, *weights, *weights_b, gains_b)


def store_shards(scal, total, keep_ref, send_ref, add_refs, order, r, count, z):
    first, second = order
    position = {"x": scal[1], "y": scal[2]}
    for one in range(2):
        for two in range(2):
            at = {first: one ^ position[first], second: two ^ position[second]}
            for k in range(count // 4):
                level = (k ^ scal[3]) * 4 if count == 16 else 0
                shard = level + at["y"] * 2 + at["x"]
                value = total[pl.ds(pl.multiple_of(shard * r, 16), r), :]
                if add_refs is not None:
                    value = value + add_refs[one][two, k].astype(F32)
                (send_ref if one else keep_ref)[two, k] = value.astype(BF16)


def weight_grad_kernel(scal, *refs, parts, order, r, count, has_add, core_zero, shards):
    xs, dys, refs = refs[:parts], refs[parts : 2 * parts], refs[2 * parts :]
    adds = None
    if has_add:
        adds, refs = refs[:2], refs[2:]

    def work():
        value = mm_tn(xs[0][...], dys[0][...])
        for x, dy in zip(xs[1:], dys[1:]):
            value = value + mm_tn(x[...], dy[...])
        if not shards:
            refs[0][...] = value
            return
        keep_ref, send_ref, total = refs
        total[...] = value
        store_shards(scal, total, keep_ref, send_ref, adds, order, r, count, pl.program_id(0))

    if core_zero:
        pl.when(scal[0] == 0)(work)
    else:
        work()


def weight_grad(scal, xs, x_lo, dys, dy_lo, rows, cols, tn, order, add=None, half=None, core_zero=False, shards=True):
    mt, nt = rows // D, cols // tn
    r = rows // 16
    count = 16 if mt == 1 else 4
    depth = xs[0].shape[0]
    kz = 4 if mt == 1 else 1

    def dy_map(m, n, s):
        offset = 0 if half is None else (s[0] if half == "own" else 1 - s[0]) * nt
        return (0, dy_lo // tn + offset + n)

    shard_spec = pl.BlockSpec((2, kz, r, tn), lambda m, n, s: (0, 0 if mt == 1 else m ^ s[3], 0, n))
    if shards:
        out_shape = [sds((2, 4, r, cols), BF16)] * 2
        out_specs = [shard_spec] * 2
        scratch = [pltpu.VMEM((D, tn), F32)]
    else:
        out_shape = sds((rows, cols), F32)
        out_specs = pl.BlockSpec((D, tn), lambda m, n, s: (m, n))
        scratch = []
    return pl.pallas_call(
        functools.partial(
            weight_grad_kernel, parts=len(xs), order=order, r=r, count=count, has_add=add is not None,
            core_zero=core_zero, shards=shards,
        ),
        name="weight_grad",
        out_shape=out_shape,
        grid_spec=pltpu.PrefetchScalarGridSpec(
            num_scalar_prefetch=1,
            grid=(mt, nt),
            in_specs=[pl.BlockSpec((depth, D), lambda m, n, s: (0, x_lo // D + m))] * len(xs)
            + [pl.BlockSpec((depth, tn), dy_map)] * len(xs) + [shard_spec] * (0 if add is None else 2),
            out_specs=out_specs,
            scratch_shapes=scratch,
        ),
        compiler_params=pltpu.CompilerParams(vmem_limit_bytes=VLIMIT),
        cost_estimate=cost(2 * depth * len(xs) * rows * cols, 2 * (depth * (rows + cols) + rows * cols)),
    )(scal, *xs, *dys, *(add or ()))


def patch_grad_kernel(scal, bytes_ref, dpp_ref, *refs, order, shards):
    bytes_f32, total = refs[-2:]

    @pl.when(pl.program_id(0) == 0)
    def _():
        fill_lanes(bytes_f32, bytes_ref)

    byte = scal[0] * (PATCH // 2) + pl.program_id(0)
    x = strided_rows(bytes_f32, byte, MB * PATCHES).astype(BF16)
    value = mm_tn(x, dpp_ref[...])
    if not shards:
        refs[0][...] = value
        return
    total[...] = value
    store_shards(scal, total, refs[0], refs[1], None, order, 192, 4, pl.program_id(0))


def patch_weight_grad(scal, states, dpp, order, shards=True):
    if shards:
        out_shape = [sds((2, 4, 192, D), BF16)] * 2
        out_specs = [pl.BlockSpec((2, 1, 192, D), lambda i, s: (0, i ^ s[3], 0, 0))] * 2
    else:
        out_shape = [sds((PATCH // 2 * D, D), F32)]
        out_specs = [pl.BlockSpec((D, D), lambda i, s: (i, 0))]
    return pl.pallas_call(
        functools.partial(patch_grad_kernel, order=order, shards=shards),
        name="patch_weight_grad",
        out_shape=out_shape,
        grid_spec=pltpu.PrefetchScalarGridSpec(
            num_scalar_prefetch=1,
            grid=(PATCH // 2,),
            in_specs=[const_block(MB * SEQ, D), const_block(MB * PATCHES, D)],
            out_specs=out_specs,
            scratch_shapes=[pltpu.VMEM((LANES, MB * SEQ, 128), F32), pltpu.VMEM((D, D), F32)],
        ),
        compiler_params=pltpu.CompilerParams(vmem_limit_bytes=VLIMIT),
        cost_estimate=cost(1.2e9, 10e6),
    )(scal, states, dpp)


def input_grad_kernel(dpp_ref, dh_ref, wp_hbm, out_ref, acc, wp, psem):
    copies = [
        pltpu.make_async_copy(wp_hbm.at[pl.ds(j * D, D)], wp.at[pl.ds(j * D, D)], psem.at[j]) for j in range(PATCH)
    ]
    for copy in copies:
        copy.start()
    for j in range(PATCH):
        copies[j].wait()
        value = mm_nt(dpp_ref[...], wp[j * D : j * D + D, :])
        for b in range(LANES):
            acc[b, pl.ds(j, PATCHES, stride=PATCH), :] = value[:, b * 128 : b * 128 + 128]
    for b in range(LANES):
        cols = slice(b * 128, b * 128 + 128)
        out_ref[:, cols] = (dh_ref[:, cols] + acc[b]).astype(BF16)


def input_grad_part(dpp_own, dh, patch_weight):
    return pl.pallas_call(
        input_grad_kernel,
        name="input_grad",
        out_shape=sds((SEQ, D), BF16),
        in_specs=[pl.BlockSpec(memory_space=pltpu.VMEM)] * 2 + [ANY],
        out_specs=pl.BlockSpec(memory_space=pltpu.VMEM),
        scratch_shapes=[
            pltpu.VMEM((LANES, SEQ, 128), F32), pltpu.VMEM((PATCH * D, D), BF16), pltpu.SemaphoreType.DMA((PATCH,)),
        ],
        compiler_params=pltpu.CompilerParams(vmem_limit_bytes=VLIMIT),
        cost_estimate=cost(1.2e9, 15e6),
    )(dpp_own, dh, patch_weight)


CORE, X, Y, ZN, ZF, XY = range(6)
QKV, OUT, UP, DOWN = range(4)
ROWS_OF = (D // 16, D // 16, D // 16, FF // 16)
HALF_OF = (3 * D // 2, D // 2, FF // 2, D // 2)
X_LO = (0, D, 2 * D, 3 * D)
DY_LO = (0, 3 * D // 2, 2 * D, 2 * D + FF // 2)
WIDTH_G = (3 * D + D + FF + D) // 2
ROWS_G = MB * PATCHES
UNIT = 384
MESH_ID = pl.DeviceIdType.MESH


class Job:
    def __init__(self, weight, lo, width, axes):
        self.weight, self.lo, self.width, self.axes = weight, lo, width, axes
        self.r = 192 if weight is None else ROWS_OF[weight]


class Alloc:
    def __init__(self):
        self.specs = []

    def __call__(self, shape, dtype):
        self.specs.append(pltpu.VMEM(shape, dtype))
        return len(self.specs) - 1


class Net:
    def __init__(self, send, recv, local):
        self.send, self.recv, self.local, self.count, self.local_count = send, recv, local, 0, 0
        self.core = lax.axis_index("section")
        at = lax.axis_index("dp")
        self.x, self.y, self.z = at % 2, (at // 2) % 2, at // 4
        self.z0, self.z1 = self.z % 2, self.z // 2
        z0, z1 = self.z0, self.z1
        spot = lambda x, y, z: {"dp": z * 4 + y * 2 + x}
        self.partner = (
            {"section": 1 - self.core}, spot(1 - self.x, self.y, self.z), spot(self.x, 1 - self.y, self.z),
            spot(self.x, self.y, 1 - z0 + 2 * z1), spot(self.x, self.y, z0 + 2 - 2 * z1),
            spot(1 - self.x, 1 - self.y, self.z),
        )

    def meet(self):
        barrier = pltpu.get_barrier_semaphore()
        for device in self.partner:
            pl.semaphore_signal(barrier, inc=1, device_id=device, device_id_type=MESH_ID)
        pl.semaphore_wait(barrier, len(self.partner))

    def remote(self, src, dst, to):
        n = self.count
        self.count += 1
        return pltpu.make_async_remote_copy(
            src_ref=src, dst_ref=dst, send_sem=self.send.at[n], recv_sem=self.recv.at[n],
            device_id=self.partner[to], device_id_type=MESH_ID,
        )

    def load(self, src, dst):
        n = self.local_count
        self.local_count += 1
        return pltpu.make_async_copy(src, dst, self.local.at[n])

    def on(self, which, fn):
        pl.when(self.core == which)(fn)

    def z_of(self, k):
        return (self.z0 + k % 2) % 2 + 2 * ((self.z1 + k // 2) % 2)


def lanes(start, size):
    return pl.ds(pl.multiple_of(start, 128), size)


def store_unit(net, total, dst, r, axes, k_tile, cols, add):
    flip = lambda here, other: 1 - here if other else here
    for place in range(4 if k_tile is not None else 16):
        xr, yr = place % 2, place // 2 % 2
        k = place // 4 if k_tile is None else k_tile
        relative = {X: xr, Y: yr, ZN: k % 2, ZF: k // 2}
        shard = flip(net.y, yr) * 2 + flip(net.x, xr)
        if k_tile is None:
            shard = shard + 4 * (flip(net.z0, k % 2) + 2 * flip(net.z1, k // 2))
        index = 0
        for axis in axes:
            index = index * 2 + relative[axis]
        at_dst = (index,) if ZN in axes else (index, relative[ZN])
        at_dst += (slice(None), cols)
        value = total[pl.ds(pl.multiple_of(shard * r, 16), r), :]
        if add:
            value = value + dst[at_dst].astype(F32)
        dst[at_dst] = value.astype(BF16)


def job_buffers(alloc, job, local):
    block = (job.r, job.width) if ZN in job.axes else (2, job.r, job.width)
    count = 2 ** len(job.axes)
    job.own = alloc((count, *block), BF16)
    job.recv = []
    while count > 1:
        count //= 2
        job.recv.append(alloc((count, *block), BF16))
    if local:
        job.peer = alloc((16, *block), BF16)
        job.lf = alloc(block, F32)
        job.lr = alloc(block, F32)


def job_copies(net, b, job, local):
    job.copies = []
    count = 2 ** len(job.axes)
    for axis, recv in zip(job.axes, job.recv):
        job.copies.append(net.remote(b[job.own].at[count // 2 : count], b[recv], axis))
        count //= 2
    if local:
        job.cd = net.remote(b[job.peer], b[job.own], CORE)
        job.c4 = net.remote(b[job.lf], b[job.lr], CORE)


def advance(b, job, i):
    job.copies[i].wait_recv()
    own, recv = b[job.own], b[job.recv[i]]

    @pl.loop(0, 2 ** (len(job.axes) - 1 - i))
    def _(k):
        own[k] = add_low(own[k], recv[k])

    job.copies[i + 1].start()


def last_sum(b, job):
    job.copies[-1].wait_recv()
    return b[job.own][0].astype(F32) + b[job.recv[-1]][0].astype(F32)


def local_sum(net, b, job):
    b[job.lf][...] = last_sum(b, job)
    net.on(0, job.c4.start)


def stage_four(net, b, job, out):
    half = HALF_OF[job.weight]

    def finish():
        job.c4.wait_recv()
        out[:, job.lo : job.lo + job.width] = b[job.lr][...]
        out[:, half + job.lo : half + job.lo + job.width] = b[job.lf][...]

    net.on(1, finish)
    net.on(0, job.c4.wait_send)


def end_job(job):
    for copy in job.copies:
        copy.wait_send()


def local_products(net, b, job, mine, xt, total, x_ref, dy_ref):
    dst = b[job.own if mine else job.peer]
    base = (net.core if mine else 1 - net.core) * HALF_OF[job.weight] + job.lo
    if mine:
        job.cd.wait_recv()
    if job.weight == DOWN:

        @pl.loop(0, 4)
        def _(k):
            xt[...] = x_ref[:, lanes(net.z_of(k) * D, D)].T
            total[...] = mm(xt[...], dy_ref[:, lanes(base, UNIT)])
            store_unit(net, total, dst, job.r, job.axes, k, slice(0, UNIT), mine)
    else:
        if x_ref is not None:
            xt[...] = x_ref[...].T

        @pl.loop(0, job.width // UNIT)
        def _(n):
            total[...] = mm(xt[...], dy_ref[:, lanes(base + n * UNIT, UNIT)])
            store_unit(net, total, dst, job.r, job.axes, None, lanes(n * UNIT, UNIT), mine)

    if mine:
        job.copies[0].start()
        job.cd.wait_send()
    else:
        job.cd.start()


def first_plan():
    alloc = Alloc()
    jobs = [Job(DOWN, 0, 384, (X, Y, ZN, ZF)), Job(UP, 0, 768, (Y, X, ZN, ZF)), Job(UP, 768, 768, (Y, X, ZN, ZF))]
    for job in jobs:
        job_buffers(alloc, job, True)
    s = lambda: None
    s.jobs = jobs
    s.ubuf, s.dz = alloc((SEQ, FF), BF16), alloc((SEQ, FF), BF16)
    s.dm = alloc((SEQ, D), BF16)
    s.xt, s.total = alloc((D, SEQ), BF16), alloc((D, UNIT), F32)
    s.wq, s.wo, s.wu, s.wd = (alloc(w, BF16) for w in ((D, 3 * D), (D, D), (D, FF), (FF, D)))
    s.gp = alloc((2, TILE, FF), BF16)
    s.bytes, s.mid = alloc((2, TILE, D), BF16), alloc((2, TILE, D), F32)
    s.qkv, s.p = alloc((2, TILE, 3 * D), BF16), alloc((2, SUBS, PAIRS, 128, 256), BF16)
    s.dr, s.dqkv, s.dh, s.do = alloc((TILE, D), BF16), alloc((TILE, 3 * D), BF16), alloc((TILE, D), F32), alloc((TILE, D), BF16)
    s.g, s.dg, s.dmg, s.dpp = (alloc((n, D), BF16) for n in (PATCHES, PATCHES, ROWS_G, ROWS_G))
    s.gains = alloc((2, 2, D), F32)
    s.specs = alloc.specs
    return s


def first_kernel(
    u_in, dm_in, c_in, gp_in, states, g_in, mid_in, qkv_in, p_in, gains_own, gains_other,
    wq_own, wo_own, wu_own, wd_own, wq_other, wo_other, wu_other, wd_other,
    start_g, mid_g, qkv_g, p_g, gp_g, pat_in,
    out_up, out_down, dr_out, dqkv_out, dh_out, dpp_out, keep_out, send_out, pat_out, gain_out,
    *refs, plan,
):
    b, (load_sem, tile_sem, send_sem, recv_sem) = refs[:-4], refs[-4:]
    net = Net(send_sem, recv_sem, load_sem)
    s = plan
    core = net.core
    down, up0, up1 = s.jobs
    net.meet()
    for job in s.jobs:
        job_copies(net, b, job, True)
    dg_copy = net.remote(b[s.dg], b[s.dmg].at[PATCHES:ROWS_G, :], CORE)
    pat_copies = [net.remote(pat_in.at[i], pat_out.at[i - 1], to) for i, to in ((1, X), (2, Y), (3, XY))]
    for copy in pat_copies:
        copy.start()

    def load(src, dst):
        copy = net.load(src, dst)
        copy.start()
        return copy

    def load_weight(own, other, dst, swap):
        copy = net.load(own.at[0], dst)
        net.on(0 if swap else 1, copy.start)
        if not swap:
            second = net.load(other.at[0], dst)
            net.on(0, second.start)

        def wait():
            if swap:
                net.on(0, copy.wait)
            else:
                net.on(1, copy.wait)
                net.on(0, second.wait)

        return wait

    u_load, dm_load = load(u_in, b[s.ubuf]), load(dm_in, b[s.dm])
    wd_wait = load_weight(wd_own, wd_other, b[s.wd], False)
    small = [load(g_in, b[s.g]), load(gains_own.at[0], b[s.gains].at[0]), load(gains_other.at[0], b[s.gains].at[1])]
    wu_wait = load_weight(wu_own, wu_other, b[s.wu], False)
    wo_wait = load_weight(wo_own, wo_other, b[s.wo], False)
    wq_wait = load_weight(wq_own, wq_other, b[s.wq], False)

    def tile_copies(t, slot, kinds):
        rows = pl.ds(pl.multiple_of(t * TILE, TILE), TILE)
        seq_rows = pl.ds(pl.multiple_of(core * SEQ + t * TILE, TILE), TILE)
        subs = pl.ds(t * SUBS, SUBS)
        table = (
            (gp_in.at[rows, :], b[s.gp].at[slot]), (states.at[seq_rows, :], b[s.bytes].at[slot]),
            (mid_in.at[rows, :], b[s.mid].at[slot]), (qkv_in.at[rows, :], b[s.qkv].at[slot]),
            (p_in.at[subs], b[s.p].at[slot]),
        )
        return [pltpu.make_async_copy(*table[i], tile_sem.at[slot, i]) for i in kinds]

    def store_copies(t):
        rows = pl.ds(pl.multiple_of(t * TILE, TILE), TILE)
        table = ((b[s.dr], dr_out), (b[s.dqkv], dqkv_out), (b[s.dh], dh_out))
        return [pltpu.make_async_copy(src, dst.at[rows, :], tile_sem.at[2, i]) for i, (src, dst) in enumerate(table)]

    for copy in tile_copies(0, 0, (0, 1, 2, 3, 4)):
        copy.start()
    u_load.wait()
    dm_load.wait()
    local_products(net, b, down, False, b[s.xt], b[s.total], b[s.ubuf], b[s.dm])
    local_products(net, b, down, True, b[s.xt], b[s.total], b[s.ubuf], b[s.dm])
    c_part = b[s.ubuf].at[:, 0:D]
    c_load = load(c_in, c_part)
    wd_wait()

    @pl.loop(0, TILES)
    def _(t):
        slot = t % 2
        tile_copies(t, slot, (0,))[0].wait()

        @pl.when(t + 1 < TILES)
        def _():
            tile_copies(t + 1, 1 - slot, (0,))[0].start()

        rows = pl.ds(pl.multiple_of(t * TILE, TILE), TILE)
        for part in range(FF // D):
            cols = slice(part * D, part * D + D)
            du = mm_nt(b[s.dm][rows, :], b[s.wd][cols, :])
            b[s.dz][rows, cols] = (du * b[s.gp][slot, :, cols].astype(F32)).astype(BF16)

    wd_wait_g = load_weight(wd_own, wd_other, b[s.wd], True)
    c_load.wait()
    local_products(net, b, up0, False, b[s.xt], b[s.total], c_part, b[s.dz])
    local_products(net, b, up1, False, b[s.xt], b[s.total], None, b[s.dz])
    local_products(net, b, up0, True, b[s.xt], b[s.total], None, b[s.dz])
    local_products(net, b, up1, True, b[s.xt], b[s.total], None, b[s.dz])
    for copy in small:
        copy.wait()
    wu_wait()
    wo_wait()
    wq_wait()
    gains = jnp.where(core == 1, b[s.gains][0], b[s.gains][1])
    gain_out[...] = jnp.zeros_like(gain_out)

    def global_loads():
        pairs = (
            (gp_g, b[s.gp].at[0]), (mid_g, b[s.mid].at[0]), (qkv_g, b[s.qkv].at[0]), (p_g, b[s.p].at[0]),
        )
        return [pltpu.make_async_copy(*pair, tile_sem.at[3, i]) for i, pair in enumerate(pairs)]

    @pl.loop(0, TILES)
    def _(t):
        slot = t % 2
        for copy in tile_copies(t, slot, (1, 2, 3, 4)):
            copy.wait()

        @pl.when(t + 1 < TILES)
        def _():
            for copy in tile_copies(t + 1, 1 - slot, (1, 2, 3, 4)):
                copy.start()

        @pl.when((t + 1 == TILES) & (core == 0))
        def _():
            for copy in global_loads():
                copy.start()

        @pl.when(t > 0)
        def _():
            for copy in store_copies(t - 1):
                copy.wait()

        rows = pl.ds(pl.multiple_of(t * TILE, TILE), TILE)
        patch_rows = pl.ds(pl.multiple_of(t * (TILE // PATCH), TILE // PATCH), TILE // PATCH)
        h = b[s.bytes][slot].astype(F32) + mm(spread_matrix(), b[s.g][patch_rows, :])
        dh, dgain = block_backward(
            b[s.dm][rows, :].astype(F32), h, gains, (b[s.wq], b[s.wo], b[s.wu]), lambda i: None,
            b[s.dz].at[rows, :], b[s.mid].at[slot], b[s.qkv].at[slot], b[s.p].at[slot], b[s.do], b[s.dr], b[s.dqkv],
        )
        b[s.dh][...] = dh
        b[s.dg][patch_rows, :] = jnp.sum(dh.reshape(TILE // PATCH, PATCH, D), axis=1).astype(BF16)
        gain_out[2:4, :] += dgain
        for copy in store_copies(t):
            copy.start()

        @pl.when(t == 0)
        def _():
            advance(b, down, 0)

        @pl.when(t == 1)
        def _():
            advance(b, up0, 0)
            advance(b, down, 1)

        @pl.when(t == 2)
        def _():
            advance(b, up1, 0)
            advance(b, down, 2)
            advance(b, up0, 1)

        @pl.when(t == 3)
        def _():
            advance(b, up0, 2)
            advance(b, up1, 1)

    wu_wait_g = load_weight(wu_own, wu_other, b[s.wu], True)
    wo_wait_g = load_weight(wo_own, wo_other, b[s.wo], True)
    wq_wait_g = load_weight(wq_own, wq_other, b[s.wq], True)
    net.on(1, dg_copy.start)
    for copy in store_copies(TILES - 1):
        copy.wait()
    dz_g = b[s.ubuf].at[0:ROWS_G, :]
    wd_wait_g()
    wu_wait_g()
    wo_wait_g()
    wq_wait_g()

    def global_backward():
        start_load = pltpu.make_async_copy(start_g, b[s.mid].at[1], tile_sem.at[3, 4])
        start_load.start()
        for copy in global_loads():
            copy.wait()
        start_load.wait()
        b[s.dmg][0:PATCHES, :] = b[s.dg][...]
        dg_copy.wait_recv()
        for part in range(FF // D):
            cols = slice(part * D, part * D + D)
            du = mm_nt(b[s.dmg][...], b[s.wd][cols, :])
            dz_g[:, cols] = (du * b[s.gp][0, :, cols].astype(F32)).astype(BF16)
        dh, dgain = block_backward(
            b[s.dmg][...].astype(F32), b[s.mid][1], b[s.gains][0], (b[s.wq], b[s.wo], b[s.wu]), lambda i: None,
            dz_g, b[s.mid].at[0], b[s.qkv].at[0], b[s.p].at[0], b[s.do], b[s.dr], b[s.dqkv],
        )
        gain_out[0:2, :] = dgain
        moved = pltpu.roll(dh, ROWS_G - 1, 0)
        row = lax.broadcasted_iota(jnp.int32, (ROWS_G, D), 0)
        b[s.dpp][...] = jnp.where((row & (PATCHES - 1)) == PATCHES - 1, 0.0, moved).astype(BF16)
        for copy in global_stores():
            copy.start()

    def global_stores():
        copies = [pltpu.make_async_copy(b[s.dpp], dpp_out, tile_sem.at[4, 0])]
        lo, n = 0, 1
        for src, width in ((b[s.dqkv], 3 * D // 2), (b[s.dr], D // 2), (dz_g, FF // 2), (b[s.dmg], D // 2)):
            for out, half in ((keep_out, net.z0), (send_out, 1 - net.z0)):
                copies.append(
                    pltpu.make_async_copy(src.at[:, lanes(half * width, width)], out.at[:, lo : lo + width], tile_sem.at[4, n])
                )
                n += 1
            lo += width
        return copies

    net.on(0, global_backward)
    advance(b, up1, 2)
    local_sum(net, b, down)
    local_sum(net, b, up0)
    local_sum(net, b, up1)
    net.on(1, dg_copy.wait_send)
    stage_four(net, b, down, out_down)
    stage_four(net, b, up0, out_up)
    stage_four(net, b, up1, out_up)
    for job in s.jobs:
        end_job(job)
    for copy in pat_copies:
        copy.wait()

    def finish():
        for copy in global_stores():
            copy.wait()

    net.on(0, finish)


def first_part(u, dm, c, gp, states, g, mid, qkv, p, gains, gains_other, weights, other, saved, pat):
    plan = first_plan()
    outs = [
        ((D // 16, FF), F32), ((FF // 16, D), F32), ((SEQ, D), BF16), ((SEQ, 3 * D), BF16), ((SEQ, D), F32),
        ((ROWS_G, D), BF16), ((ROWS_G, WIDTH_G), BF16), ((ROWS_G, WIDTH_G), BF16), ((3, ROWS_G, D), BF16), ((8, D), F32),
    ]
    vmem = pl.BlockSpec(memory_space=pltpu.VMEM)
    operands = (u, dm, c, gp, states, g, mid, qkv, p, gains, gains_other, *weights, *other, *saved, pat)
    return pl.pallas_call(
        functools.partial(first_kernel, plan=plan),
        name="first_part",
        out_shape=[sds(*o) for o in outs],
        in_specs=[ANY] * len(operands),
        out_specs=[vmem] * 2 + [ANY] * 7 + [vmem],
        scratch_shapes=plan.specs + [
            pltpu.SemaphoreType.DMA((32,)), pltpu.SemaphoreType.DMA((5, 9)), pltpu.SemaphoreType.DMA((40,)),
            pltpu.SemaphoreType.DMA((40,)),
        ],
        compiler_params=pltpu.CompilerParams(vmem_limit_bytes=63 * 2**20, collective_id=1, has_side_effects=True),
        cost_estimate=cost(35e9, 80e6),
    )(*operands)


def second_plan():
    alloc = Alloc()
    s = lambda: None
    s.local = [Job(QKV, 0, 768, (X, Y, ZN, ZF)), Job(QKV, 768, 384, (Y, X, ZN, ZF)), Job(OUT, 0, 384, (Y, X, ZN, ZF))]
    s.patch = Job(None, 0, D, (ZN, ZF))
    s.glob = [
        Job(DOWN, 0, 384, (X, Y, ZF)), Job(UP, 0, 768, (Y, X, ZF)), Job(UP, 768, 768, (X, Y, ZF)),
        Job(QKV, 0, 768, (Y, X, ZF)), Job(QKV, 768, 384, (Y, X, ZF)), Job(OUT, 0, 384, (X, Y, ZF)),
    ]
    for job in s.local:
        job_buffers(alloc, job, True)
    job_buffers(alloc, s.patch, False)
    for job in s.glob:
        job_buffers(alloc, job, False)
        job.swap = alloc((2, job.r, job.width), BF16)
    s.dqkv = alloc((SEQ, 3 * D), BF16)
    s.a, s.o, s.dr = (alloc((SEQ, D), BF16) for _ in range(3))
    s.xt, s.total = alloc((D, SEQ), BF16), alloc((D, UNIT), F32)
    s.pat, s.dpp = alloc((4 * ROWS_G, D), BF16), alloc((4 * ROWS_G, D), BF16)
    s.xg, s.xn = alloc((ROWS_G, XG), BF16), alloc((ROWS_G, XG), BF16)
    s.dyk, s.dyn = alloc((ROWS_G, WIDTH_G), BF16), alloc((ROWS_G, WIDTH_G), BF16)
    s.gains = alloc((6, 8, D), F32)
    s.wp, s.dh, s.acc = alloc((2, D, D), BF16), alloc((SEQ, D), F32), alloc((LANES, SEQ, 128), F32)
    s.specs = alloc.specs
    return s


def second_kernel(
    pat_own, pat_in, dpp_in, o_in, dr_in, a_in, dqkv_in, xg_in, xn_in, keep_in, send_in, dh_in, wp_in, gains_in,
    up_in, down_in,
    out_qkv, out_out, out_up, out_down, out_patch, out_gains, out_mine, out_peer, *refs, plan,
):
    b, (load_sem, wp_sem, send_sem, recv_sem) = refs[:-4], refs[-4:]
    net = Net(send_sem, recv_sem, load_sem)
    s = plan
    core = net.core
    q0, q1, proj = s.local
    outs = (out_qkv, out_out, out_up, out_down)
    net.meet()
    for job in s.local:
        job_copies(net, b, job, True)
    job_copies(net, b, s.patch, False)
    for job in s.glob:
        job_copies(net, b, job, False)
        job.swap_copy = net.remote(b[job.swap].at[0], b[job.swap].at[1], ZN)
    gain_copies = [
        net.remote(b[s.gains].at[0], b[s.gains].at[i + 1], to) for i, to in enumerate((CORE, X, Y, ZN, ZF))
    ]
    dpp_slots = [b[s.dpp].at[i * ROWS_G : i * ROWS_G + ROWS_G, :] for i in range(4)]
    dpp_gives = [net.remote(dpp_in, dpp_slots[0], CORE)] + [net.remote(slot, slot, CORE) for slot in dpp_slots[1:]]
    dpp_copies = [net.remote(dpp_in, dpp_slots[i], to) for i, to in ((1, X), (2, Y), (3, XY))]
    dyn_copy = net.remote(send_in, b[s.dyn], ZN)
    grad_copy = net.remote(out_mine, out_peer, CORE)
    dpp_load = net.load(dpp_in, dpp_slots[0])
    global_copies = [net.load(*pair) for pair in ((xg_in, b[s.xg]), (xn_in, b[s.xn]), (keep_in, b[s.dyk]))]

    def give():
        dpp_gives[0].start()
        for copy in dpp_copies:
            copy.start()
        dyn_copy.start()
        dpp_load.start()

    net.on(0, give)
    rest = [net.load(*pair) for pair in ((dqkv_in, b[s.dqkv]), (a_in, b[s.a]), (o_in, b[s.o]), (dr_in, b[s.dr]))]
    pat_loads = [net.load(pat_own.at[0], b[s.pat].at[0:ROWS_G, :])]
    pat_loads += [net.load(pat_in.at[i], b[s.pat].at[(i + 1) * ROWS_G : (i + 2) * ROWS_G, :]) for i in range(3)]
    gain_load = net.load(gains_in, b[s.gains].at[0])
    dh_load = net.load(dh_in, b[s.dh])
    for copy in rest + [gain_load] + pat_loads + [dh_load]:
        copy.start()
    net.on(0, lambda: [copy.start() for copy in global_copies] and None)

    def gain_step(i):
        if i == 0:
            gain_load.wait()
        else:
            gain_copies[i - 1].wait_recv()
            b[s.gains][0] = b[s.gains][0] + b[s.gains][i]
        if i < 5:
            gain_copies[i].start()
            gain_copies[i].wait_send()

    def forward_dpp():
        def work():
            for copy, give_copy in zip(dpp_copies, dpp_gives[1:]):
                copy.wait_recv()
                give_copy.start()

        net.on(0, work)

    def patch_products(job):
        for copy in pat_loads:
            copy.wait()
        b[s.xt][...] = b[s.pat][...].T
        net.on(0, dpp_load.wait)
        net.on(1, dpp_gives[0].wait_recv)
        net.on(1, lambda: [copy.wait_recv() for copy in dpp_gives[1:]] and None)
        for n in range(2):
            cols = slice(n * UNIT, n * UNIT + UNIT)
            b[s.total][...] = mm(b[s.xt][...], b[s.dpp][:, cols])
            for k in range(4):
                z = (1 - net.z0 if k // 2 else net.z0) + 2 * (1 - net.z1 if k % 2 else net.z1)
                b[job.own][k, :, cols] = b[s.total][pl.ds(pl.multiple_of(z * 192, 16), 192), :].astype(BF16)
        job.copies[0].start()

    def global_products(job):
        base = DY_LO[job.weight] + job.lo

        def product(cols, n):
            dy = slice(base + n * UNIT, base + n * UNIT + UNIT)
            return mm_tn(b[s.xg][:, cols], b[s.dyk][:, dy]) + mm_tn(b[s.xn][:, cols], b[s.dyn][:, dy])

        def work():
            if job.weight == DOWN:

                @pl.loop(0, 4)
                def _(k):
                    b[s.total][...] = product(lanes(X_LO[DOWN] + net.z_of(k) * D, D), 0)
                    store_unit(net, b[s.total], b[job.own], job.r, job.axes, k, slice(0, UNIT), False)
            else:
                for n in range(job.width // UNIT):
                    b[s.total][...] = product(slice(X_LO[job.weight], X_LO[job.weight] + D), n)
                    store_unit(
                        net, b[s.total], b[job.own], job.r, job.axes, None, slice(n * UNIT, n * UNIT + UNIT), False
                    )
            job.copies[0].start()

        net.on(0, work)

    def global_advance(job, i):
        net.on(0, lambda: advance(b, job, i))

    def global_sum(job):
        def work():
            value = last_sum(b, job)
            b[job.swap][0] = value[1].astype(BF16)
            job.swap_copy.start()
            outs[job.weight][:, lanes(net.z0 * HALF_OF[job.weight] + job.lo, job.width)] = value[0]

        net.on(0, work)

    def global_end(job):
        def work():
            job.swap_copy.wait_recv()
            cols = lanes((1 - net.z0) * HALF_OF[job.weight] + job.lo, job.width)
            outs[job.weight][:, cols] = b[job.swap][1].astype(F32)

        net.on(0, work)

    def wp_copy(j):
        slot = j % 2
        rows = pl.ds(pl.multiple_of(j * D, D), D)
        return pltpu.make_async_copy(wp_in.at[rows, :], b[s.wp].at[slot], wp_sem.at[slot])

    def input_grads():
        own = pl.ds(pl.multiple_of(core * PATCHES, PATCHES), PATCHES)

        @pl.loop(0, PATCH)
        def _(j):
            wp_copy(j).wait()

            @pl.when(j + 1 < PATCH)
            def _():
                wp_copy(j + 1).start()

            value = mm_nt(b[s.dpp][own, :], b[s.wp][j % 2])
            for i in range(LANES):
                b[s.acc][i, pl.ds(j, PATCHES, stride=PATCH), :] = value[:, i * 128 : i * 128 + 128]

        dh_load.wait()
        for i in range(LANES):
            cols = slice(i * 128, i * 128 + 128)
            out_mine[:, cols] = (b[s.dh][:, cols] + b[s.acc][i]).astype(BF16)
        grad_copy.start()

    def first_wait():
        for copy in global_copies:
            copy.wait()
        dyn_copy.wait_recv()

    wp_copy(0).start()
    g_down, g_up0, g_up1, g_q0, g_q1, g_out = s.glob
    for copy in rest:
        copy.wait()
    xt, total = b[s.xt], b[s.total]
    local_products(net, b, q0, False, xt, total, b[s.a], b[s.dqkv])
    local_products(net, b, q1, False, xt, total, None, b[s.dqkv])
    local_products(net, b, q0, True, xt, total, None, b[s.dqkv])
    local_products(net, b, q1, True, xt, total, None, b[s.dqkv])
    gain_step(0)
    forward_dpp()
    local_products(net, b, proj, False, xt, total, b[s.o], b[s.dr])
    gain_step(1)
    local_products(net, b, proj, True, xt, total, None, b[s.dr])
    patch_products(s.patch)
    net.on(0, first_wait)
    gain_step(2)
    global_products(g_down)
    advance(b, q0, 0)
    global_products(g_up0)
    global_products(g_up1)
    advance(b, q1, 0)
    global_products(g_q0)
    global_products(g_q1)
    global_products(g_out)
    gain_step(3)
    advance(b, proj, 0)
    advance(b, q0, 1)
    advance(b, q1, 1)
    advance(b, proj, 1)
    advance(b, s.patch, 0)
    gain_step(4)
    input_grads()
    gain_step(5)
    advance(b, q0, 2)
    advance(b, q1, 2)
    advance(b, proj, 2)
    global_advance(g_down, 0)
    global_advance(g_up0, 0)
    local_sum(net, b, q0)
    global_advance(g_up1, 0)
    global_advance(g_q0, 0)
    global_advance(g_down, 1)
    global_advance(g_up0, 1)
    local_sum(net, b, q1)
    global_advance(g_q1, 0)
    global_advance(g_out, 0)
    local_sum(net, b, proj)
    global_advance(g_up1, 1)
    global_advance(g_q0, 1)
    out_patch[...] = last_sum(b, s.patch)
    global_advance(g_q1, 1)
    global_advance(g_out, 1)
    global_sum(g_down)
    global_sum(g_up0)
    stage_four(net, b, q0, out_qkv)
    stage_four(net, b, q1, out_qkv)
    stage_four(net, b, proj, out_out)
    out_gains[...] = b[s.gains][0]

    def copy_first():
        out_up[...] = up_in[...]
        out_down[...] = down_in[...]

    net.on(1, copy_first)
    global_sum(g_up1)
    global_sum(g_q0)
    global_sum(g_q1)
    global_sum(g_out)
    for job in s.glob:
        global_end(job)
    for job in s.local + [s.patch]:
        end_job(job)
    grad_copy.wait()

    def drain():
        for copy in dpp_gives + dpp_copies + [dyn_copy]:
            copy.wait_send()
        for job in s.glob:
            end_job(job)
            job.swap_copy.wait_send()

    net.on(0, drain)


def second_part(*operands):
    plan = second_plan()
    outs = [((ROWS_OF[w], 2 * HALF_OF[w]), F32) for w in (QKV, OUT, UP, DOWN)] + [((192, D), F32), ((8, D), F32)]
    outs += [((SEQ, D), BF16)] * 2
    vmem = pl.BlockSpec(memory_space=pltpu.VMEM)
    return pl.pallas_call(
        functools.partial(second_kernel, plan=plan),
        name="second_part",
        out_shape=[sds(*o) for o in outs],
        in_specs=[ANY] * (len(operands) - 2) + [vmem] * 2,
        out_specs=[vmem] * len(outs),
        scratch_shapes=plan.specs + [
            pltpu.SemaphoreType.DMA((16,)), pltpu.SemaphoreType.DMA((2,)), pltpu.SemaphoreType.DMA((64,)),
            pltpu.SemaphoreType.DMA((64,)),
        ],
        compiler_params=pltpu.CompilerParams(vmem_limit_bytes=63 * 2**20, collective_id=2, has_side_effects=True),
        cost_estimate=cost(15e9, 60e6),
    )(*operands)


def swap_core(value):
    return lax.ppermute(value, "section", [(0, 1), (1, 0)])


def hop(value, mask, cores):
    size = lax.axis_size("dp")
    if cores == (0, 1):
        return lax.ppermute(value, "dp", [(i, i ^ mask) for i in range(size)])
    pairs = [(c * size + i, c * size + (i ^ mask)) for c in cores for i in range(size)]
    return lax.ppermute(value, ("section", "dp"), pairs)


HOPS = {"x": 1, "y": 2}


def body(states, lengths, patch_weight, w_qkv, w_out, w_up, w_down, gains, cotangent):
    size = lax.axis_size("dp")
    fast = size == 16
    core = lax.axis_index("section")
    at = lax.axis_index("dp")
    mx, my, mz = at % 2, (at // 2) % 2, (at // 4) % 4
    length = jnp.where(core == 0, lengths[0], lengths[1])
    scal = jnp.stack([core, mx, my, mz, length]).astype(jnp.int32)
    weights = (w_qkv, w_out, w_up, w_down)
    other = tuple(swap_core(w) for w in weights)
    gains_other = swap_core(gains)

    g_all, xg, start, qkv_g, p_g, mid_g, gp_g, pat = global_forward(scal, states, gains, patch_weight, weights)
    g_recv = swap_core(g_all[PATCHES:])
    g_own = jnp.where(core == 0, g_all[:PATCHES], g_recv)
    if fast:
        xg_next = hop(xg, 4, (0,))

    y, dm, a, qkv, p, o, mid, c, u, gp = local_forward(
        scal, states, cotangent, g_own, gains, weights, gains_other, other
    )
    y_recv = swap_core(y)
    g_rows = jnp.broadcast_to(g_all[:, None, :], (MB * PATCHES, PATCH, D)).reshape(MB * SEQ, D)
    section_outputs = jnp.where(core == 0, g_rows, jnp.concatenate([y_recv, y], axis=0))[None]

    saved = (start, mid_g, qkv_g, p_g, gp_g)
    if fast:
        up_l, down_l, dr, dqkv, dh, dpp, dy_keep, dy_send, pat_next, gain_parts = first_part(
            u, dm, c, gp, states, g_own, mid, qkv, p, gains, gains_other, weights, other, saved, pat
        )
        *grads, patch_grad, gain_sums, own_grad, peer_grad = second_part(
            pat, pat_next, dpp, o, dr, a, dqkv, xg, xg_next, dy_keep, dy_send, dh, patch_weight, gain_parts, up_l, down_l
        )
        outs = tuple(g[None] for g in grads)
    else:
        dz = local_dz(scal, dm, gp, w_down, other[3])
        dr, dqkv, dh, dg, dgain_l = local_backward(
            scal, dz, dm, states, g_own, mid, qkv, p, gains, weights[:3], gains_other, other[:3]
        )
        dpp, dy_keep, dy_send, dgain_g = global_backward(scal, (dg, swap_core(dg)), saved, gains, weights)
        gain_parts = jnp.concatenate([dgain_g[:2], dgain_l[:2], jnp.zeros((4, D), F32)], axis=0)
        dpp = jnp.where(core == 0, dpp, swap_core(dpp))
        own_grad = input_grad_part(jnp.where(core == 0, dpp[:PATCHES], dpp[PATCHES:]), dh, patch_weight)
        peer_grad = swap_core(own_grad)
        gain_sums = lax.psum(gain_parts, ("section", "dp"))
        (patch_half,) = patch_weight_grad(scal, states, dpp, "xy", shards=False)
        patch_grad = lax.psum_scatter(patch_half, "dp", scatter_dimension=0, tiled=True)
        half = D // 2
        swap_halves = lambda keep, send, lo, width: jnp.where(
            mx == 0,
            jnp.concatenate([keep[:, lo : lo + width], send[:, lo : lo + width]], axis=1),
            jnp.concatenate([send[:, lo : lo + width], keep[:, lo : lo + width]], axis=1),
        )

        def whole_grad(x_lo, dy_lo, x, dy, rows, cols):
            dy_g = swap_halves(dy_keep, dy_send, dy_lo, cols // 2)
            glob = weight_grad(scal, [xg], x_lo, [dy_g], 0, rows, cols, 384, "xy", shards=False)
            loc = weight_grad(scal, [x], 0, [dy], 0, rows, cols, 384, "xy", shards=False)
            total = jnp.where(core == 0, glob, loc + swap_core(loc))
            return lax.psum_scatter(total, "dp", scatter_dimension=0, tiled=True)[None]

        outs = (
            whole_grad(0, 0, a, dqkv, D, 3 * D),
            whole_grad(D, 3 * half, o, dr, D, D),
            whole_grad(2 * D, 4 * half, c, dz, D, FF),
            whole_grad(3 * D, 8 * half, u, dm, FF, D),
        )
    input_grad = jnp.where(
        core == 0, jnp.concatenate([own_grad, peer_grad]), jnp.concatenate([peer_grad, own_grad])
    ).astype(F32)
    share = D // size
    own_gains = jnp.where(core == 0, gain_sums[0:2], gain_sums[2:4])
    gain_grad = lax.dynamic_slice(own_gains, (0, at * share), (2, share))
    return (section_outputs, input_grad, patch_grad, *outs, gain_grad[None])


def solution(mesh):
    return jax.shard_map(
        body,
        mesh=mesh,
        in_specs=(
            P("dp", None), P("dp"), P(), P("section", None, None), P("section", None, None),
            P("section", None, None), P("section", None, None), P("section", None, None), P("dp", None),
        ),
        out_specs=(
            P("section", "dp", None), P("dp", None), P(("section", "dp"), None), P("section", "dp", None),
            P("section", "dp", None), P("section", "dp", None), P("section", "dp", None), P("section", None, "dp"),
        ),
        check_vma=False,
    )
```

```python
import functools

import jax
import jax.numpy as jnp
from jax import lax
from jax.experimental import pallas as pl
from jax.experimental.pallas import tpu as pltpu
from jax.sharding import PartitionSpec as P

D = 768
HEADS = 12
HDIM = 64
FF = 3072
PATCH = 8
SEQ = 1024
PATCHES = SEQ // PATCH
TILE = 256
SUBS = TILE // 128
PAIRS = HEADS // 2
TILES = SEQ // TILE
MB = 2
XG = 3 * D + FF
F32 = jnp.float32
BF16 = jnp.bfloat16
ANY = pl.BlockSpec(memory_space=pl.ANY)
VLIMIT = 56 * 2**20


def sds(shape, dtype):
    return jax.ShapeDtypeStruct(shape, dtype)


def mm(a, b):
    return jnp.dot(a, b, preferred_element_type=F32)


def mm_nt(a, b):
    return lax.dot_general(a, b, (((1,), (1,)), ((), ())), preferred_element_type=F32)


def mm_tn(a, b):
    return lax.dot_general(a, b, (((0,), (0,)), ((), ())), preferred_element_type=F32)


def normalized(v):
    centered = v - jnp.mean(v, axis=-1, keepdims=True)
    scale = lax.rsqrt(jnp.mean(centered * centered, axis=-1, keepdims=True) + 1e-5)
    return centered * scale, scale


def norm_backward(grad, gain, hat, scale):
    scaled = grad * gain
    inner = scaled - jnp.mean(scaled, axis=-1, keepdims=True)
    inner = inner - hat * jnp.mean(scaled * hat, axis=-1, keepdims=True)
    return inner * scale, jnp.sum(grad * hat, axis=0, keepdims=True)


def gelu_pair(z):
    cdf = 0.5 + 0.5 * lax.erf(z * 0.7071067811865476)
    bell = jnp.exp2(z * z * (-0.5 * 1.4426950408889634))
    return z * cdf, cdf + z * (bell * 0.3989422804014327)


def lane_masks():
    lane = lax.broadcasted_iota(jnp.int32, (128, 128), 1)
    first = jnp.where(lane < HDIM, 1.0, 0.0)
    return first.astype(BF16), (1.0 - first).astype(BF16), lane < HDIM


def split_heads(v, first, second):
    return jnp.concatenate([v * first, v * second], axis=0)


def attention_forward(qkv_ref, o_ref, p_ref, shift):
    first, second, _ = lane_masks()
    key = lax.broadcasted_iota(jnp.int32, (128, 128), 0)
    query = lax.broadcasted_iota(jnp.int32, (128, 128), 1)
    allowed = (key <= query) & ((key >> shift) == (query >> shift))
    for sub in range(SUBS):
        rows = slice(sub * 128, sub * 128 + 128)
        scores, probs = [], []
        for lo in range(0, D, 128):
            k2 = split_heads(qkv_ref[rows, D + lo : D + lo + 128], first, second)
            scores.append(mm_nt(k2, qkv_ref[rows, lo : lo + 128]) * 0.125)
        for pair in range(PAIRS):
            parts = []
            for half in range(2):
                sh = jnp.where(allowed, scores[pair][half * 128 : half * 128 + 128], -1e30)
                e = jnp.exp(sh - jnp.max(sh, axis=0, keepdims=True))
                parts.append(e * (1.0 / jnp.sum(e, axis=0, keepdims=True)))
            probs.append(jnp.concatenate(parts, axis=0).astype(BF16))
            p_ref[sub, pair] = probs[pair]
        for pair in range(PAIRS):
            lo = pair * 128
            v2 = split_heads(qkv_ref[rows, 2 * D + lo : 2 * D + lo + 128], first, second)
            o_ref[rows, lo : lo + 128] = mm_tn(probs[pair], v2).astype(BF16)


def attention_backward(qkv_ref, p_ref, do_ref, dqkv_ref):
    first, second, is_first = lane_masks()
    for sub in range(SUBS):
        rows = slice(sub * 128, sub * 128 + 128)
        dps, dss = [], []
        for lo in range(0, D, 128):
            v2 = split_heads(qkv_ref[rows, 2 * D + lo : 2 * D + lo + 128], first, second)
            dps.append(mm_nt(v2, do_ref[rows, lo : lo + 128]))
        for pair in range(PAIRS):
            pf = p_ref[sub, pair].astype(F32)
            weighted = pf * dps[pair]
            parts = []
            for half in range(2):
                keys = slice(half * 128, half * 128 + 128)
                parts.append(weighted[keys] - pf[keys] * jnp.sum(weighted[keys], axis=0, keepdims=True))
            dss.append(jnp.concatenate(parts, axis=0).astype(BF16))
        for pair in range(PAIRS):
            lo = pair * 128
            k2 = split_heads(qkv_ref[rows, D + lo : D + lo + 128], first, second)
            dq = mm_tn(dss[pair], k2) * 0.125
            dk2 = mm(dss[pair], qkv_ref[rows, lo : lo + 128]) * 0.125
            dv2 = mm(p_ref[sub, pair], do_ref[rows, lo : lo + 128])
            dqkv_ref[rows, lo : lo + 128] = dq.astype(BF16)
            dqkv_ref[rows, D + lo : D + lo + 128] = jnp.where(is_first, dk2[:128], dk2[128:]).astype(BF16)
            dqkv_ref[rows, 2 * D + lo : 2 * D + lo + 128] = jnp.where(is_first, dv2[:128], dv2[128:]).astype(BF16)


def block_forward(h, gains, w, wait, shift, a_ref, qkv_ref, p_ref, o_ref, mid_ref, c_ref, u_ref, gp_ref):
    wq, wo, wu, wd = w
    a_ref[...] = (normalized(h)[0] * gains[0:1, :]).astype(BF16)
    wait(0)
    for part in range(3):
        cols = slice(part * D, part * D + D)
        qkv_ref[:, cols] = mm(a_ref[...], wq[:, cols]).astype(BF16)
    attention_forward(qkv_ref, o_ref, p_ref, shift)
    wait(1)
    mid = h + mm(o_ref[...], wo[...])
    mid_ref[...] = mid
    c_ref[...] = (normalized(mid)[0] * gains[1:2, :]).astype(BF16)
    wait(2)
    for part in range(FF // D):
        cols = slice(part * D, part * D + D)
        u, gp = gelu_pair(mm(c_ref[...], wu[:, cols]))
        u_ref[:, cols] = u.astype(BF16)
        gp_ref[:, cols] = gp.astype(BF16)
    wait(3)
    return mid_ref[...] + mm(u_ref[...], wd[...])


def backward_upper(dout, gains, wo, wu, dz_ref, mid_ref, dr_ref, do_ref, dmid_ref):
    hat, scale = normalized(mid_ref[...])
    dc = mm_nt(dz_ref[...], wu[...])
    back, dgain = norm_backward(dc, gains[1:2, :], hat, scale)
    dmid_ref[...] = dout + back
    dr_ref[...] = dmid_ref[...].astype(BF16)
    do_ref[...] = mm_nt(dr_ref[...], wo[...]).astype(BF16)
    return dgain


def backward_lower(h, gains, wq, qkv_ref, p_ref, do_ref, dqkv_ref, dmid_ref):
    attention_backward(qkv_ref, p_ref, do_ref, dqkv_ref)
    da = mm_nt(dqkv_ref[...], wq[...])
    hat, scale = normalized(h)
    back, dgain = norm_backward(da, gains[0:1, :], hat, scale)
    return dmid_ref[...] + back, dgain


def block_backward(dout, h, gains, w, wait, dz_ref, mid_ref, qkv_ref, p_ref, do_ref, dr_ref, dqkv_ref, dmid_ref):
    wq, wo, wu = w
    for i in (2, 1, 0):
        wait(i)
    dgain_two = backward_upper(dout, gains, wo, wu, dz_ref, mid_ref, dr_ref, do_ref, dmid_ref)
    dh, dgain_one = backward_lower(h, gains, wq, qkv_ref, p_ref, do_ref, dqkv_ref, dmid_ref)
    return dh, jnp.concatenate([dgain_one, dgain_two], axis=0)


LANES = D // 128


def fill_lanes(dst, src):
    for b in range(LANES):
        dst[b] = src[:, b * 128 : b * 128 + 128].astype(F32)


def strided_rows(ref, start, rows):
    picked = [ref[b, pl.ds(start, rows, stride=PATCH), :] for b in range(LANES)]
    return jnp.concatenate(picked, axis=1)


def spread_matrix():
    row = lax.broadcasted_iota(jnp.int32, (TILE, TILE // PATCH), 0) // PATCH
    col = lax.broadcasted_iota(jnp.int32, (TILE, TILE // PATCH), 1)
    return jnp.where(row == col, 1.0, 0.0).astype(BF16)


def add_low(a, b):
    return (a.astype(F32) + b.astype(F32)).astype(BF16)


def cost(flops, nbytes):
    return pl.CostEstimate(flops=int(flops), bytes_accessed=int(nbytes), transcendentals=0)


WSCRATCH = {
    "q": pltpu.VMEM((D, 3 * D), BF16),
    "o": pltpu.VMEM((D, D), BF16),
    "u": pltpu.VMEM((D, FF), BF16),
    "d": pltpu.VMEM((FF, D), BF16),
}


def global_forward_kernel(
    scal, bytes_ref, gains_ref, wp_hbm, wq_hbm, wo_hbm, wu_hbm, wd_hbm,
    g_ref, x_ref, start_ref, qkv_ref, p_ref, mid_ref, gp_ref, pat_ref,
    bytes_f32, wp, wq, wo, wu, wd, psem, wsem,
):
    rows = MB * PATCHES
    fill_lanes(bytes_f32, bytes_ref)

    def share_out(j, t):
        xj = strided_rows(bytes_f32, j, rows).astype(BF16)
        for piece in range(4):
            relative = (piece % 2) ^ scal[1] | (((piece // 2) ^ scal[2]) << 1)
            pat_ref[relative, :, t * 192 : t * 192 + 192] = xj[:, piece * 192 : piece * 192 + 192]
        return xj

    @pl.when(scal[0] == 1)
    def _():
        for t in range(PATCH // 2):
            share_out(PATCH // 2 + t, t)

    @pl.when(scal[0] == 0)
    def _():
        pcopies = [
            pltpu.make_async_copy(wp_hbm.at[pl.ds(j * D, D)], wp.at[pl.ds(j * D, D)], psem.at[j])
            for j in range(PATCH)
        ]
        wcopies = [
            pltpu.make_async_copy(src.at[0], dst, wsem.at[i])
            for i, (src, dst) in enumerate(((wq_hbm, wq), (wo_hbm, wo), (wu_hbm, wu), (wd_hbm, wd)))
        ]
        for copy in pcopies + wcopies:
            copy.start()
        acc = jnp.zeros((rows, D), F32)
        for j in range(PATCH):
            pcopies[j].wait()
            xj = share_out(j, j) if j < PATCH // 2 else strided_rows(bytes_f32, j, rows).astype(BF16)
            acc = acc + mm(xj, wp[j * D : j * D + D, :])
        moved = pltpu.roll(acc, 1, 0)
        row = lax.broadcasted_iota(jnp.int32, (rows, D), 0)
        start_ref[...] = jnp.where((row & (PATCHES - 1)) == 0, 0.0, moved)
        out = block_forward(
            start_ref[...], gains_ref[0], (wq, wo, wu, wd), lambda i: wcopies[i].wait(), 7,
            x_ref.at[:, 0:D], qkv_ref, p_ref, x_ref.at[:, D : 2 * D], mid_ref,
            x_ref.at[:, 2 * D : 3 * D], x_ref.at[:, 3 * D : 3 * D + FF], gp_ref,
        )
        g_ref[...] = out.astype(BF16)


def global_forward(scal, states, gains, patch_weight, weights):
    rows = MB * PATCHES
    full = lambda *shape: pl.BlockSpec(shape, lambda i, s: (0,) * len(shape), pipeline_mode=pl.Buffered(1))
    outs = (
        ((rows, D), BF16), ((rows, XG), BF16), ((rows, D), F32), ((rows, 3 * D), BF16),
        ((SUBS, PAIRS, 256, 128), BF16), ((rows, D), F32), ((rows, FF), BF16),
        ((4, rows, D), BF16),
    )
    return pl.pallas_call(
        global_forward_kernel,
        name="global_forward",
        out_shape=[sds(*o) for o in outs],
        grid_spec=pltpu.PrefetchScalarGridSpec(
            num_scalar_prefetch=1,
            grid=(1,),
            in_specs=[full(MB * SEQ, D), full(1, 2, D)] + [ANY] * 5,
            out_specs=[full(*o[0]) for o in outs],
            scratch_shapes=[
                pltpu.VMEM((LANES, MB * SEQ, 128), F32), pltpu.VMEM((PATCH * D, D), BF16),
                WSCRATCH["q"], WSCRATCH["o"], WSCRATCH["u"], WSCRATCH["d"],
                pltpu.SemaphoreType.DMA((PATCH,)), pltpu.SemaphoreType.DMA((4,)),
            ],
        ),
        compiler_params=pltpu.CompilerParams(vmem_limit_bytes=VLIMIT),
        cost_estimate=cost(6e9, 32e6),
    )(scal, states, gains, patch_weight, *weights)


def global_backward_kernel(
    scal, dg0_ref, dg1_ref, start_ref, mid_ref, qkv_ref, p_ref, gp_ref, gains_ref, wq_hbm, wo_hbm, wu_hbm, wd_hbm,
    dpp_ref, keep_ref, send_ref, dgain_ref,
    dm_s, dz_s, do_s, dr_s, dqkv_s, dmid_s, wq, wo, wu, wd, wsem,
):
    @pl.when(scal[0] == 0)
    def _():
        rows = MB * PATCHES
        wcopies = [
            pltpu.make_async_copy(src.at[0], dst, wsem.at[i])
            for i, (src, dst) in enumerate(((wq_hbm, wq), (wo_hbm, wo), (wu_hbm, wu), (wd_hbm, wd)))
        ]
        for i in (3, 2, 1, 0):
            wcopies[i].start()
        dm_s[0:PATCHES, :] = dg0_ref[...]
        dm_s[PATCHES:, :] = dg1_ref[...]
        wcopies[3].wait()
        for part in range(FF // D):
            cols = slice(part * D, part * D + D)
            du = mm_nt(dm_s[...], wd[cols, :])
            dz_s[:, cols] = (du * gp_ref[:, cols].astype(F32)).astype(BF16)
        dh, dgain = block_backward(
            dm_s[...].astype(F32), start_ref[...], gains_ref[0], (wq, wo, wu), lambda i: wcopies[i].wait(),
            dz_s, mid_ref, qkv_ref, p_ref, do_s, dr_s, dqkv_s, dmid_s,
        )
        dgain_ref[...] = jnp.zeros_like(dgain_ref)
        dgain_ref[0:2, :] = dgain
        moved = pltpu.roll(dh, rows - 1, 0)
        row = lax.broadcasted_iota(jnp.int32, (rows, D), 0)
        dpp_ref[...] = jnp.where((row & (PATCHES - 1)) == PATCHES - 1, 0.0, moved).astype(BF16)
        for half in range(2):
            def fill(ref):
                lo = 0
                for src, width in ((dqkv_s, 3 * D // 2), (dr_s, D // 2), (dz_s, FF // 2), (dm_s, D // 2)):
                    ref[:, lo : lo + width] = src[:, half * width : half * width + width]
                    lo += width
            pl.when(scal[1] == half)(functools.partial(fill, keep_ref))
            pl.when(scal[1] != half)(functools.partial(fill, send_ref))

    @pl.when(scal[0] != 0)
    def _():
        dgain_ref[...] = jnp.zeros_like(dgain_ref)


def global_backward(scal, dgs, saved, gains, weights):
    rows = MB * PATCHES
    full = lambda *shape: pl.BlockSpec(shape, lambda i, s: (0,) * len(shape), pipeline_mode=pl.Buffered(1))
    width = (3 * D + D + FF + D) // 2
    outs = (((rows, D), BF16), ((rows, width), BF16), ((rows, width), BF16), ((8, D), F32))
    return pl.pallas_call(
        global_backward_kernel,
        name="global_backward",
        out_shape=[sds(*o) for o in outs],
        grid_spec=pltpu.PrefetchScalarGridSpec(
            num_scalar_prefetch=1,
            grid=(1,),
            in_specs=[full(PATCHES, D)] * 2 + [full(*v.shape) for v in saved] + [full(1, 2, D)] + [ANY] * 4,
            out_specs=[full(*o[0]) for o in outs],
            scratch_shapes=[
                pltpu.VMEM((rows, D), BF16), pltpu.VMEM((rows, FF), BF16), pltpu.VMEM((rows, D), BF16),
                pltpu.VMEM((rows, D), BF16), pltpu.VMEM((rows, 3 * D), BF16), pltpu.VMEM((rows, D), F32),
                WSCRATCH["q"], WSCRATCH["o"], WSCRATCH["u"], WSCRATCH["d"],
                pltpu.SemaphoreType.DMA((4,)),
            ],
        ),
        compiler_params=pltpu.CompilerParams(vmem_limit_bytes=VLIMIT),
        cost_estimate=cost(6e9, 24e6),
    )(scal, *dgs, *saved, gains, *weights)


def start_weights(scal, pairs, sems, order):
    step = pl.program_id(0)
    for i in order:
        own, recv, dst = pairs[i]

        @pl.when((step == 0) & (scal[0] == 1))
        def _(own=own, dst=dst, i=i):
            pltpu.make_async_copy(own.at[0], dst, sems.at[i]).start()

        @pl.when((step == 0) & (scal[0] == 0))
        def _(recv=recv, dst=dst, i=i):
            pltpu.make_async_copy(recv.at[0], dst, sems.at[i]).start()

    def wait(i):
        @pl.when(step == 0)
        def _():
            pltpu.make_async_copy(pairs[i][1].at[0], pairs[i][2], sems.at[i]).wait()

    return wait


def live_rows(scal):
    step = pl.program_id(0)
    row = lax.broadcasted_iota(jnp.int32, (TILE, D), 0) + step * TILE
    return row < scal[4]


def local_forward_kernel(
    scal, bytes_ref, cot_ref, g_ref, gains_ref, wq_a, wo_a, wu_a, wd_a, wq_b, wo_b, wu_b, wd_b, gains_b,
    y_ref, dm_ref, a_ref, qkv_ref, p_ref, o_ref, mid_ref, c_ref, u_ref, gp_ref,
    wq, wo, wu, wd, wsem,
):
    pairs = ((wq_a, wq_b, wq), (wo_a, wo_b, wo), (wu_a, wu_b, wu), (wd_a, wd_b, wd))
    wait = start_weights(scal, pairs, wsem, (0, 1, 2, 3))
    gains = jnp.where(scal[0] == 1, gains_ref[0], gains_b[0])
    h = bytes_ref[...].astype(F32) + mm(spread_matrix(), g_ref[...])
    out = block_forward(h, gains, (wq, wo, wu, wd), wait, 3, a_ref, qkv_ref, p_ref, o_ref, mid_ref, c_ref, u_ref, gp_ref)
    live = live_rows(scal)
    y_ref[...] = jnp.where(live, out, 0.0).astype(BF16)
    dm_ref[...] = jnp.where(live, cot_ref[...].astype(F32), 0.0).astype(BF16)


def row_block(*shape):
    return pl.BlockSpec(shape, lambda i, s: (i,) + (0,) * (len(shape) - 1))


def const_block(*shape):
    return pl.BlockSpec(shape, lambda i, s: (0,) * len(shape), pipeline_mode=pl.Buffered(1))


def seq_block():
    return pl.BlockSpec((TILE, D), lambda i, s: (s[0] * TILES + i, 0))


def local_forward(scal, states, cotangent, g_own, gains, weights, gains_b, weights_b):
    outs = (
        ((SEQ, D), BF16), ((SEQ, D), BF16), ((SEQ, D), BF16), ((SEQ, 3 * D), BF16),
        ((SEQ // 128, PAIRS, 256, 128), BF16), ((SEQ, D), BF16), ((SEQ, D), F32), ((SEQ, D), BF16),
        ((SEQ, FF), BF16), ((SEQ, FF), BF16),
    )
    return pl.pallas_call(
        local_forward_kernel,
        name="local_forward",
        out_shape=[sds(*o) for o in outs],
        grid_spec=pltpu.PrefetchScalarGridSpec(
            num_scalar_prefetch=1,
            grid=(TILES,),
            in_specs=[seq_block(), seq_block(), row_block(TILE // PATCH, D), const_block(1, 2, D)]
            + [ANY] * 8 + [const_block(1, 2, D)],
            out_specs=[row_block(o[0][0] // TILES, *o[0][1:]) for o in outs],
            scratch_shapes=[
                WSCRATCH["q"], WSCRATCH["o"], WSCRATCH["u"], WSCRATCH["d"], pltpu.SemaphoreType.DMA((4,)),
            ],
        ),
        compiler_params=pltpu.CompilerParams(vmem_limit_bytes=VLIMIT),
        cost_estimate=cost(14.5e9, 60e6),
    )(scal, states, cotangent, g_own, gains, *weights, *weights_b, gains_b)


def local_dz_kernel(scal, dm_ref, gp_ref, wd_a, wd_b, dz_ref, wd, wsem):
    wait = start_weights(scal, ((wd_a, wd_b, wd),), wsem, (0,))
    wait(0)
    for part in range(FF // D):
        cols = slice(part * D, part * D + D)
        du = mm_nt(dm_ref[...], wd[cols, :])
        dz_ref[:, cols] = (du * gp_ref[:, cols].astype(F32)).astype(BF16)


def local_dz(scal, dm, gp, wd_a, wd_b):
    return pl.pallas_call(
        local_dz_kernel,
        name="local_dz",
        out_shape=sds((SEQ, FF), BF16),
        grid_spec=pltpu.PrefetchScalarGridSpec(
            num_scalar_prefetch=1,
            grid=(TILES,),
            in_specs=[row_block(TILE, D), row_block(TILE, FF), ANY, ANY],
            out_specs=row_block(TILE, FF),
            scratch_shapes=[WSCRATCH["d"], pltpu.SemaphoreType.DMA((1,))],
        ),
        compiler_params=pltpu.CompilerParams(vmem_limit_bytes=VLIMIT),
        cost_estimate=cost(4.8e9, 18e6),
    )(scal, dm, gp, wd_a, wd_b)


def local_backward_kernel(
    scal, dz_ref, dm_ref, bytes_ref, g_ref, mid_ref, qkv_ref, p_ref, gains_ref,
    wq_a, wo_a, wu_a, wq_b, wo_b, wu_b, gains_b,
    dr_ref, dqkv_ref, dh_ref, dg_ref, dgain_ref,
    do_s, wq, wo, wu, wsem,
):
    pairs = ((wq_a, wq_b, wq), (wo_a, wo_b, wo), (wu_a, wu_b, wu))
    wait = start_weights(scal, pairs, wsem, (2, 1, 0))
    gains = jnp.where(scal[0] == 1, gains_ref[0], gains_b[0])
    h = bytes_ref[...].astype(F32) + mm(spread_matrix(), g_ref[...])
    dh, dgain = block_backward(
        dm_ref[...].astype(F32), h, gains, (wq, wo, wu), wait, dz_ref, mid_ref, qkv_ref, p_ref, do_s, dr_ref, dqkv_ref,
        dh_ref,
    )
    dh_ref[...] = dh
    dg_ref[...] = jnp.sum(dh.reshape(TILE // PATCH, PATCH, D), axis=1).astype(BF16)

    @pl.when(pl.program_id(0) == 0)
    def _():
        dgain_ref[...] = jnp.zeros_like(dgain_ref)

    dgain_ref[0:2, :] += dgain


def local_backward(scal, dz, dm, states, g_own, mid, qkv, p, gains, weights, gains_b, weights_b):
    outs = (
        ((SEQ, D), BF16), ((SEQ, 3 * D), BF16), ((SEQ, D), F32), ((PATCHES, D), BF16), ((8, D), F32),
    )
    return pl.pallas_call(
        local_backward_kernel,
        name="local_backward",
        out_shape=[sds(*o) for o in outs],
        grid_spec=pltpu.PrefetchScalarGridSpec(
            num_scalar_prefetch=1,
            grid=(TILES,),
            in_specs=[
                row_block(TILE, FF), row_block(TILE, D), seq_block(), row_block(TILE // PATCH, D), row_block(TILE, D),
                row_block(TILE, 3 * D), row_block(SUBS, PAIRS, 256, 128), const_block(1, 2, D),
            ] + [ANY] * 6 + [const_block(1, 2, D)],
            out_specs=[row_block(o[0][0] // TILES, *o[0][1:]) for o in outs[:4]] + [const_block(8, D)],
            scratch_shapes=[
                pltpu.VMEM((TILE, D), BF16), WSCRATCH["q"], WSCRATCH["o"], WSCRATCH["u"], pltpu.SemaphoreType.DMA((3,)),
            ],
        ),
        compiler_params=pltpu.CompilerParams(vmem_limit_bytes=VLIMIT),
        cost_estimate=cost(10e9, 50e6),
    )(scal, dz, dm, states, g_own, mid, qkv, p, gains, *weights, *weights_b, gains_b)


def store_shards(scal, total, keep_ref, send_ref, add_refs, order, r, count, z):
    first, second = order
    position = {"x": scal[1], "y": scal[2]}
    for one in range(2):
        for two in range(2):
            at = {first: one ^ position[first], second: two ^ position[second]}
            for k in range(count // 4):
                level = (k ^ scal[3]) * 4 if count == 16 else 0
                shard = level + at["y"] * 2 + at["x"]
                value = total[pl.ds(pl.multiple_of(shard * r, 16), r), :]
                if add_refs is not None:
                    value = value + add_refs[one][two, k].astype(F32)
                (send_ref if one else keep_ref)[two, k] = value.astype(BF16)


def weight_grad_kernel(scal, *refs, parts, order, r, count, has_add, core_zero, shards):
    xs, dys, refs = refs[:parts], refs[parts : 2 * parts], refs[2 * parts :]
    adds = None
    if has_add:
        adds, refs = refs[:2], refs[2:]

    def work():
        value = mm_tn(xs[0][...], dys[0][...])
        for x, dy in zip(xs[1:], dys[1:]):
            value = value + mm_tn(x[...], dy[...])
        if not shards:
            refs[0][...] = value
            return
        keep_ref, send_ref, total = refs
        total[...] = value
        store_shards(scal, total, keep_ref, send_ref, adds, order, r, count, pl.program_id(0))

    if core_zero:
        pl.when(scal[0] == 0)(work)
    else:
        work()


def weight_grad(scal, xs, x_lo, dys, dy_lo, rows, cols, tn, order, add=None, half=None, core_zero=False, shards=True):
    mt, nt = rows // D, cols // tn
    r = rows // 16
    count = 16 if mt == 1 else 4
    depth = xs[0].shape[0]
    kz = 4 if mt == 1 else 1

    def dy_map(m, n, s):
        offset = 0 if half is None else (s[0] if half == "own" else 1 - s[0]) * nt
        return (0, dy_lo // tn + offset + n)

    shard_spec = pl.BlockSpec((2, kz, r, tn), lambda m, n, s: (0, 0 if mt == 1 else m ^ s[3], 0, n))
    if shards:
        out_shape = [sds((2, 4, r, cols), BF16)] * 2
        out_specs = [shard_spec] * 2
        scratch = [pltpu.VMEM((D, tn), F32)]
    else:
        out_shape = sds((rows, cols), F32)
        out_specs = pl.BlockSpec((D, tn), lambda m, n, s: (m, n))
        scratch = []
    return pl.pallas_call(
        functools.partial(
            weight_grad_kernel, parts=len(xs), order=order, r=r, count=count, has_add=add is not None,
            core_zero=core_zero, shards=shards,
        ),
        name="weight_grad",
        out_shape=out_shape,
        grid_spec=pltpu.PrefetchScalarGridSpec(
            num_scalar_prefetch=1,
            grid=(mt, nt),
            in_specs=[pl.BlockSpec((depth, D), lambda m, n, s: (0, x_lo // D + m))] * len(xs)
            + [pl.BlockSpec((depth, tn), dy_map)] * len(xs) + [shard_spec] * (0 if add is None else 2),
            out_specs=out_specs,
            scratch_shapes=scratch,
        ),
        compiler_params=pltpu.CompilerParams(vmem_limit_bytes=VLIMIT),
        cost_estimate=cost(2 * depth * len(xs) * rows * cols, 2 * (depth * (rows + cols) + rows * cols)),
    )(scal, *xs, *dys, *(add or ()))


def patch_grad_kernel(scal, bytes_ref, dpp_ref, *refs, order, shards):
    bytes_f32, total = refs[-2:]

    @pl.when(pl.program_id(0) == 0)
    def _():
        fill_lanes(bytes_f32, bytes_ref)

    byte = scal[0] * (PATCH // 2) + pl.program_id(0)
    x = strided_rows(bytes_f32, byte, MB * PATCHES).astype(BF16)
    value = mm_tn(x, dpp_ref[...])
    if not shards:
        refs[0][...] = value
        return
    total[...] = value
    store_shards(scal, total, refs[0], refs[1], None, order, 192, 4, pl.program_id(0))


def patch_weight_grad(scal, states, dpp, order, shards=True):
    if shards:
        out_shape = [sds((2, 4, 192, D), BF16)] * 2
        out_specs = [pl.BlockSpec((2, 1, 192, D), lambda i, s: (0, i ^ s[3], 0, 0))] * 2
    else:
        out_shape = [sds((PATCH // 2 * D, D), F32)]
        out_specs = [pl.BlockSpec((D, D), lambda i, s: (i, 0))]
    return pl.pallas_call(
        functools.partial(patch_grad_kernel, order=order, shards=shards),
        name="patch_weight_grad",
        out_shape=out_shape,
        grid_spec=pltpu.PrefetchScalarGridSpec(
            num_scalar_prefetch=1,
            grid=(PATCH // 2,),
            in_specs=[const_block(MB * SEQ, D), const_block(MB * PATCHES, D)],
            out_specs=out_specs,
            scratch_shapes=[pltpu.VMEM((LANES, MB * SEQ, 128), F32), pltpu.VMEM((D, D), F32)],
        ),
        compiler_params=pltpu.CompilerParams(vmem_limit_bytes=VLIMIT),
        cost_estimate=cost(1.2e9, 10e6),
    )(scal, states, dpp)


def input_grad_kernel(dpp_ref, dh_ref, wp_hbm, out_ref, acc, wp, psem):
    copies = [
        pltpu.make_async_copy(wp_hbm.at[pl.ds(j * D, D)], wp.at[pl.ds(j * D, D)], psem.at[j]) for j in range(PATCH)
    ]
    for copy in copies:
        copy.start()
    for j in range(PATCH):
        copies[j].wait()
        value = mm_nt(dpp_ref[...], wp[j * D : j * D + D, :])
        for b in range(LANES):
            acc[b, pl.ds(j, PATCHES, stride=PATCH), :] = value[:, b * 128 : b * 128 + 128]
    for b in range(LANES):
        cols = slice(b * 128, b * 128 + 128)
        out_ref[:, cols] = (dh_ref[:, cols] + acc[b]).astype(BF16)


def input_grad_part(dpp_own, dh, patch_weight):
    return pl.pallas_call(
        input_grad_kernel,
        name="input_grad",
        out_shape=sds((SEQ, D), BF16),
        in_specs=[pl.BlockSpec(memory_space=pltpu.VMEM)] * 2 + [ANY],
        out_specs=pl.BlockSpec(memory_space=pltpu.VMEM),
        scratch_shapes=[
            pltpu.VMEM((LANES, SEQ, 128), F32), pltpu.VMEM((PATCH * D, D), BF16), pltpu.SemaphoreType.DMA((PATCH,)),
        ],
        compiler_params=pltpu.CompilerParams(vmem_limit_bytes=VLIMIT),
        cost_estimate=cost(1.2e9, 15e6),
    )(dpp_own, dh, patch_weight)


CORE, X, Y, ZN, ZF, XY = range(6)
QKV, OUT, UP, DOWN = range(4)
ROWS_OF = (D // 16, D // 16, D // 16, FF // 16)
HALF_OF = (3 * D // 2, D // 2, FF // 2, D // 2)
X_LO = (0, D, 2 * D, 3 * D)
DY_LO = (0, 3 * D // 2, 2 * D, 2 * D + FF // 2)
WIDTH_G = (3 * D + D + FF + D) // 2
ROWS_G = MB * PATCHES
UNIT = 384
MESH_ID = pl.DeviceIdType.MESH


class Job:
    def __init__(self, weight, lo, width, axes):
        self.weight, self.lo, self.width, self.axes = weight, lo, width, axes
        self.r = 192 if weight is None else ROWS_OF[weight]


class Alloc:
    def __init__(self):
        self.specs = []

    def __call__(self, shape, dtype):
        self.specs.append(pltpu.VMEM(shape, dtype))
        return len(self.specs) - 1


class Net:
    def __init__(self, send, recv, local):
        self.send, self.recv, self.local, self.count, self.local_count = send, recv, local, 0, 0
        self.core = lax.axis_index("section")
        at = lax.axis_index("dp")
        self.x, self.y, self.z = at % 2, (at // 2) % 2, at // 4
        self.z0, self.z1 = self.z % 2, self.z // 2
        z0, z1 = self.z0, self.z1
        spot = lambda x, y, z: {"dp": z * 4 + y * 2 + x}
        self.partner = (
            {"section": 1 - self.core}, spot(1 - self.x, self.y, self.z), spot(self.x, 1 - self.y, self.z),
            spot(self.x, self.y, 1 - z0 + 2 * z1), spot(self.x, self.y, z0 + 2 - 2 * z1),
            spot(1 - self.x, 1 - self.y, self.z),
        )

    def meet(self):
        barrier = pltpu.get_barrier_semaphore()
        for device in self.partner:
            pl.semaphore_signal(barrier, inc=1, device_id=device, device_id_type=MESH_ID)
        pl.semaphore_wait(barrier, len(self.partner))

    def remote(self, src, dst, to):
        n = self.count
        self.count += 1
        return pltpu.make_async_remote_copy(
            src_ref=src, dst_ref=dst, send_sem=self.send.at[n], recv_sem=self.recv.at[n],
            device_id=self.partner[to], device_id_type=MESH_ID,
        )

    def load(self, src, dst):
        n = self.local_count
        self.local_count += 1
        return pltpu.make_async_copy(src, dst, self.local.at[n])

    def on(self, which, fn):
        pl.when(self.core == which)(fn)

    def z_of(self, k):
        return (self.z0 + k % 2) % 2 + 2 * ((self.z1 + k // 2) % 2)


def lanes(start, size):
    return pl.ds(pl.multiple_of(start, 128), size)


def store_unit(net, total, dst, r, axes, k_tile, cols, add):
    flip = lambda here, other: 1 - here if other else here
    for place in range(4 if k_tile is not None else 16):
        xr, yr = place % 2, place // 2 % 2
        k = place // 4 if k_tile is None else k_tile
        relative = {X: xr, Y: yr, ZN: k % 2, ZF: k // 2}
        shard = flip(net.y, yr) * 2 + flip(net.x, xr)
        if k_tile is None:
            shard = shard + 4 * (flip(net.z0, k % 2) + 2 * flip(net.z1, k // 2))
        index = 0
        for axis in axes:
            index = index * 2 + relative[axis]
        at_dst = (index,) if ZN in axes else (index, relative[ZN])
        at_dst += (slice(None), cols)
        value = total[pl.ds(pl.multiple_of(shard * r, 16), r), :]
        if add:
            value = value + dst[at_dst].astype(F32)
        dst[at_dst] = value.astype(BF16)


def job_buffers(alloc, job, local):
    block = (job.r, job.width) if ZN in job.axes else (2, job.r, job.width)
    count = 2 ** len(job.axes)
    job.own = alloc((count, *block), BF16)
    job.recv = []
    while count > 1:
        count //= 2
        job.recv.append(alloc((count, *block), BF16))
    if local:
        job.peer = alloc((16, *block), BF16)
        job.lf = alloc(block, F32)
        job.lr = alloc(block, F32)


def job_copies(net, b, job, local):
    job.copies = []
    count = 2 ** len(job.axes)
    for axis, recv in zip(job.axes, job.recv):
        job.copies.append(net.remote(b[job.own].at[count // 2 : count], b[recv], axis))
        count //= 2
    if local:
        job.cd = net.remote(b[job.peer], b[job.own], CORE)
        job.c4 = net.remote(b[job.lf], b[job.lr], CORE)


def advance(b, job, i):
    job.copies[i].wait_recv()
    own, recv = b[job.own], b[job.recv[i]]

    @pl.loop(0, 2 ** (len(job.axes) - 1 - i))
    def _(k):
        own[k] = add_low(own[k], recv[k])

    job.copies[i + 1].start()


def last_sum(b, job):
    job.copies[-1].wait_recv()
    return b[job.own][0].astype(F32) + b[job.recv[-1]][0].astype(F32)


def local_sum(net, b, job):
    b[job.lf][...] = last_sum(b, job)
    net.on(0, job.c4.start)


def stage_four(net, b, job, out):
    half = HALF_OF[job.weight]

    def finish():
        job.c4.wait_recv()
        out[:, job.lo : job.lo + job.width] = b[job.lr][...]
        out[:, half + job.lo : half + job.lo + job.width] = b[job.lf][...]

    net.on(1, finish)
    net.on(0, job.c4.wait_send)


def end_job(job):
    for copy in job.copies:
        copy.wait_send()


def local_products(net, b, jobs, mine, xt, total, x_ref, dy_ref):
    buffer = lambda job: b[job.own if mine else job.peer]
    job = jobs[0]
    base = (net.core if mine else 1 - net.core) * HALF_OF[job.weight] + job.lo
    if mine:
        for job in jobs:
            job.cd.wait_recv()
    if job.weight == DOWN:

        @pl.loop(0, 4)
        def _(k):
            xt[...] = x_ref[:, lanes(net.z_of(k) * D, D)].T
            total[...] = mm(xt[...], dy_ref[:, lanes(base, UNIT)])
            for job in jobs:
                part = total.at[:, job.lo : job.lo + job.width]
                store_unit(net, part, buffer(job), job.r, job.axes, k, slice(0, job.width), mine)
    else:
        if x_ref is not None:
            xt[...] = x_ref[...].T

        @pl.loop(0, job.width // UNIT)
        def _(n):
            total[...] = mm(xt[...], dy_ref[:, lanes(base + n * UNIT, UNIT)])
            store_unit(net, total, buffer(job), job.r, job.axes, None, lanes(n * UNIT, UNIT), mine)

    for job in jobs:
        if mine:
            job.copies[0].start()
            job.cd.wait_send()
        else:
            job.cd.start()


def first_plan():
    alloc = Alloc()
    jobs = [
        Job(DOWN, 0, 256, (X, Y, ZN, ZF)), Job(DOWN, 256, 128, (Y, X, ZN, ZF)),
        Job(UP, 0, 768, (X, Y, ZN, ZF)), Job(UP, 768, 768, (X, Y, ZN, ZF)),
    ]
    for job in jobs:
        job_buffers(alloc, job, True)
    s = lambda: None
    s.jobs = jobs
    s.ubuf, s.dz = alloc((SEQ, FF), BF16), alloc((SEQ, FF), BF16)
    s.dm = alloc((SEQ, D), BF16)
    s.xt, s.total = alloc((D, SEQ), BF16), alloc((D, UNIT), F32)
    s.wq, s.wo, s.wu, s.wd = (alloc(w, BF16) for w in ((D, 3 * D), (D, D), (D, FF), (FF, D)))
    s.gp = alloc((2, TILE, FF), BF16)
    s.bytes, s.mid = alloc((2, TILE, D), BF16), alloc((2, TILE, D), F32)
    s.qkv, s.p = alloc((2, TILE, 3 * D), BF16), alloc((2, SUBS, PAIRS, 256, 128), BF16)
    s.dr, s.dqkv, s.dh, s.do = alloc((TILE, D), BF16), alloc((TILE, 3 * D), BF16), alloc((TILE, D), F32), alloc((TILE, D), BF16)
    s.g, s.dg, s.dmg, s.dpp = (alloc((n, D), BF16) for n in (PATCHES, PATCHES, ROWS_G, ROWS_G))
    s.gains = alloc((2, 2, D), F32)
    s.specs = alloc.specs
    return s


def first_kernel(
    u_in, dm_in, c_in, gp_in, states, g_in, mid_in, qkv_in, p_in, gains_own, gains_other,
    wq_own, wo_own, wu_own, wd_own, wq_other, wo_other, wu_other, wd_other,
    start_g, mid_g, qkv_g, p_g, gp_g, pat_in,
    out_up, out_down, dr_out, dqkv_out, dh_out, dpp_out, keep_out, send_out, pat_out, gain_out,
    *refs, plan,
):
    b, (load_sem, tile_sem, send_sem, recv_sem) = refs[:-4], refs[-4:]
    net = Net(send_sem, recv_sem, load_sem)
    s = plan
    core = net.core
    down0, down1, up0, up1 = s.jobs
    net.meet()
    for job in s.jobs:
        job_copies(net, b, job, True)
    dg_copy = net.remote(b[s.dg], b[s.dmg].at[PATCHES:ROWS_G, :], CORE)
    pat_copies = [net.remote(pat_in.at[i], pat_out.at[i - 1], to) for i, to in ((1, X), (2, Y), (3, XY))]
    for copy in pat_copies:
        copy.start()

    def load(src, dst):
        copy = net.load(src, dst)
        copy.start()
        return copy

    def load_weight(own, other, dst, swap):
        copy = net.load(own.at[0], dst)
        net.on(0 if swap else 1, copy.start)
        if not swap:
            second = net.load(other.at[0], dst)
            net.on(0, second.start)

        def wait():
            if swap:
                net.on(0, copy.wait)
            else:
                net.on(1, copy.wait)
                net.on(0, second.wait)

        return wait

    u_load, dm_load = load(u_in, b[s.ubuf]), load(dm_in, b[s.dm])
    wd_wait = load_weight(wd_own, wd_other, b[s.wd], False)
    small = [load(g_in, b[s.g]), load(gains_own.at[0], b[s.gains].at[0]), load(gains_other.at[0], b[s.gains].at[1])]
    wu_wait = load_weight(wu_own, wu_other, b[s.wu], False)
    wo_wait = load_weight(wo_own, wo_other, b[s.wo], False)
    wq_wait = load_weight(wq_own, wq_other, b[s.wq], False)

    def tile_copies(t, slot, kinds):
        rows = pl.ds(pl.multiple_of(t * TILE, TILE), TILE)
        seq_rows = pl.ds(pl.multiple_of(core * SEQ + t * TILE, TILE), TILE)
        subs = pl.ds(t * SUBS, SUBS)
        table = (
            (gp_in.at[rows, :], b[s.gp].at[slot]), (states.at[seq_rows, :], b[s.bytes].at[slot]),
            (mid_in.at[rows, :], b[s.mid].at[slot]), (qkv_in.at[rows, :], b[s.qkv].at[slot]),
            (p_in.at[subs], b[s.p].at[slot]),
        )
        return [pltpu.make_async_copy(*table[i], tile_sem.at[slot, i]) for i in kinds]

    def store_copies(t):
        rows = pl.ds(pl.multiple_of(t * TILE, TILE), TILE)
        table = ((b[s.dr], dr_out), (b[s.dqkv], dqkv_out), (b[s.dh], dh_out))
        return [pltpu.make_async_copy(src, dst.at[rows, :], tile_sem.at[2, i]) for i, (src, dst) in enumerate(table)]

    for copy in tile_copies(0, 0, (0, 1, 2, 3, 4)):
        copy.start()
    u_load.wait()
    dm_load.wait()
    xt, total = b[s.xt], b[s.total]

    def dz_tiles(first, last):
        @pl.loop(first, last)
        def _(t):
            slot = t % 2
            tile_copies(t, slot, (0,))[0].wait()

            @pl.when(t + 1 < TILES)
            def _():
                tile_copies(t + 1, 1 - slot, (0,))[0].start()

            rows = pl.ds(pl.multiple_of(t * TILE, TILE), TILE)
            for part in range(FF // D):
                cols = slice(part * D, part * D + D)
                du = mm_nt(b[s.dm][rows, :], b[s.wd][cols, :])
                b[s.dz][rows, cols] = (du * b[s.gp][slot, :, cols].astype(F32)).astype(BF16)

    local_products(net, b, [down0, down1], False, xt, total, b[s.ubuf], b[s.dm])
    wd_wait()
    dz_tiles(0, 2)
    local_products(net, b, [down0, down1], True, xt, total, b[s.ubuf], b[s.dm])
    c_part = b[s.ubuf].at[:, 0:D]
    c_load = load(c_in, c_part)
    dz_tiles(2, TILES)
    wd_wait_g = load_weight(wd_own, wd_other, b[s.wd], True)
    c_load.wait()
    local_products(net, b, [up0], False, xt, total, c_part, b[s.dz])
    local_products(net, b, [up1], False, xt, total, None, b[s.dz])
    advance(b, down1, 0)
    local_products(net, b, [up0], True, xt, total, None, b[s.dz])
    local_products(net, b, [up1], True, xt, total, None, b[s.dz])
    for copy in small:
        copy.wait()
    wu_wait()
    wo_wait()
    wq_wait()
    gains = jnp.where(core == 1, b[s.gains][0], b[s.gains][1])
    gain_out[...] = jnp.zeros_like(gain_out)

    def global_loads():
        pairs = (
            (gp_g, b[s.gp].at[0]), (mid_g, b[s.mid].at[0]), (qkv_g, b[s.qkv].at[0]), (p_g, b[s.p].at[0]),
        )
        return [pltpu.make_async_copy(*pair, tile_sem.at[3, i]) for i, pair in enumerate(pairs)]

    @pl.loop(0, TILES)
    def _(t):
        slot = t % 2
        for copy in tile_copies(t, slot, (1, 2, 3, 4)):
            copy.wait()

        @pl.when(t + 1 < TILES)
        def _():
            for copy in tile_copies(t + 1, 1 - slot, (1, 2, 3, 4)):
                copy.start()

        @pl.when((t + 1 == TILES) & (core == 0))
        def _():
            for copy in global_loads():
                copy.start()

        @pl.when(t > 0)
        def _():
            for copy in store_copies(t - 1):
                copy.wait()

        rows = pl.ds(pl.multiple_of(t * TILE, TILE), TILE)
        patch_rows = pl.ds(pl.multiple_of(t * (TILE // PATCH), TILE // PATCH), TILE // PATCH)
        h = b[s.bytes][slot].astype(F32) + mm(spread_matrix(), b[s.g][patch_rows, :])
        dh, dgain = block_backward(
            b[s.dm][rows, :].astype(F32), h, gains, (b[s.wq], b[s.wo], b[s.wu]), lambda i: None,
            b[s.dz].at[rows, :], b[s.mid].at[slot], b[s.qkv].at[slot], b[s.p].at[slot], b[s.do], b[s.dr], b[s.dqkv],
            b[s.dh],
        )
        b[s.dh][...] = dh
        b[s.dg][patch_rows, :] = jnp.sum(dh.reshape(TILE // PATCH, PATCH, D), axis=1).astype(BF16)
        gain_out[2:4, :] += dgain
        for copy in store_copies(t):
            copy.start()

        @pl.when(t == 0)
        def _():
            advance(b, down1, 1)
            advance(b, down0, 0)

        @pl.when(t == 1)
        def _():
            advance(b, down1, 2)

        @pl.when(t == 2)
        def _():
            local_sum(net, b, down1)
            advance(b, down0, 1)
            advance(b, up0, 0)

        @pl.when(t == 3)
        def _():
            advance(b, down0, 2)
            advance(b, up0, 1)
            advance(b, up1, 0)

    wu_wait_g = load_weight(wu_own, wu_other, b[s.wu], True)
    wo_wait_g = load_weight(wo_own, wo_other, b[s.wo], True)
    wq_wait_g = load_weight(wq_own, wq_other, b[s.wq], True)
    net.on(1, dg_copy.start)
    for copy in store_copies(TILES - 1):
        copy.wait()
    dz_g = b[s.ubuf].at[0:ROWS_G, :]
    wd_wait_g()
    wu_wait_g()
    wo_wait_g()
    wq_wait_g()

    start_load = pltpu.make_async_copy(start_g, b[s.mid].at[1], tile_sem.at[3, 4])

    def global_upper():
        start_load.start()
        for copy in global_loads():
            copy.wait()
        b[s.dmg][0:PATCHES, :] = b[s.dg][...]
        dg_copy.wait_recv()
        for part in range(FF // D):
            cols = slice(part * D, part * D + D)
            du = mm_nt(b[s.dmg][...], b[s.wd][cols, :])
            dz_g[:, cols] = (du * b[s.gp][0, :, cols].astype(F32)).astype(BF16)
        gain_out[1:2, :] = backward_upper(
            b[s.dmg][...].astype(F32), b[s.gains][0], b[s.wo], b[s.wu], dz_g, b[s.mid].at[0], b[s.dr], b[s.do], b[s.dh]
        )

    def global_lower():
        start_load.wait()
        dh, dgain = backward_lower(
            b[s.mid][1], b[s.gains][0], b[s.wq], b[s.qkv].at[0], b[s.p].at[0], b[s.do], b[s.dqkv], b[s.dh]
        )
        gain_out[0:1, :] = dgain
        moved = pltpu.roll(dh, ROWS_G - 1, 0)
        row = lax.broadcasted_iota(jnp.int32, (ROWS_G, D), 0)
        b[s.dpp][...] = jnp.where((row & (PATCHES - 1)) == PATCHES - 1, 0.0, moved).astype(BF16)
        for copy in global_stores():
            copy.start()

    def global_stores():
        copies = [pltpu.make_async_copy(b[s.dpp], dpp_out, tile_sem.at[4, 0])]
        lo, n = 0, 1
        for src, width in ((b[s.dqkv], 3 * D // 2), (b[s.dr], D // 2), (dz_g, FF // 2), (b[s.dmg], D // 2)):
            for out, half in ((keep_out, net.z0), (send_out, 1 - net.z0)):
                copies.append(
                    pltpu.make_async_copy(src.at[:, lanes(half * width, width)], out.at[:, lo : lo + width], tile_sem.at[4, n])
                )
                n += 1
            lo += width
        return copies

    net.on(0, global_upper)
    local_sum(net, b, down0)
    advance(b, up0, 2)
    advance(b, up1, 1)
    net.on(0, global_lower)
    stage_four(net, b, down1, out_down)
    stage_four(net, b, down0, out_down)
    local_sum(net, b, up0)
    advance(b, up1, 2)
    stage_four(net, b, up0, out_up)
    local_sum(net, b, up1)
    net.on(1, dg_copy.wait_send)
    stage_four(net, b, up1, out_up)
    for job in s.jobs:
        end_job(job)
    for copy in pat_copies:
        copy.wait()

    def finish():
        for copy in global_stores():
            copy.wait()

    net.on(0, finish)


def first_part(u, dm, c, gp, states, g, mid, qkv, p, gains, gains_other, weights, other, saved, pat):
    plan = first_plan()
    outs = [
        ((D // 16, FF), F32), ((FF // 16, D), F32), ((SEQ, D), BF16), ((SEQ, 3 * D), BF16), ((SEQ, D), F32),
        ((ROWS_G, D), BF16), ((ROWS_G, WIDTH_G), BF16), ((ROWS_G, WIDTH_G), BF16), ((3, ROWS_G, D), BF16), ((8, D), F32),
    ]
    vmem = pl.BlockSpec(memory_space=pltpu.VMEM)
    operands = (u, dm, c, gp, states, g, mid, qkv, p, gains, gains_other, *weights, *other, *saved, pat)
    return pl.pallas_call(
        functools.partial(first_kernel, plan=plan),
        name="first_part",
        out_shape=[sds(*o) for o in outs],
        in_specs=[ANY] * len(operands),
        out_specs=[vmem] * 2 + [ANY] * 7 + [vmem],
        scratch_shapes=plan.specs + [
            pltpu.SemaphoreType.DMA((32,)), pltpu.SemaphoreType.DMA((5, 9)), pltpu.SemaphoreType.DMA((40,)),
            pltpu.SemaphoreType.DMA((40,)),
        ],
        compiler_params=pltpu.CompilerParams(vmem_limit_bytes=63 * 2**20, collective_id=1, has_side_effects=True),
        cost_estimate=cost(35e9, 80e6),
    )(*operands)


def second_plan():
    alloc = Alloc()
    s = lambda: None
    s.local = [Job(QKV, 0, 768, (X, Y, ZN, ZF)), Job(QKV, 768, 384, (X, Y, ZN, ZF)), Job(OUT, 0, 384, (Y, X, ZN, ZF))]
    s.patch = Job(None, 0, D, (ZN, ZF))
    s.glob = [
        Job(DOWN, 0, 384, (Y, X, ZF)), Job(UP, 0, 768, (X, Y, ZF)), Job(UP, 768, 768, (Y, X, ZF)),
        Job(QKV, 0, 768, (Y, X, ZF)), Job(QKV, 768, 384, (Y, X, ZF)), Job(OUT, 0, 384, (Y, X, ZF)),
    ]
    for job in s.local:
        job_buffers(alloc, job, True)
    job_buffers(alloc, s.patch, False)
    for job in s.glob:
        job_buffers(alloc, job, False)
        job.swap = alloc((2, job.r, job.width), BF16)
    s.dqkv = alloc((SEQ, 3 * D), BF16)
    s.a, s.o, s.dr = (alloc((SEQ, D), BF16) for _ in range(3))
    s.xt, s.xo, s.total = alloc((D, SEQ), BF16), alloc((D, SEQ), BF16), alloc((D, UNIT), F32)
    s.pat, s.dpp = alloc((4 * ROWS_G, D), BF16), alloc((4 * ROWS_G, D), BF16)
    s.xg, s.xn = alloc((ROWS_G, XG), BF16), alloc((ROWS_G, XG), BF16)
    s.dyk, s.dyn = alloc((ROWS_G, WIDTH_G), BF16), alloc((ROWS_G, WIDTH_G), BF16)
    s.gains = alloc((6, 8, D), F32)
    s.g, s.spread = alloc((ROWS_G, D), BF16), alloc((2, TILE, D), BF16)
    s.wp, s.acc = alloc((2, D, D), BF16), alloc((LANES, SEQ, 128), F32)
    s.specs = alloc.specs
    return s


def second_kernel(
    pat_own, pat_in, dpp_in, o_in, dr_in, a_in, dqkv_in, xg_in, xn_in, keep_in, send_in, dh_in, wp_in, g_in, y_in,
    gains_in, up_in, down_in,
    out_qkv, out_out, out_up, out_down, out_patch, out_gains, out_mine, out_peer, out_rows, *refs, plan,
):
    b, (load_sem, wp_sem, row_sem, send_sem, recv_sem) = refs[:-5], refs[-5:]
    net = Net(send_sem, recv_sem, load_sem)
    s = plan
    core = net.core
    q0, q1, proj = s.local
    outs = (out_qkv, out_out, out_up, out_down)
    net.meet()
    for job in s.local:
        job_copies(net, b, job, True)
    job_copies(net, b, s.patch, False)
    for job in s.glob:
        job_copies(net, b, job, False)
        job.swap_copy = net.remote(b[job.swap].at[0], b[job.swap].at[1], ZN)
    gain_copies = [
        net.remote(b[s.gains].at[0], b[s.gains].at[i + 1], to) for i, to in enumerate((CORE, X, Y, ZN, ZF))
    ]
    dpp_slots = [b[s.dpp].at[i * ROWS_G : i * ROWS_G + ROWS_G, :] for i in range(4)]
    dpp_gives = [net.remote(dpp_in, dpp_slots[0], CORE)] + [net.remote(slot, slot, CORE) for slot in dpp_slots[1:]]
    dpp_copies = [net.remote(dpp_in, dpp_slots[i], to) for i, to in ((1, X), (2, Y), (3, XY))]
    dyn_copy = net.remote(send_in, b[s.dyn], ZN)
    grad_copy = net.remote(out_mine, out_peer, CORE)
    y_copy = net.remote(y_in, out_rows.at[0:SEQ, :], CORE)
    y_own = net.load(y_in, out_rows.at[SEQ : MB * SEQ, :])
    g_load = net.load(g_in, b[s.g])
    dpp_load = net.load(dpp_in, dpp_slots[0])
    global_copies = [net.load(*pair) for pair in ((xg_in, b[s.xg]), (xn_in, b[s.xn]), (keep_in, b[s.dyk]))]

    def give():
        dpp_gives[0].start()
        for copy in dpp_copies:
            copy.start()
        dyn_copy.start()
        dpp_load.start()
        g_load.start()
        y_copy.start()

    net.on(0, give)
    net.on(1, y_own.start)
    rest = [net.load(*pair) for pair in ((dqkv_in, b[s.dqkv]), (a_in, b[s.a]), (o_in, b[s.o]), (dr_in, b[s.dr]))]
    pat_loads = [net.load(pat_own.at[0], b[s.pat].at[0:ROWS_G, :])]
    pat_loads += [net.load(pat_in.at[i], b[s.pat].at[(i + 1) * ROWS_G : (i + 2) * ROWS_G, :]) for i in range(3)]
    gain_load = net.load(gains_in, b[s.gains].at[0])
    dh_loads = [net.load(dh_in.at[:, i * 128 : i * 128 + 128], b[s.acc].at[i]) for i in range(LANES)]
    for copy in rest + [gain_load] + pat_loads + dh_loads:
        copy.start()
    net.on(0, lambda: [copy.start() for copy in global_copies] and None)

    def gain_step(i):
        if i == 0:
            gain_load.wait()
        else:
            gain_copies[i - 1].wait_recv()
            b[s.gains][0] = b[s.gains][0] + b[s.gains][i]
        if i < 5:
            gain_copies[i].start()
            gain_copies[i].wait_send()

    def forward_dpp():
        def work():
            for copy, give_copy in zip(dpp_copies, dpp_gives[1:]):
                copy.wait_recv()
                give_copy.start()

        net.on(0, work)

    def patch_products(job):
        for copy in pat_loads:
            copy.wait()
        b[s.xt][...] = b[s.pat][...].T
        net.on(1, lambda: [copy.wait_recv() for copy in dpp_gives[1:]] and None)
        for n in range(2):
            cols = slice(n * UNIT, n * UNIT + UNIT)
            b[s.total][...] = mm(b[s.xt][...], b[s.dpp][:, cols])
            for k in range(4):
                z = (1 - net.z0 if k // 2 else net.z0) + 2 * (1 - net.z1 if k % 2 else net.z1)
                b[job.own][k, :, cols] = b[s.total][pl.ds(pl.multiple_of(z * 192, 16), 192), :].astype(BF16)
        job.copies[0].start()

    def global_products(job):
        base = DY_LO[job.weight] + job.lo

        def product(cols, n):
            dy = slice(base + n * UNIT, base + n * UNIT + UNIT)
            return mm_tn(b[s.xg][:, cols], b[s.dyk][:, dy]) + mm_tn(b[s.xn][:, cols], b[s.dyn][:, dy])

        def work():
            if job.weight == DOWN:

                @pl.loop(0, 4)
                def _(k):
                    b[s.total][...] = product(lanes(X_LO[DOWN] + net.z_of(k) * D, D), 0)
                    store_unit(net, b[s.total], b[job.own], job.r, job.axes, k, slice(0, UNIT), False)
            else:
                for n in range(job.width // UNIT):
                    b[s.total][...] = product(slice(X_LO[job.weight], X_LO[job.weight] + D), n)
                    store_unit(
                        net, b[s.total], b[job.own], job.r, job.axes, None, slice(n * UNIT, n * UNIT + UNIT), False
                    )
            job.copies[0].start()

        net.on(0, work)

    def global_advance(job, i):
        net.on(0, lambda: advance(b, job, i))

    def global_sum(job):
        def work():
            value = last_sum(b, job)
            b[job.swap][0] = value[1].astype(BF16)
            job.swap_copy.start()
            outs[job.weight][:, lanes(net.z0 * HALF_OF[job.weight] + job.lo, job.width)] = value[0]

        net.on(0, work)

    def global_end(job):
        def work():
            job.swap_copy.wait_recv()
            cols = lanes((1 - net.z0) * HALF_OF[job.weight] + job.lo, job.width)
            outs[job.weight][:, cols] = b[job.swap][1].astype(F32)

        net.on(0, work)

    def wp_copy(j):
        slot = j % 2
        rows = pl.ds(pl.multiple_of(j * D, D), D)
        return pltpu.make_async_copy(wp_in.at[rows, :], b[s.wp].at[slot], wp_sem.at[slot])

    def input_grads():
        own = pl.ds(pl.multiple_of(core * PATCHES, PATCHES), PATCHES)
        for copy in dh_loads:
            copy.wait()

        @pl.loop(0, PATCH)
        def _(j):
            wp_copy(j).wait()

            @pl.when(j + 1 < PATCH)
            def _():
                wp_copy(j + 1).start()

            value = mm_nt(b[s.dpp][own, :], b[s.wp][j % 2])
            for i in range(LANES):
                places = (i, pl.ds(j, PATCHES, stride=PATCH), slice(None))
                b[s.acc][places] = b[s.acc][places] + value[:, i * 128 : i * 128 + 128]

        for i in range(LANES):
            out_mine[:, i * 128 : i * 128 + 128] = b[s.acc][i].astype(BF16)
        grad_copy.start()

    def first_wait():
        for copy in global_copies:
            copy.wait()
        dyn_copy.wait_recv()

    def spread_copy(i):
        return pltpu.make_async_copy(
            b[s.spread].at[i % 2], out_rows.at[pl.ds(pl.multiple_of(i * TILE, TILE), TILE), :], row_sem.at[i % 2]
        )

    def spread_rows():
        g_load.wait()
        matrix = spread_matrix()

        @pl.loop(0, MB * TILES)
        def _(i):
            @pl.when(i >= 2)
            def _():
                spread_copy(i - 2).wait()

            rows = pl.ds(pl.multiple_of(i * (TILE // PATCH), TILE // PATCH), TILE // PATCH)
            b[s.spread][i % 2] = mm(matrix, b[s.g][rows, :]).astype(BF16)
            spread_copy(i).start()

        for i in (MB * TILES - 2, MB * TILES - 1):
            spread_copy(i).wait()

    wp_copy(0).start()
    g_down, g_up0, g_up1, g_q0, g_q1, g_out = s.glob
    patch = s.patch
    for copy in rest:
        copy.wait()
    xt, xo, total = b[s.xt], b[s.xo], b[s.total]
    local_products(net, b, [q0], False, xt, total, b[s.a], b[s.dqkv])
    local_products(net, b, [q1], False, xt, total, None, b[s.dqkv])
    local_products(net, b, [proj], False, xo, total, b[s.o], b[s.dr])
    gain_step(0)
    net.on(0, dpp_load.wait)
    net.on(1, dpp_gives[0].wait_recv)
    input_grads()
    gain_step(1)
    forward_dpp()
    local_products(net, b, [q0], True, xt, total, None, b[s.dqkv])
    local_products(net, b, [q1], True, xt, total, None, b[s.dqkv])
    local_products(net, b, [proj], True, xo, total, None, b[s.dr])
    net.on(0, first_wait)
    gain_step(2)
    global_products(g_down)
    patch_products(patch)
    global_products(g_up0)
    advance(b, proj, 0)
    global_products(g_up1)
    advance(b, q0, 0)
    global_products(g_q0)
    global_products(g_q1)
    global_products(g_out)
    net.on(0, spread_rows)
    gain_step(3)
    advance(b, q1, 0)
    global_advance(g_down, 0)
    advance(b, patch, 0)
    global_advance(g_up0, 0)
    gain_step(4)
    global_advance(g_up1, 0)
    advance(b, proj, 1)
    advance(b, proj, 2)
    advance(b, q0, 1)
    global_advance(g_down, 1)
    gain_step(5)
    out_patch[...] = last_sum(b, patch)
    out_gains[...] = b[s.gains][0]

    def copy_first():
        out_up[...] = up_in[...]
        out_down[...] = down_in[...]

    net.on(1, copy_first)
    global_advance(g_up1, 1)
    local_sum(net, b, proj)
    global_advance(g_q0, 0)
    stage_four(net, b, proj, out_out)
    advance(b, q0, 2)
    global_advance(g_q1, 0)
    global_sum(g_down)
    global_advance(g_q0, 1)
    global_advance(g_out, 0)
    global_advance(g_q1, 1)
    global_sum(g_up1)
    advance(b, q1, 1)
    global_advance(g_out, 1)
    local_sum(net, b, q0)
    global_end(g_down)
    global_advance(g_up0, 1)
    stage_four(net, b, q0, out_qkv)
    global_sum(g_q0)
    global_end(g_up1)
    global_sum(g_q1)
    advance(b, q1, 2)
    global_sum(g_out)
    global_sum(g_up0)
    global_end(g_q0)
    global_end(g_q1)
    local_sum(net, b, q1)
    global_end(g_out)
    global_end(g_up0)
    stage_four(net, b, q1, out_qkv)
    for job in s.local + [patch]:
        end_job(job)
    grad_copy.wait()

    def end_rows():
        y_own.wait()
        y_copy.wait_recv()

    net.on(1, end_rows)

    def drain():
        for copy in dpp_gives + dpp_copies + [dyn_copy, y_copy]:
            copy.wait_send()
        for job in s.glob:
            end_job(job)
            job.swap_copy.wait_send()

    net.on(0, drain)


def second_part(*operands):
    plan = second_plan()
    outs = [((ROWS_OF[w], 2 * HALF_OF[w]), F32) for w in (QKV, OUT, UP, DOWN)] + [((192, D), F32), ((8, D), F32)]
    outs += [((SEQ, D), BF16)] * 2 + [((MB * SEQ, D), BF16)]
    vmem = pl.BlockSpec(memory_space=pltpu.VMEM)
    return pl.pallas_call(
        functools.partial(second_kernel, plan=plan),
        name="second_part",
        out_shape=[sds(*o) for o in outs],
        in_specs=[ANY] * (len(operands) - 2) + [vmem] * 2,
        out_specs=[vmem] * (len(outs) - 1) + [ANY],
        scratch_shapes=plan.specs + [
            pltpu.SemaphoreType.DMA((24,)), pltpu.SemaphoreType.DMA((2,)), pltpu.SemaphoreType.DMA((2,)),
            pltpu.SemaphoreType.DMA((64,)), pltpu.SemaphoreType.DMA((64,)),
        ],
        compiler_params=pltpu.CompilerParams(vmem_limit_bytes=63 * 2**20, collective_id=2, has_side_effects=True),
        cost_estimate=cost(15e9, 60e6),
    )(*operands)


def swap_core(value):
    return lax.ppermute(value, "section", [(0, 1), (1, 0)])


def hop(value, mask, cores):
    size = lax.axis_size("dp")
    if cores == (0, 1):
        return lax.ppermute(value, "dp", [(i, i ^ mask) for i in range(size)])
    pairs = [(c * size + i, c * size + (i ^ mask)) for c in cores for i in range(size)]
    return lax.ppermute(value, ("section", "dp"), pairs)


HOPS = {"x": 1, "y": 2}


def body(states, lengths, patch_weight, w_qkv, w_out, w_up, w_down, gains, cotangent):
    size = lax.axis_size("dp")
    fast = size == 16
    core = lax.axis_index("section")
    at = lax.axis_index("dp")
    mx, my, mz = at % 2, (at // 2) % 2, (at // 4) % 4
    length = jnp.where(core == 0, lengths[0], lengths[1])
    scal = jnp.stack([core, mx, my, mz, length]).astype(jnp.int32)
    weights = (w_qkv, w_out, w_up, w_down)
    other = tuple(swap_core(w) for w in weights)
    gains_other = swap_core(gains)

    g_all, xg, start, qkv_g, p_g, mid_g, gp_g, pat = global_forward(scal, states, gains, patch_weight, weights)
    g_recv = swap_core(g_all[PATCHES:])
    g_own = jnp.where(core == 0, g_all[:PATCHES], g_recv)
    if fast:
        xg_next = hop(xg, 4, (0,))

    y, dm, a, qkv, p, o, mid, c, u, gp = local_forward(
        scal, states, cotangent, g_own, gains, weights, gains_other, other
    )
    saved = (start, mid_g, qkv_g, p_g, gp_g)
    if fast:
        up_l, down_l, dr, dqkv, dh, dpp, dy_keep, dy_send, pat_next, gain_parts = first_part(
            u, dm, c, gp, states, g_own, mid, qkv, p, gains, gains_other, weights, other, saved, pat
        )
        *grads, patch_grad, gain_sums, own_grad, peer_grad, section_rows = second_part(
            pat, pat_next, dpp, o, dr, a, dqkv, xg, xg_next, dy_keep, dy_send, dh, patch_weight, g_all, y,
            gain_parts, up_l, down_l
        )
        outs = tuple(g[None] for g in grads)
    else:
        dz = local_dz(scal, dm, gp, w_down, other[3])
        dr, dqkv, dh, dg, dgain_l = local_backward(
            scal, dz, dm, states, g_own, mid, qkv, p, gains, weights[:3], gains_other, other[:3]
        )
        dpp, dy_keep, dy_send, dgain_g = global_backward(scal, (dg, swap_core(dg)), saved, gains, weights)
        gain_parts = jnp.concatenate([dgain_g[:2], dgain_l[:2], jnp.zeros((4, D), F32)], axis=0)
        dpp = jnp.where(core == 0, dpp, swap_core(dpp))
        own_grad = input_grad_part(jnp.where(core == 0, dpp[:PATCHES], dpp[PATCHES:]), dh, patch_weight)
        peer_grad = swap_core(own_grad)
        g_rows = jnp.broadcast_to(g_all[:, None, :], (MB * PATCHES, PATCH, D)).reshape(MB * SEQ, D)
        section_rows = jnp.where(core == 0, g_rows, jnp.concatenate([swap_core(y), y], axis=0))
        gain_sums = lax.psum(gain_parts, ("section", "dp"))
        (patch_half,) = patch_weight_grad(scal, states, dpp, "xy", shards=False)
        patch_grad = lax.psum_scatter(patch_half, "dp", scatter_dimension=0, tiled=True)
        half = D // 2
        swap_halves = lambda keep, send, lo, width: jnp.where(
            mx == 0,
            jnp.concatenate([keep[:, lo : lo + width], send[:, lo : lo + width]], axis=1),
            jnp.concatenate([send[:, lo : lo + width], keep[:, lo : lo + width]], axis=1),
        )

        def whole_grad(x_lo, dy_lo, x, dy, rows, cols):
            dy_g = swap_halves(dy_keep, dy_send, dy_lo, cols // 2)
            glob = weight_grad(scal, [xg], x_lo, [dy_g], 0, rows, cols, 384, "xy", shards=False)
            loc = weight_grad(scal, [x], 0, [dy], 0, rows, cols, 384, "xy", shards=False)
            total = jnp.where(core == 0, glob, loc + swap_core(loc))
            return lax.psum_scatter(total, "dp", scatter_dimension=0, tiled=True)[None]

        outs = (
            whole_grad(0, 0, a, dqkv, D, 3 * D),
            whole_grad(D, 3 * half, o, dr, D, D),
            whole_grad(2 * D, 4 * half, c, dz, D, FF),
            whole_grad(3 * D, 8 * half, u, dm, FF, D),
        )
    input_grad = jnp.where(
        core == 0, jnp.concatenate([own_grad, peer_grad]), jnp.concatenate([peer_grad, own_grad])
    ).astype(F32)
    share = D // size
    own_gains = jnp.where(core == 0, gain_sums[0:2], gain_sums[2:4])
    gain_grad = lax.dynamic_slice(own_gains, (0, at * share), (2, share))
    return (section_rows[None], input_grad, patch_grad, *outs, gain_grad[None])


def solution(mesh):
    return jax.shard_map(
        body,
        mesh=mesh,
        in_specs=(
            P("dp", None), P("dp"), P(), P("section", None, None), P("section", None, None),
            P("section", None, None), P("section", None, None), P("section", None, None), P("dp", None),
        ),
        out_specs=(
            P("section", "dp", None), P("dp", None), P(("section", "dp"), None), P("section", "dp", None),
            P("section", "dp", None), P("section", "dp", None), P("section", "dp", None), P("section", None, "dp"),
        ),
        check_vma=False,
    )
```

```python
import functools

import jax
import jax.numpy as jnp
from jax import lax
from jax.experimental import pallas as pl
from jax.experimental.pallas import tpu as pltpu
from jax.sharding import PartitionSpec as P

D = 768
HEADS = 12
HDIM = 64
FF = 3072
PATCH = 8
SEQ = 1024
PATCHES = SEQ // PATCH
TILE = 256
SUBS = TILE // 128
PAIRS = HEADS // 2
TILES = SEQ // TILE
MB = 2
XG = 3 * D + FF
F32 = jnp.float32
BF16 = jnp.bfloat16
ANY = pl.BlockSpec(memory_space=pl.ANY)
VLIMIT = 56 * 2**20


def sds(shape, dtype):
    return jax.ShapeDtypeStruct(shape, dtype)


def mm(a, b):
    return jnp.dot(a, b, preferred_element_type=F32)


def mm_nt(a, b):
    return lax.dot_general(a, b, (((1,), (1,)), ((), ())), preferred_element_type=F32)


def mm_tn(a, b):
    return lax.dot_general(a, b, (((0,), (0,)), ((), ())), preferred_element_type=F32)


def lanes(start, size):
    return pl.ds(pl.multiple_of(start, 128), size)


def normalized(v):
    centered = v - jnp.mean(v, axis=-1, keepdims=True)
    scale = lax.rsqrt(jnp.mean(centered * centered, axis=-1, keepdims=True) + 1e-5)
    return centered * scale, scale


def norm_backward(grad, gain, hat, scale):
    scaled = grad * gain
    inner = scaled - jnp.mean(scaled, axis=-1, keepdims=True)
    inner = inner - hat * jnp.mean(scaled * hat, axis=-1, keepdims=True)
    return inner * scale, jnp.sum(grad * hat, axis=0, keepdims=True)


def gelu_pair(z):
    cdf = 0.5 + 0.5 * lax.erf(z * 0.7071067811865476)
    bell = jnp.exp2(z * z * (-0.5 * 1.4426950408889634))
    return z * cdf, cdf + z * (bell * 0.3989422804014327)


def lane_masks():
    lane = lax.broadcasted_iota(jnp.int32, (128, 128), 1)
    first = jnp.where(lane < HDIM, 1.0, 0.0)
    return first.astype(BF16), (1.0 - first).astype(BF16), lane < HDIM


def split_heads(v, first, second):
    return jnp.concatenate([v * first, v * second], axis=0)


def attention_forward(qkv_ref, o_ref, p_ref, shift):
    first, second, _ = lane_masks()
    key = lax.broadcasted_iota(jnp.int32, (128, 128), 0)
    query = lax.broadcasted_iota(jnp.int32, (128, 128), 1)
    allowed = (key <= query) & ((key >> shift) == (query >> shift))

    @pl.loop(0, SUBS)
    def _(sub):
        rows = pl.ds(pl.multiple_of(sub * 128, 128), 128)
        scores, probs = [], []
        for lo in range(0, D, 128):
            k2 = split_heads(qkv_ref[rows, D + lo : D + lo + 128], first, second)
            scores.append(mm_nt(k2, qkv_ref[rows, lo : lo + 128]) * 0.125)
        for pair in range(PAIRS):
            parts = []
            for half in range(2):
                sh = jnp.where(allowed, scores[pair][half * 128 : half * 128 + 128], -1e30)
                e = jnp.exp(sh - jnp.max(sh, axis=0, keepdims=True))
                parts.append(e * (1.0 / jnp.sum(e, axis=0, keepdims=True)))
            probs.append(jnp.concatenate(parts, axis=0).astype(BF16))
            p_ref[sub, pair] = probs[pair]
        for pair in range(PAIRS):
            lo = pair * 128
            v2 = split_heads(qkv_ref[rows, 2 * D + lo : 2 * D + lo + 128], first, second)
            o_ref[rows, lo : lo + 128] = mm_tn(probs[pair], v2).astype(BF16)


def attention_backward(qkv_ref, p_ref, do_ref, dqkv_ref):
    first, second, is_first = lane_masks()

    @pl.loop(0, SUBS)
    def _(sub):
        rows = pl.ds(pl.multiple_of(sub * 128, 128), 128)
        dps, dss = [], []
        for lo in range(0, D, 128):
            v2 = split_heads(qkv_ref[rows, 2 * D + lo : 2 * D + lo + 128], first, second)
            dps.append(mm_nt(v2, do_ref[rows, lo : lo + 128]))
        for pair in range(PAIRS):
            pf = p_ref[sub, pair].astype(F32)
            weighted = pf * dps[pair]
            parts = []
            for half in range(2):
                keys = slice(half * 128, half * 128 + 128)
                parts.append(weighted[keys] - pf[keys] * jnp.sum(weighted[keys], axis=0, keepdims=True))
            dss.append(jnp.concatenate(parts, axis=0).astype(BF16))
        for pair in range(PAIRS):
            lo = pair * 128
            k2 = split_heads(qkv_ref[rows, D + lo : D + lo + 128], first, second)
            dq = mm_tn(dss[pair], k2) * 0.125
            dk2 = mm(dss[pair], qkv_ref[rows, lo : lo + 128]) * 0.125
            dv2 = mm(p_ref[sub, pair], do_ref[rows, lo : lo + 128])
            dqkv_ref[rows, lo : lo + 128] = dq.astype(BF16)
            dqkv_ref[rows, D + lo : D + lo + 128] = jnp.where(is_first, dk2[:128], dk2[128:]).astype(BF16)
            dqkv_ref[rows, 2 * D + lo : 2 * D + lo + 128] = jnp.where(is_first, dv2[:128], dv2[128:]).astype(BF16)


def block_forward(
    h, gains, w, wait, shift, a_ref, qkv_ref, p_ref, o_ref, mid_ref, c_ref, u_ref, gp_ref, done=lambda i: None
):
    wq, wo, wu, wd = w
    a_ref[...] = (normalized(h)[0] * gains[0:1, :]).astype(BF16)
    wait(0)

    @pl.loop(0, 3)
    def _(part):
        cols = lanes(part * D, D)
        qkv_ref[:, cols] = mm(a_ref[...], wq[:, cols]).astype(BF16)

    attention_forward(qkv_ref, o_ref, p_ref, shift)
    done(0)
    wait(1)
    mid = h + mm(o_ref[...], wo[...])
    mid_ref[...] = mid
    c_ref[...] = (normalized(mid)[0] * gains[1:2, :]).astype(BF16)
    done(1)
    wait(2)

    @pl.loop(0, FF // D)
    def _(part):
        cols = lanes(part * D, D)
        u, gp = gelu_pair(mm(c_ref[...], wu[:, cols]))
        u_ref[:, cols] = u.astype(BF16)
        gp_ref[:, cols] = gp.astype(BF16)

    done(2)
    wait(3)
    return mid_ref[...] + mm(u_ref[...], wd[...])


def dz_product(dm, wd, gp_ref, dz_ref):
    @pl.loop(0, FF // D)
    def _(part):
        cols = lanes(part * D, D)
        du = mm_nt(dm, wd[pl.ds(pl.multiple_of(part * D, D), D), :])
        dz_ref[:, cols] = (du * gp_ref[:, cols].astype(F32)).astype(BF16)


def backward_upper(dout, gains, wo, wu, dz_ref, mid_ref, dr_ref, do_ref, dmid_ref):
    hat, scale = normalized(mid_ref[...])
    dc = mm_nt(dz_ref[...], wu[...])
    back, dgain = norm_backward(dc, gains[1:2, :], hat, scale)
    dmid_ref[...] = dout + back
    dr_ref[...] = dmid_ref[...].astype(BF16)
    do_ref[...] = mm_nt(dr_ref[...], wo[...]).astype(BF16)
    return dgain


def backward_lower(h, gains, wq, qkv_ref, p_ref, do_ref, dqkv_ref, dmid_ref):
    attention_backward(qkv_ref, p_ref, do_ref, dqkv_ref)
    da = mm_nt(dqkv_ref[...], wq[...])
    hat, scale = normalized(h)
    back, dgain = norm_backward(da, gains[0:1, :], hat, scale)
    return dmid_ref[...] + back, dgain


def block_backward(dout, h, gains, w, wait, dz_ref, mid_ref, qkv_ref, p_ref, do_ref, dr_ref, dqkv_ref, dmid_ref):
    wq, wo, wu = w
    for i in (2, 1, 0):
        wait(i)
    dgain_two = backward_upper(dout, gains, wo, wu, dz_ref, mid_ref, dr_ref, do_ref, dmid_ref)
    dh, dgain_one = backward_lower(h, gains, wq, qkv_ref, p_ref, do_ref, dqkv_ref, dmid_ref)
    return dh, jnp.concatenate([dgain_one, dgain_two], axis=0)


LANES = D // 128


def fill_lanes(dst, src):
    for b in range(LANES):
        dst[b] = src[:, b * 128 : b * 128 + 128].astype(F32)


def strided_rows(ref, start, rows):
    picked = [ref[b, pl.ds(start, rows, stride=PATCH), :] for b in range(LANES)]
    return jnp.concatenate(picked, axis=1)


def spread_matrix():
    row = lax.broadcasted_iota(jnp.int32, (TILE, TILE // PATCH), 0) // PATCH
    col = lax.broadcasted_iota(jnp.int32, (TILE, TILE // PATCH), 1)
    return jnp.where(row == col, 1.0, 0.0).astype(BF16)


def add_low(a, b):
    return (a.astype(F32) + b.astype(F32)).astype(BF16)


def cost(flops, nbytes):
    return pl.CostEstimate(flops=int(flops), bytes_accessed=int(nbytes), transcendentals=0)


WSCRATCH = {
    "q": pltpu.VMEM((D, 3 * D), BF16),
    "o": pltpu.VMEM((D, D), BF16),
    "u": pltpu.VMEM((D, FF), BF16),
    "d": pltpu.VMEM((FF, D), BF16),
}


CORE, X, Y, ZN, ZF, XY = range(6)
QKV, OUT, UP, DOWN = range(4)
ROWS_OF = (D // 16, D // 16, D // 16, FF // 16)
HALF_OF = (3 * D // 2, D // 2, FF // 2, D // 2)
X_LO = (0, D, 2 * D, 3 * D)
DY_LO = (0, 3 * D // 2, 2 * D, 2 * D + FF // 2)
WIDTH_G = (3 * D + D + FF + D) // 2
ROWS_G = MB * PATCHES
UNIT = 384
MESH_ID = pl.DeviceIdType.MESH


class Net:
    def __init__(self, send, recv, local):
        self.send, self.recv, self.local, self.count, self.local_count = send, recv, local, 0, 0
        self.core = lax.axis_index("section")
        at = lax.axis_index("dp")
        self.x, self.y, self.z = at % 2, (at // 2) % 2, at // 4
        self.z0, self.z1 = self.z % 2, self.z // 2
        z0, z1 = self.z0, self.z1
        spot = lambda x, y, z: {"dp": z * 4 + y * 2 + x}
        self.partner = (
            {"section": 1 - self.core}, spot(1 - self.x, self.y, self.z), spot(self.x, 1 - self.y, self.z),
            spot(self.x, self.y, 1 - z0 + 2 * z1), spot(self.x, self.y, z0 + 2 - 2 * z1),
            spot(1 - self.x, 1 - self.y, self.z),
        )

    def meet(self):
        barrier = pltpu.get_barrier_semaphore()
        for device in self.partner:
            pl.semaphore_signal(barrier, inc=1, device_id=device, device_id_type=MESH_ID)
        pl.semaphore_wait(barrier, len(self.partner))

    def remote(self, src, dst, to):
        n = self.count
        self.count += 1
        return pltpu.make_async_remote_copy(
            src_ref=src, dst_ref=dst, send_sem=self.send.at[n], recv_sem=self.recv.at[n],
            device_id=self.partner[to], device_id_type=MESH_ID,
        )

    def load(self, src, dst):
        n = self.local_count
        self.local_count += 1
        return pltpu.make_async_copy(src, dst, self.local.at[n])

    def on(self, which, fn):
        pl.when(self.core == which)(fn)

    def z_of(self, k):
        return (self.z0 + k % 2) % 2 + 2 * ((self.z1 + k // 2) % 2)


def global_forward_kernel(
    bytes_ref, gains_ref, wp_hbm, wq_hbm, wo_hbm, wu_hbm, wd_hbm,
    own_out, g_out, x_out, start_out, qkv_out, p_out, mid_out, gp_out, pat_out,
    bytes_f32, wp, wq, wo, wu, wd, x_s, start_s, qkv_s, p_s, mid_s, gp_s, pat_s, g_s, psem, wsem, osem, send, recv,
):
    net = Net(send, recv, osem)
    core = net.core
    barrier = pltpu.get_barrier_semaphore()
    pl.semaphore_signal(barrier, inc=1, device_id=net.partner[CORE], device_id_type=MESH_ID)

    def wp_copy(j):
        rows = pl.ds(pl.multiple_of(j * D, D), D)
        return pltpu.make_async_copy(wp_hbm.at[rows, :], wp.at[rows, :], psem.at[j])

    wcopies = [
        pltpu.make_async_copy(src.at[0], dst, wsem.at[i])
        for i, (src, dst) in enumerate(((wq_hbm, wq), (wo_hbm, wo), (wu_hbm, wu), (wd_hbm, wd)))
    ]

    def start_weights():
        for j in range(PATCH):
            wp_copy(j).start()
        for copy in wcopies:
            copy.start()

    net.on(0, start_weights)
    fill_lanes(bytes_f32, bytes_ref)
    start_s[...] = jnp.zeros_like(start_s)

    @pl.loop(0, PATCH)
    def _(j):
        mine = j // (PATCH // 2) == core

        @pl.when((core == 0) | mine)
        def _():
            xj = strided_rows(bytes_f32, j, ROWS_G).astype(BF16)

            @pl.when(core == 0)
            def _():
                wp_copy(j).wait()
                start_s[...] = start_s[...] + mm(xj, wp[pl.ds(pl.multiple_of(j * D, D), D), :])

            @pl.when(mine)
            def _():
                for piece in range(4):
                    xr = 1 - net.x if piece % 2 else net.x
                    yr = 1 - net.y if piece // 2 else net.y
                    pat_s[yr * 2 + xr, j % (PATCH // 2)] = xj[:, piece * 192 : piece * 192 + 192]

    pat_copy = net.load(pat_s, pat_out)
    pat_copy.start()
    pl.semaphore_wait(barrier, 1)
    outs = [
        net.load(*pair) for pair in (
            (start_s, start_out), (qkv_s, qkv_out), (p_s, p_out), (mid_s, mid_out), (gp_s, gp_out), (x_s, x_out),
            (g_s, g_out), (g_s.at[0:PATCHES, :], own_out),
        )
    ]
    give = net.remote(g_s.at[PATCHES:ROWS_G, :], own_out, CORE)

    def work():
        moved = pltpu.roll(start_s[...], 1, 0)
        row = lax.broadcasted_iota(jnp.int32, (ROWS_G, D), 0)
        start_s[...] = jnp.where((row & (PATCHES - 1)) == 0, 0.0, moved)
        outs[0].start()

        def done(i):
            for copy in ((outs[1], outs[2]), (outs[3],), (outs[4], outs[5]))[i]:
                copy.start()

        out = block_forward(
            start_s[...], gains_ref[0], (wq, wo, wu, wd), lambda i: wcopies[i].wait(), 7,
            x_s.at[:, 0:D], qkv_s, p_s, x_s.at[:, D : 2 * D], mid_s,
            x_s.at[:, 2 * D : 3 * D], x_s.at[:, 3 * D : 3 * D + FF], gp_s, done,
        )
        g_s[...] = out.astype(BF16)
        give.start()
        outs[6].start()
        outs[7].start()
        for copy in outs:
            copy.wait()
        give.wait_send()

    net.on(0, work)
    net.on(1, give.wait_recv)
    pat_copy.wait()


def global_forward(states, gains, patch_weight, weights):
    outs = (
        ((PATCHES, D), BF16), ((ROWS_G, D), BF16), ((ROWS_G, XG), BF16), ((ROWS_G, D), F32), ((ROWS_G, 3 * D), BF16),
        ((SUBS, PAIRS, 256, 128), BF16), ((ROWS_G, D), F32), ((ROWS_G, FF), BF16), ((4, PATCH // 2, ROWS_G, 192), BF16),
    )
    vmem = pl.BlockSpec(memory_space=pltpu.VMEM)
    held = [pltpu.VMEM(*o) for o in outs[2:]] + [pltpu.VMEM((ROWS_G, D), BF16)]
    return pl.pallas_call(
        global_forward_kernel,
        name="global_forward",
        out_shape=[sds(*o) for o in outs],
        in_specs=[vmem] * 2 + [ANY] * 5,
        out_specs=[ANY] * len(outs),
        scratch_shapes=[
            pltpu.VMEM((LANES, MB * SEQ, 128), F32), pltpu.VMEM((PATCH * D, D), BF16),
            WSCRATCH["q"], WSCRATCH["o"], WSCRATCH["u"], WSCRATCH["d"], *held,
            pltpu.SemaphoreType.DMA((PATCH,)), pltpu.SemaphoreType.DMA((4,)), pltpu.SemaphoreType.DMA((9,)),
            pltpu.SemaphoreType.DMA((1,)), pltpu.SemaphoreType.DMA((1,)),
        ],
        compiler_params=pltpu.CompilerParams(vmem_limit_bytes=VLIMIT, collective_id=3, has_side_effects=True),
        cost_estimate=cost(6e9, 32e6),
    )(states, gains, patch_weight, *weights)


def global_backward_kernel(
    scal, dg0_ref, dg1_ref, start_ref, mid_ref, qkv_ref, p_ref, gp_ref, gains_ref, wq_hbm, wo_hbm, wu_hbm, wd_hbm,
    dpp_ref, keep_ref, send_ref, dgain_ref,
    dm_s, dz_s, do_s, dr_s, dqkv_s, dmid_s, wq, wo, wu, wd, wsem,
):
    @pl.when(scal[0] == 0)
    def _():
        rows = MB * PATCHES
        wcopies = [
            pltpu.make_async_copy(src.at[0], dst, wsem.at[i])
            for i, (src, dst) in enumerate(((wq_hbm, wq), (wo_hbm, wo), (wu_hbm, wu), (wd_hbm, wd)))
        ]
        for i in (3, 2, 1, 0):
            wcopies[i].start()
        dm_s[0:PATCHES, :] = dg0_ref[...]
        dm_s[PATCHES:, :] = dg1_ref[...]
        wcopies[3].wait()
        dz_product(dm_s[...], wd, gp_ref, dz_s)
        dh, dgain = block_backward(
            dm_s[...].astype(F32), start_ref[...], gains_ref[0], (wq, wo, wu), lambda i: wcopies[i].wait(),
            dz_s, mid_ref, qkv_ref, p_ref, do_s, dr_s, dqkv_s, dmid_s,
        )
        dgain_ref[...] = jnp.zeros_like(dgain_ref)
        dgain_ref[0:2, :] = dgain
        moved = pltpu.roll(dh, rows - 1, 0)
        row = lax.broadcasted_iota(jnp.int32, (rows, D), 0)
        dpp_ref[...] = jnp.where((row & (PATCHES - 1)) == PATCHES - 1, 0.0, moved).astype(BF16)
        for half in range(2):
            def fill(ref):
                lo = 0
                for src, width in ((dqkv_s, 3 * D // 2), (dr_s, D // 2), (dz_s, FF // 2), (dm_s, D // 2)):
                    ref[:, lo : lo + width] = src[:, half * width : half * width + width]
                    lo += width
            pl.when(scal[1] == half)(functools.partial(fill, keep_ref))
            pl.when(scal[1] != half)(functools.partial(fill, send_ref))

    @pl.when(scal[0] != 0)
    def _():
        dgain_ref[...] = jnp.zeros_like(dgain_ref)


def global_backward(scal, dgs, saved, gains, weights):
    rows = MB * PATCHES
    full = lambda *shape: pl.BlockSpec(shape, lambda i, s: (0,) * len(shape), pipeline_mode=pl.Buffered(1))
    width = (3 * D + D + FF + D) // 2
    outs = (((rows, D), BF16), ((rows, width), BF16), ((rows, width), BF16), ((8, D), F32))
    return pl.pallas_call(
        global_backward_kernel,
        name="global_backward",
        out_shape=[sds(*o) for o in outs],
        grid_spec=pltpu.PrefetchScalarGridSpec(
            num_scalar_prefetch=1,
            grid=(1,),
            in_specs=[full(PATCHES, D)] * 2 + [full(*v.shape) for v in saved] + [full(1, 2, D)] + [ANY] * 4,
            out_specs=[full(*o[0]) for o in outs],
            scratch_shapes=[
                pltpu.VMEM((rows, D), BF16), pltpu.VMEM((rows, FF), BF16), pltpu.VMEM((rows, D), BF16),
                pltpu.VMEM((rows, D), BF16), pltpu.VMEM((rows, 3 * D), BF16), pltpu.VMEM((rows, D), F32),
                WSCRATCH["q"], WSCRATCH["o"], WSCRATCH["u"], WSCRATCH["d"],
                pltpu.SemaphoreType.DMA((4,)),
            ],
        ),
        compiler_params=pltpu.CompilerParams(vmem_limit_bytes=VLIMIT),
        cost_estimate=cost(6e9, 24e6),
    )(scal, *dgs, *saved, gains, *weights)


def start_weights(scal, pairs, sems, order):
    step = pl.program_id(0)
    for i in order:
        own, recv, dst = pairs[i]

        @pl.when((step == 0) & (scal[0] == 1))
        def _(own=own, dst=dst, i=i):
            pltpu.make_async_copy(own.at[0], dst, sems.at[i]).start()

        @pl.when((step == 0) & (scal[0] == 0))
        def _(recv=recv, dst=dst, i=i):
            pltpu.make_async_copy(recv.at[0], dst, sems.at[i]).start()

    def wait(i):
        @pl.when(step == 0)
        def _():
            pltpu.make_async_copy(pairs[i][1].at[0], pairs[i][2], sems.at[i]).wait()

    return wait


def live_rows(scal):
    step = pl.program_id(0)
    row = lax.broadcasted_iota(jnp.int32, (TILE, D), 0) + step * TILE
    return row < scal[4]


def local_forward_kernel(
    scal, bytes_ref, cot_ref, g_ref, gains_ref, wq_a, wo_a, wu_a, wd_a, wq_b, wo_b, wu_b, wd_b, gains_b,
    y_ref, dm_ref, a_ref, qkv_ref, p_ref, o_ref, mid_ref, c_ref, u_ref, gp_ref,
    wq, wo, wu, wd, wsem,
):
    pairs = ((wq_a, wq_b, wq), (wo_a, wo_b, wo), (wu_a, wu_b, wu), (wd_a, wd_b, wd))
    wait = start_weights(scal, pairs, wsem, (0, 1, 2, 3))
    gains = jnp.where(scal[0] == 1, gains_ref[0], gains_b[0])
    h = bytes_ref[...].astype(F32) + mm(spread_matrix(), g_ref[...])
    out = block_forward(h, gains, (wq, wo, wu, wd), wait, 3, a_ref, qkv_ref, p_ref, o_ref, mid_ref, c_ref, u_ref, gp_ref)
    live = live_rows(scal)
    y_ref[...] = jnp.where(live, out, 0.0).astype(BF16)
    dm_ref[...] = jnp.where(live, cot_ref[...].astype(F32), 0.0).astype(BF16)


def row_block(*shape):
    return pl.BlockSpec(shape, lambda i, s: (i,) + (0,) * (len(shape) - 1))


def const_block(*shape):
    return pl.BlockSpec(shape, lambda i, s: (0,) * len(shape), pipeline_mode=pl.Buffered(1))


def seq_block():
    return pl.BlockSpec((TILE, D), lambda i, s: (s[0] * TILES + i, 0))


def local_forward(scal, states, cotangent, g_own, gains, weights, gains_b, weights_b):
    outs = (
        ((SEQ, D), BF16), ((SEQ, D), BF16), ((SEQ, D), BF16), ((SEQ, 3 * D), BF16),
        ((SEQ // 128, PAIRS, 256, 128), BF16), ((SEQ, D), BF16), ((SEQ, D), F32), ((SEQ, D), BF16),
        ((SEQ, FF), BF16), ((SEQ, FF), BF16),
    )
    return pl.pallas_call(
        local_forward_kernel,
        name="local_forward",
        out_shape=[sds(*o) for o in outs],
        grid_spec=pltpu.PrefetchScalarGridSpec(
            num_scalar_prefetch=1,
            grid=(TILES,),
            in_specs=[seq_block(), seq_block(), row_block(TILE // PATCH, D), const_block(1, 2, D)]
            + [ANY] * 8 + [const_block(1, 2, D)],
            out_specs=[row_block(o[0][0] // TILES, *o[0][1:]) for o in outs],
            scratch_shapes=[
                WSCRATCH["q"], WSCRATCH["o"], WSCRATCH["u"], WSCRATCH["d"], pltpu.SemaphoreType.DMA((4,)),
            ],
        ),
        compiler_params=pltpu.CompilerParams(vmem_limit_bytes=VLIMIT),
        cost_estimate=cost(14.5e9, 60e6),
    )(scal, states, cotangent, g_own, gains, *weights, *weights_b, gains_b)


def local_dz_kernel(scal, dm_ref, gp_ref, wd_a, wd_b, dz_ref, wd, wsem):
    wait = start_weights(scal, ((wd_a, wd_b, wd),), wsem, (0,))
    wait(0)
    dz_product(dm_ref[...], wd, gp_ref, dz_ref)


def local_dz(scal, dm, gp, wd_a, wd_b):
    return pl.pallas_call(
        local_dz_kernel,
        name="local_dz",
        out_shape=sds((SEQ, FF), BF16),
        grid_spec=pltpu.PrefetchScalarGridSpec(
            num_scalar_prefetch=1,
            grid=(TILES,),
            in_specs=[row_block(TILE, D), row_block(TILE, FF), ANY, ANY],
            out_specs=row_block(TILE, FF),
            scratch_shapes=[WSCRATCH["d"], pltpu.SemaphoreType.DMA((1,))],
        ),
        compiler_params=pltpu.CompilerParams(vmem_limit_bytes=VLIMIT),
        cost_estimate=cost(4.8e9, 18e6),
    )(scal, dm, gp, wd_a, wd_b)


def local_backward_kernel(
    scal, dz_ref, dm_ref, bytes_ref, g_ref, mid_ref, qkv_ref, p_ref, gains_ref,
    wq_a, wo_a, wu_a, wq_b, wo_b, wu_b, gains_b,
    dr_ref, dqkv_ref, dh_ref, dg_ref, dgain_ref,
    do_s, wq, wo, wu, wsem,
):
    pairs = ((wq_a, wq_b, wq), (wo_a, wo_b, wo), (wu_a, wu_b, wu))
    wait = start_weights(scal, pairs, wsem, (2, 1, 0))
    gains = jnp.where(scal[0] == 1, gains_ref[0], gains_b[0])
    h = bytes_ref[...].astype(F32) + mm(spread_matrix(), g_ref[...])
    dh, dgain = block_backward(
        dm_ref[...].astype(F32), h, gains, (wq, wo, wu), wait, dz_ref, mid_ref, qkv_ref, p_ref, do_s, dr_ref, dqkv_ref,
        dh_ref,
    )
    dh_ref[...] = dh
    dg_ref[...] = jnp.sum(dh.reshape(TILE // PATCH, PATCH, D), axis=1).astype(BF16)

    @pl.when(pl.program_id(0) == 0)
    def _():
        dgain_ref[...] = jnp.zeros_like(dgain_ref)

    dgain_ref[0:2, :] += dgain


def local_backward(scal, dz, dm, states, g_own, mid, qkv, p, gains, weights, gains_b, weights_b):
    outs = (
        ((SEQ, D), BF16), ((SEQ, 3 * D), BF16), ((SEQ, D), F32), ((PATCHES, D), BF16), ((8, D), F32),
    )
    return pl.pallas_call(
        local_backward_kernel,
        name="local_backward",
        out_shape=[sds(*o) for o in outs],
        grid_spec=pltpu.PrefetchScalarGridSpec(
            num_scalar_prefetch=1,
            grid=(TILES,),
            in_specs=[
                row_block(TILE, FF), row_block(TILE, D), seq_block(), row_block(TILE // PATCH, D), row_block(TILE, D),
                row_block(TILE, 3 * D), row_block(SUBS, PAIRS, 256, 128), const_block(1, 2, D),
            ] + [ANY] * 6 + [const_block(1, 2, D)],
            out_specs=[row_block(o[0][0] // TILES, *o[0][1:]) for o in outs[:4]] + [const_block(8, D)],
            scratch_shapes=[
                pltpu.VMEM((TILE, D), BF16), WSCRATCH["q"], WSCRATCH["o"], WSCRATCH["u"], pltpu.SemaphoreType.DMA((3,)),
            ],
        ),
        compiler_params=pltpu.CompilerParams(vmem_limit_bytes=VLIMIT),
        cost_estimate=cost(10e9, 50e6),
    )(scal, dz, dm, states, g_own, mid, qkv, p, gains, *weights, *weights_b, gains_b)


def store_shards(scal, total, keep_ref, send_ref, add_refs, order, r, count, z):
    first, second = order
    position = {"x": scal[1], "y": scal[2]}
    for one in range(2):
        for two in range(2):
            at = {first: one ^ position[first], second: two ^ position[second]}
            for k in range(count // 4):
                level = (k ^ scal[3]) * 4 if count == 16 else 0
                shard = level + at["y"] * 2 + at["x"]
                value = total[pl.ds(pl.multiple_of(shard * r, 16), r), :]
                if add_refs is not None:
                    value = value + add_refs[one][two, k].astype(F32)
                (send_ref if one else keep_ref)[two, k] = value.astype(BF16)


def weight_grad_kernel(scal, *refs, parts, order, r, count, has_add, core_zero, shards):
    xs, dys, refs = refs[:parts], refs[parts : 2 * parts], refs[2 * parts :]
    adds = None
    if has_add:
        adds, refs = refs[:2], refs[2:]

    def work():
        value = mm_tn(xs[0][...], dys[0][...])
        for x, dy in zip(xs[1:], dys[1:]):
            value = value + mm_tn(x[...], dy[...])
        if not shards:
            refs[0][...] = value
            return
        keep_ref, send_ref, total = refs
        total[...] = value
        store_shards(scal, total, keep_ref, send_ref, adds, order, r, count, pl.program_id(0))

    if core_zero:
        pl.when(scal[0] == 0)(work)
    else:
        work()


def weight_grad(scal, xs, x_lo, dys, dy_lo, rows, cols, tn, order, add=None, half=None, core_zero=False, shards=True):
    mt, nt = rows // D, cols // tn
    r = rows // 16
    count = 16 if mt == 1 else 4
    depth = xs[0].shape[0]
    kz = 4 if mt == 1 else 1

    def dy_map(m, n, s):
        offset = 0 if half is None else (s[0] if half == "own" else 1 - s[0]) * nt
        return (0, dy_lo // tn + offset + n)

    shard_spec = pl.BlockSpec((2, kz, r, tn), lambda m, n, s: (0, 0 if mt == 1 else m ^ s[3], 0, n))
    if shards:
        out_shape = [sds((2, 4, r, cols), BF16)] * 2
        out_specs = [shard_spec] * 2
        scratch = [pltpu.VMEM((D, tn), F32)]
    else:
        out_shape = sds((rows, cols), F32)
        out_specs = pl.BlockSpec((D, tn), lambda m, n, s: (m, n))
        scratch = []
    return pl.pallas_call(
        functools.partial(
            weight_grad_kernel, parts=len(xs), order=order, r=r, count=count, has_add=add is not None,
            core_zero=core_zero, shards=shards,
        ),
        name="weight_grad",
        out_shape=out_shape,
        grid_spec=pltpu.PrefetchScalarGridSpec(
            num_scalar_prefetch=1,
            grid=(mt, nt),
            in_specs=[pl.BlockSpec((depth, D), lambda m, n, s: (0, x_lo // D + m))] * len(xs)
            + [pl.BlockSpec((depth, tn), dy_map)] * len(xs) + [shard_spec] * (0 if add is None else 2),
            out_specs=out_specs,
            scratch_shapes=scratch,
        ),
        compiler_params=pltpu.CompilerParams(vmem_limit_bytes=VLIMIT),
        cost_estimate=cost(2 * depth * len(xs) * rows * cols, 2 * (depth * (rows + cols) + rows * cols)),
    )(scal, *xs, *dys, *(add or ()))


def patch_grad_kernel(scal, bytes_ref, dpp_ref, *refs, order, shards):
    bytes_f32, total = refs[-2:]

    @pl.when(pl.program_id(0) == 0)
    def _():
        fill_lanes(bytes_f32, bytes_ref)

    byte = scal[0] * (PATCH // 2) + pl.program_id(0)
    x = strided_rows(bytes_f32, byte, MB * PATCHES).astype(BF16)
    value = mm_tn(x, dpp_ref[...])
    if not shards:
        refs[0][...] = value
        return
    total[...] = value
    store_shards(scal, total, refs[0], refs[1], None, order, 192, 4, pl.program_id(0))


def patch_weight_grad(scal, states, dpp, order, shards=True):
    if shards:
        out_shape = [sds((2, 4, 192, D), BF16)] * 2
        out_specs = [pl.BlockSpec((2, 1, 192, D), lambda i, s: (0, i ^ s[3], 0, 0))] * 2
    else:
        out_shape = [sds((PATCH // 2 * D, D), F32)]
        out_specs = [pl.BlockSpec((D, D), lambda i, s: (i, 0))]
    return pl.pallas_call(
        functools.partial(patch_grad_kernel, order=order, shards=shards),
        name="patch_weight_grad",
        out_shape=out_shape,
        grid_spec=pltpu.PrefetchScalarGridSpec(
            num_scalar_prefetch=1,
            grid=(PATCH // 2,),
            in_specs=[const_block(MB * SEQ, D), const_block(MB * PATCHES, D)],
            out_specs=out_specs,
            scratch_shapes=[pltpu.VMEM((LANES, MB * SEQ, 128), F32), pltpu.VMEM((D, D), F32)],
        ),
        compiler_params=pltpu.CompilerParams(vmem_limit_bytes=VLIMIT),
        cost_estimate=cost(1.2e9, 10e6),
    )(scal, states, dpp)


def input_grad_kernel(dpp_ref, dh_ref, wp_hbm, out_ref, acc, wp, psem):
    copies = [
        pltpu.make_async_copy(wp_hbm.at[pl.ds(j * D, D)], wp.at[pl.ds(j * D, D)], psem.at[j]) for j in range(PATCH)
    ]
    for copy in copies:
        copy.start()
    for j in range(PATCH):
        copies[j].wait()
        value = mm_nt(dpp_ref[...], wp[j * D : j * D + D, :])
        for b in range(LANES):
            acc[b, pl.ds(j, PATCHES, stride=PATCH), :] = value[:, b * 128 : b * 128 + 128]
    for b in range(LANES):
        cols = slice(b * 128, b * 128 + 128)
        out_ref[:, cols] = (dh_ref[:, cols] + acc[b]).astype(BF16)


def input_grad_part(dpp_own, dh, patch_weight):
    return pl.pallas_call(
        input_grad_kernel,
        name="input_grad",
        out_shape=sds((SEQ, D), BF16),
        in_specs=[pl.BlockSpec(memory_space=pltpu.VMEM)] * 2 + [ANY],
        out_specs=pl.BlockSpec(memory_space=pltpu.VMEM),
        scratch_shapes=[
            pltpu.VMEM((LANES, SEQ, 128), F32), pltpu.VMEM((PATCH * D, D), BF16), pltpu.SemaphoreType.DMA((PATCH,)),
        ],
        compiler_params=pltpu.CompilerParams(vmem_limit_bytes=VLIMIT),
        cost_estimate=cost(1.2e9, 15e6),
    )(dpp_own, dh, patch_weight)


class Job:
    def __init__(self, weight, lo, width, axes):
        self.weight, self.lo, self.width, self.axes = weight, lo, width, axes
        self.r = 192 if weight is None else ROWS_OF[weight]


class Alloc:
    def __init__(self):
        self.specs = []

    def __call__(self, shape, dtype):
        self.specs.append(pltpu.VMEM(shape, dtype))
        return len(self.specs) - 1


def store_unit(net, total, dst, r, axes, k_tile, cols, add):
    flip = lambda here, other: 1 - here if other else here
    for place in range(4 if k_tile is not None else 16):
        xr, yr = place % 2, place // 2 % 2
        k = place // 4 if k_tile is None else k_tile
        relative = {X: xr, Y: yr, ZN: k % 2, ZF: k // 2}
        shard = flip(net.y, yr) * 2 + flip(net.x, xr)
        if k_tile is None:
            shard = shard + 4 * (flip(net.z0, k % 2) + 2 * flip(net.z1, k // 2))
        index = 0
        for axis in axes:
            index = index * 2 + relative[axis]
        at_dst = (index,) if ZN in axes else (index, relative[ZN])
        at_dst += (slice(None), cols)
        value = total[pl.ds(pl.multiple_of(shard * r, 16), r), :]
        if add:
            value = value + dst[at_dst].astype(F32)
        dst[at_dst] = value.astype(BF16)


def job_buffers(alloc, job, local):
    block = (job.r, job.width) if ZN in job.axes else (2, job.r, job.width)
    count = 2 ** len(job.axes)
    job.own = alloc((count, *block), BF16)
    job.recv = []
    while count > 1:
        count //= 2
        job.recv.append(alloc((count, *block), BF16))
    if local:
        job.peer = alloc((16, *block), BF16)
        job.lf = alloc(block, F32)
        job.lr = alloc(block, F32)


def job_copies(net, b, job, local):
    job.copies = []
    count = 2 ** len(job.axes)
    for axis, recv in zip(job.axes, job.recv):
        job.copies.append(net.remote(b[job.own].at[count // 2 : count], b[recv], axis))
        count //= 2
    if local:
        job.cd = net.remote(b[job.peer], b[job.own], CORE)
        job.c4 = net.remote(b[job.lf], b[job.lr], CORE)


def advance(b, job, i):
    job.copies[i].wait_recv()
    own, recv = b[job.own], b[job.recv[i]]

    @pl.loop(0, 2 ** (len(job.axes) - 1 - i))
    def _(k):
        own[k] = add_low(own[k], recv[k])

    job.copies[i + 1].start()


def last_sum(b, job):
    job.copies[-1].wait_recv()
    return b[job.own][0].astype(F32) + b[job.recv[-1]][0].astype(F32)


def local_sum(net, b, job):
    b[job.lf][...] = last_sum(b, job)
    net.on(0, job.c4.start)


def stage_four(net, b, job, out):
    half = HALF_OF[job.weight]

    def finish():
        job.c4.wait_recv()
        out[:, job.lo : job.lo + job.width] = b[job.lr][...]
        out[:, half + job.lo : half + job.lo + job.width] = b[job.lf][...]

    net.on(1, finish)
    net.on(0, job.c4.wait_send)


def end_job(job):
    for copy in job.copies:
        copy.wait_send()


def local_products(net, b, jobs, mine, xt, total, x_ref, dy_ref):
    buffer = lambda job: b[job.own if mine else job.peer]
    job = jobs[0]
    base = (net.core if mine else 1 - net.core) * HALF_OF[job.weight] + job.lo
    if mine:
        for job in jobs:
            job.cd.wait_recv()
    if job.weight == DOWN:

        @pl.loop(0, 4)
        def _(k):
            xt[...] = x_ref[:, lanes(net.z_of(k) * D, D)].T
            total[...] = mm(xt[...], dy_ref[:, lanes(base, UNIT)])
            for job in jobs:
                part = total.at[:, job.lo : job.lo + job.width]
                store_unit(net, part, buffer(job), job.r, job.axes, k, slice(0, job.width), mine)
    else:
        if x_ref is not None:
            xt[...] = x_ref[...].T

        @pl.loop(0, job.width // UNIT)
        def _(n):
            total[...] = mm(xt[...], dy_ref[:, lanes(base + n * UNIT, UNIT)])
            store_unit(net, total, buffer(job), job.r, job.axes, None, lanes(n * UNIT, UNIT), mine)

    for job in jobs:
        if mine:
            job.copies[0].start()
            job.cd.wait_send()
        else:
            job.cd.start()


def first_plan():
    alloc = Alloc()
    jobs = [
        Job(DOWN, 0, 256, (X, Y, ZN, ZF)), Job(DOWN, 256, 128, (Y, X, ZN, ZF)),
        Job(UP, 0, 768, (X, Y, ZN, ZF)), Job(UP, 768, 768, (X, Y, ZN, ZF)),
    ]
    for job in jobs:
        job_buffers(alloc, job, True)
    s = lambda: None
    s.jobs = jobs
    s.ubuf, s.dz = alloc((SEQ, FF), BF16), alloc((SEQ, FF), BF16)
    s.dm = alloc((SEQ, D), BF16)
    s.xt, s.total = alloc((D, SEQ), BF16), alloc((D, UNIT), F32)
    s.wq, s.wo, s.wu, s.wd = (alloc(w, BF16) for w in ((D, 3 * D), (D, D), (D, FF), (FF, D)))
    s.gp = alloc((2, TILE, FF), BF16)
    s.bytes, s.mid = alloc((2, TILE, D), BF16), alloc((2, TILE, D), F32)
    s.qkv, s.p = alloc((2, TILE, 3 * D), BF16), alloc((2, SUBS, PAIRS, 256, 128), BF16)
    s.dr, s.dqkv, s.dh, s.do = alloc((TILE, D), BF16), alloc((TILE, 3 * D), BF16), alloc((TILE, D), F32), alloc((TILE, D), BF16)
    s.g, s.dg, s.dmg, s.dpp = (alloc((n, D), BF16) for n in (PATCHES, PATCHES, ROWS_G, ROWS_G))
    s.gains = alloc((2, 2, D), F32)
    s.specs = alloc.specs
    return s


def first_kernel(
    u_in, dm_in, c_in, gp_in, states, g_in, mid_in, qkv_in, p_in, gains_own, gains_other,
    wq_own, wo_own, wu_own, wd_own, wq_other, wo_other, wu_other, wd_other,
    start_g, mid_g, qkv_g, p_g, gp_g, pat_in, xg_in,
    out_up, out_down, dr_out, dqkv_out, dh_out, dpp_out, keep_out, send_out, pat_out, xn_out, gain_out,
    *refs, plan,
):
    b, (load_sem, tile_sem, send_sem, recv_sem) = refs[:-4], refs[-4:]
    net = Net(send_sem, recv_sem, load_sem)
    s = plan
    core = net.core
    down0, down1, up0, up1 = s.jobs
    net.meet()
    for job in s.jobs:
        job_copies(net, b, job, True)
    dg_copy = net.remote(b[s.dg], b[s.dmg].at[PATCHES:ROWS_G, :], CORE)
    pat_copies = [net.remote(pat_in.at[i], pat_out.at[i - 1], to) for i, to in ((1, X), (2, Y), (3, XY))]
    xg_copy = net.remote(xg_in, xn_out, ZN)
    net.on(0, xg_copy.start)

    def load(src, dst):
        copy = net.load(src, dst)
        copy.start()
        return copy

    def load_weight(own, other, dst, swap):
        copy = net.load(own.at[0], dst)
        net.on(0 if swap else 1, copy.start)
        if not swap:
            second = net.load(other.at[0], dst)
            net.on(0, second.start)

        def wait():
            if swap:
                net.on(0, copy.wait)
            else:
                net.on(1, copy.wait)
                net.on(0, second.wait)

        return wait

    u_load, dm_load = load(u_in, b[s.ubuf]), load(dm_in, b[s.dm])
    wd_wait = load_weight(wd_own, wd_other, b[s.wd], False)
    small = [load(g_in, b[s.g]), load(gains_own.at[0], b[s.gains].at[0]), load(gains_other.at[0], b[s.gains].at[1])]
    wu_wait = load_weight(wu_own, wu_other, b[s.wu], False)
    wo_wait = load_weight(wo_own, wo_other, b[s.wo], False)
    wq_wait = load_weight(wq_own, wq_other, b[s.wq], False)

    def tile_copies(t, slot, kinds):
        rows = pl.ds(pl.multiple_of(t * TILE, TILE), TILE)
        seq_rows = pl.ds(pl.multiple_of(core * SEQ + t * TILE, TILE), TILE)
        subs = pl.ds(t * SUBS, SUBS)
        table = (
            (gp_in.at[rows, :], b[s.gp].at[slot]), (states.at[seq_rows, :], b[s.bytes].at[slot]),
            (mid_in.at[rows, :], b[s.mid].at[slot]), (qkv_in.at[rows, :], b[s.qkv].at[slot]),
            (p_in.at[subs], b[s.p].at[slot]),
        )
        return [pltpu.make_async_copy(*table[i], tile_sem.at[slot, i]) for i in kinds]

    def store_copies(t):
        rows = pl.ds(pl.multiple_of(t * TILE, TILE), TILE)
        table = ((b[s.dr], dr_out), (b[s.dqkv], dqkv_out), (b[s.dh], dh_out))
        return [pltpu.make_async_copy(src, dst.at[rows, :], tile_sem.at[2, i]) for i, (src, dst) in enumerate(table)]

    for copy in tile_copies(0, 0, (0, 1, 2, 3, 4)):
        copy.start()
    u_load.wait()
    dm_load.wait()
    xt, total = b[s.xt], b[s.total]

    def dz_tiles(first, last):
        @pl.loop(first, last)
        def _(t):
            slot = t % 2
            tile_copies(t, slot, (0,))[0].wait()

            @pl.when(t + 1 < TILES)
            def _():
                tile_copies(t + 1, 1 - slot, (0,))[0].start()

            rows = pl.ds(pl.multiple_of(t * TILE, TILE), TILE)
            dz_product(b[s.dm][rows, :], b[s.wd], b[s.gp].at[slot], b[s.dz].at[rows, :])

    local_products(net, b, [down0, down1], False, xt, total, b[s.ubuf], b[s.dm])
    wd_wait()
    dz_tiles(0, 2)
    local_products(net, b, [down0, down1], True, xt, total, b[s.ubuf], b[s.dm])
    c_part = b[s.ubuf].at[:, 0:D]
    c_load = load(c_in, c_part)
    dz_tiles(2, TILES)
    wd_wait_g = load_weight(wd_own, wd_other, b[s.wd], True)
    c_load.wait()
    local_products(net, b, [up0], False, xt, total, c_part, b[s.dz])
    local_products(net, b, [up1], False, xt, total, None, b[s.dz])
    advance(b, down1, 0)
    local_products(net, b, [up0], True, xt, total, None, b[s.dz])
    local_products(net, b, [up1], True, xt, total, None, b[s.dz])
    for copy in small:
        copy.wait()
    wu_wait()
    wo_wait()
    wq_wait()
    gains = jnp.where(core == 1, b[s.gains][0], b[s.gains][1])
    gain_out[...] = jnp.zeros_like(gain_out)

    def global_loads():
        pairs = (
            (gp_g, b[s.gp].at[0]), (mid_g, b[s.mid].at[0]), (qkv_g, b[s.qkv].at[0]), (p_g, b[s.p].at[0]),
        )
        return [pltpu.make_async_copy(*pair, tile_sem.at[3, i]) for i, pair in enumerate(pairs)]

    @pl.loop(0, TILES)
    def _(t):
        slot = t % 2
        for copy in tile_copies(t, slot, (1, 2, 3, 4)):
            copy.wait()

        @pl.when(t + 1 < TILES)
        def _():
            for copy in tile_copies(t + 1, 1 - slot, (1, 2, 3, 4)):
                copy.start()

        @pl.when((t + 1 == TILES) & (core == 0))
        def _():
            for copy in global_loads():
                copy.start()

        @pl.when(t > 0)
        def _():
            for copy in store_copies(t - 1):
                copy.wait()

        rows = pl.ds(pl.multiple_of(t * TILE, TILE), TILE)
        patch_rows = pl.ds(pl.multiple_of(t * (TILE // PATCH), TILE // PATCH), TILE // PATCH)
        h = b[s.bytes][slot].astype(F32) + mm(spread_matrix(), b[s.g][patch_rows, :])
        dh, dgain = block_backward(
            b[s.dm][rows, :].astype(F32), h, gains, (b[s.wq], b[s.wo], b[s.wu]), lambda i: None,
            b[s.dz].at[rows, :], b[s.mid].at[slot], b[s.qkv].at[slot], b[s.p].at[slot], b[s.do], b[s.dr], b[s.dqkv],
            b[s.dh],
        )
        b[s.dh][...] = dh
        b[s.dg][patch_rows, :] = jnp.sum(dh.reshape(TILE // PATCH, PATCH, D), axis=1).astype(BF16)
        gain_out[2:4, :] += dgain
        for copy in store_copies(t):
            copy.start()

        @pl.when(t == 0)
        def _():
            advance(b, down1, 1)
            advance(b, down0, 0)

        @pl.when(t == 1)
        def _():
            for copy in pat_copies:
                copy.start()
            advance(b, down1, 2)

        @pl.when(t == 2)
        def _():
            local_sum(net, b, down1)
            advance(b, down0, 1)
            advance(b, up0, 0)

        @pl.when(t == 3)
        def _():
            advance(b, down0, 2)
            advance(b, up0, 1)
            advance(b, up1, 0)

    wu_wait_g = load_weight(wu_own, wu_other, b[s.wu], True)
    wo_wait_g = load_weight(wo_own, wo_other, b[s.wo], True)
    wq_wait_g = load_weight(wq_own, wq_other, b[s.wq], True)
    net.on(1, dg_copy.start)
    for copy in store_copies(TILES - 1):
        copy.wait()
    dz_g = b[s.ubuf].at[0:ROWS_G, :]
    wd_wait_g()
    wu_wait_g()
    wo_wait_g()
    wq_wait_g()

    start_load = pltpu.make_async_copy(start_g, b[s.mid].at[1], tile_sem.at[3, 4])

    def global_upper():
        start_load.start()
        for copy in global_loads():
            copy.wait()
        b[s.dmg][0:PATCHES, :] = b[s.dg][...]
        dg_copy.wait_recv()
        dz_product(b[s.dmg][...], b[s.wd], b[s.gp].at[0], dz_g)
        gain_out[1:2, :] = backward_upper(
            b[s.dmg][...].astype(F32), b[s.gains][0], b[s.wo], b[s.wu], dz_g, b[s.mid].at[0], b[s.dr], b[s.do], b[s.dh]
        )

    def global_lower():
        start_load.wait()
        dh, dgain = backward_lower(
            b[s.mid][1], b[s.gains][0], b[s.wq], b[s.qkv].at[0], b[s.p].at[0], b[s.do], b[s.dqkv], b[s.dh]
        )
        gain_out[0:1, :] = dgain
        moved = pltpu.roll(dh, ROWS_G - 1, 0)
        row = lax.broadcasted_iota(jnp.int32, (ROWS_G, D), 0)
        b[s.dpp][...] = jnp.where((row & (PATCHES - 1)) == PATCHES - 1, 0.0, moved).astype(BF16)
        for copy in global_stores():
            copy.start()

    def global_stores():
        copies = [pltpu.make_async_copy(b[s.dpp], dpp_out, tile_sem.at[4, 0])]
        lo, n = 0, 1
        for src, width in ((b[s.dqkv], 3 * D // 2), (b[s.dr], D // 2), (dz_g, FF // 2), (b[s.dmg], D // 2)):
            for out, half in ((keep_out, net.z0), (send_out, 1 - net.z0)):
                copies.append(
                    pltpu.make_async_copy(src.at[:, lanes(half * width, width)], out.at[:, lo : lo + width], tile_sem.at[4, n])
                )
                n += 1
            lo += width
        return copies

    net.on(0, global_upper)
    local_sum(net, b, down0)
    advance(b, up0, 2)
    advance(b, up1, 1)
    net.on(0, global_lower)
    stage_four(net, b, down1, out_down)
    stage_four(net, b, down0, out_down)
    local_sum(net, b, up0)
    advance(b, up1, 2)
    stage_four(net, b, up0, out_up)
    local_sum(net, b, up1)
    net.on(1, dg_copy.wait_send)
    stage_four(net, b, up1, out_up)
    for job in s.jobs:
        end_job(job)
    for copy in pat_copies:
        copy.wait()
    net.on(0, xg_copy.wait)

    def finish():
        for copy in global_stores():
            copy.wait()

    net.on(0, finish)


def first_part(u, dm, c, gp, states, g, mid, qkv, p, gains, gains_other, weights, other, saved, pat, xg):
    plan = first_plan()
    outs = [
        ((D // 16, FF), F32), ((FF // 16, D), F32), ((SEQ, D), BF16), ((SEQ, 3 * D), BF16), ((SEQ, D), F32),
        ((ROWS_G, D), BF16), ((ROWS_G, WIDTH_G), BF16), ((ROWS_G, WIDTH_G), BF16), ((3, PATCH // 2, ROWS_G, 192), BF16), ((ROWS_G, XG), BF16),
        ((8, D), F32),
    ]
    vmem = pl.BlockSpec(memory_space=pltpu.VMEM)
    operands = (u, dm, c, gp, states, g, mid, qkv, p, gains, gains_other, *weights, *other, *saved, pat, xg)
    return pl.pallas_call(
        functools.partial(first_kernel, plan=plan),
        name="first_part",
        out_shape=[sds(*o) for o in outs],
        in_specs=[ANY] * len(operands),
        out_specs=[vmem] * 2 + [ANY] * 8 + [vmem],
        scratch_shapes=plan.specs + [
            pltpu.SemaphoreType.DMA((32,)), pltpu.SemaphoreType.DMA((5, 9)), pltpu.SemaphoreType.DMA((40,)),
            pltpu.SemaphoreType.DMA((40,)),
        ],
        compiler_params=pltpu.CompilerParams(vmem_limit_bytes=63 * 2**20, collective_id=1, has_side_effects=True),
        cost_estimate=cost(35e9, 80e6),
    )(*operands)


def second_plan():
    alloc = Alloc()
    s = lambda: None
    s.local = [Job(QKV, 0, 768, (X, Y, ZN, ZF)), Job(QKV, 768, 384, (X, Y, ZN, ZF)), Job(OUT, 0, 384, (Y, X, ZN, ZF))]
    s.patch = Job(None, 0, D, (ZN, ZF))
    s.glob = [
        Job(DOWN, 0, 384, (Y, X, ZF)), Job(UP, 0, 768, (X, Y, ZF)), Job(UP, 768, 768, (Y, X, ZF)),
        Job(QKV, 0, 768, (Y, X, ZF)), Job(QKV, 768, 384, (Y, X, ZF)), Job(OUT, 0, 384, (Y, X, ZF)),
    ]
    for job in s.local:
        job_buffers(alloc, job, True)
    job_buffers(alloc, s.patch, False)
    for job in s.glob:
        job_buffers(alloc, job, False)
        job.swap = alloc((2, job.r, job.width), BF16)
    s.dqkv = alloc((SEQ, 3 * D), BF16)
    s.a, s.o, s.dr = (alloc((SEQ, D), BF16) for _ in range(3))
    s.xt, s.xo, s.total = alloc((D, SEQ), BF16), alloc((D, SEQ), BF16), alloc((D, UNIT), F32)
    s.pat, s.dpp = alloc((PATCH // 2, 4 * ROWS_G, 192), BF16), alloc((4 * ROWS_G, D), BF16)
    s.xg, s.dy = alloc((2 * ROWS_G, XG), BF16), alloc((2 * ROWS_G, WIDTH_G), BF16)
    s.gains = alloc((6, 8, D), F32)
    s.g, s.spread = alloc((ROWS_G, D), BF16), alloc((2, TILE, D), BF16)
    s.wp, s.acc = alloc((2, D, D), BF16), alloc((LANES, SEQ, 128), F32)
    s.specs = alloc.specs
    return s


def second_kernel(
    pat_own, pat_in, dpp_in, o_in, dr_in, a_in, dqkv_in, xg_in, xn_in, keep_in, send_in, dh_in, wp_in, g_in, y_in,
    gains_in, up_in, down_in,
    out_qkv, out_out, out_up, out_down, out_patch, out_gains, out_mine, out_peer, out_rows, *refs, plan,
):
    b, (load_sem, wp_sem, row_sem, send_sem, recv_sem) = refs[:-5], refs[-5:]
    net = Net(send_sem, recv_sem, load_sem)
    s = plan
    core = net.core
    q0, q1, proj = s.local
    outs = (out_qkv, out_out, out_up, out_down)
    net.meet()
    for job in s.local:
        job_copies(net, b, job, True)
    job_copies(net, b, s.patch, False)
    for job in s.glob:
        job_copies(net, b, job, False)
        job.swap_copy = net.remote(b[job.swap].at[0], b[job.swap].at[1], ZN)
    gain_copies = [
        net.remote(b[s.gains].at[0], b[s.gains].at[i + 1], to) for i, to in enumerate((CORE, X, Y, ZN, ZF))
    ]
    dpp_slots = [b[s.dpp].at[i * ROWS_G : i * ROWS_G + ROWS_G, :] for i in range(4)]
    dpp_gives = [net.remote(dpp_in, dpp_slots[0], CORE)] + [net.remote(slot, slot, CORE) for slot in dpp_slots[1:]]
    dpp_copies = [net.remote(dpp_in, dpp_slots[i], to) for i, to in ((1, X), (2, Y), (3, XY))]
    own_part, next_part = slice(0, ROWS_G), slice(ROWS_G, 2 * ROWS_G)
    dyn_copy = net.remote(send_in, b[s.dy].at[next_part, :], ZN)
    grad_copy = net.remote(out_mine, out_peer, CORE)
    y_copy = net.remote(y_in, out_rows.at[0:SEQ, :], CORE)
    y_own = net.load(y_in, out_rows.at[SEQ : MB * SEQ, :])
    g_load = net.load(g_in, b[s.g])
    dpp_load = net.load(dpp_in, dpp_slots[0])
    global_copies = [net.load(*pair) for pair in (
        (xg_in, b[s.xg].at[own_part, :]), (xn_in, b[s.xg].at[next_part, :]), (keep_in, b[s.dy].at[own_part, :]),
    )]

    def give():
        dpp_gives[0].start()
        for copy in dpp_copies:
            copy.start()
        dyn_copy.start()
        dpp_load.start()
        g_load.start()
        y_copy.start()

    net.on(0, give)
    net.on(1, y_own.start)
    rest = [net.load(*pair) for pair in ((dqkv_in, b[s.dqkv]), (a_in, b[s.a]), (o_in, b[s.o]), (dr_in, b[s.dr]))]
    pat_parts = [pat_own.at[0]] + [pat_in.at[i] for i in range(3)]
    pat_loads = [
        net.load(part, b[s.pat].at[:, i * ROWS_G : i * ROWS_G + ROWS_G, :]) for i, part in enumerate(pat_parts)
    ]
    gain_load = net.load(gains_in, b[s.gains].at[0])
    dh_loads = [net.load(dh_in.at[:, i * 128 : i * 128 + 128], b[s.acc].at[i]) for i in range(LANES)]
    for copy in rest + [gain_load] + pat_loads + dh_loads:
        copy.start()
    net.on(0, lambda: [copy.start() for copy in global_copies] and None)

    def gain_step(i):
        if i == 0:
            gain_load.wait()
        else:
            gain_copies[i - 1].wait_recv()
            b[s.gains][0] = b[s.gains][0] + b[s.gains][i]
        if i < 5:
            gain_copies[i].start()
            gain_copies[i].wait_send()

    def forward_dpp():
        def work():
            for copy, give_copy in zip(dpp_copies, dpp_gives[1:]):
                copy.wait_recv()
                give_copy.start()

        net.on(0, work)

    def patch_products(job):
        for copy in pat_loads:
            copy.wait()
        for i in range(PATCH // 2):
            b[s.xt][i * 192 : i * 192 + 192, :] = b[s.pat][i].T
        net.on(1, lambda: [copy.wait_recv() for copy in dpp_gives[1:]] and None)

        @pl.loop(0, D // UNIT)
        def _(n):
            cols = lanes(n * UNIT, UNIT)
            b[s.total][...] = mm(b[s.xt][...], b[s.dpp][:, cols])
            for k in range(4):
                z = (1 - net.z0 if k // 2 else net.z0) + 2 * (1 - net.z1 if k % 2 else net.z1)
                b[job.own][k, :, cols] = b[s.total][pl.ds(pl.multiple_of(z * 192, 16), 192), :].astype(BF16)
        job.copies[0].start()

    def global_products(job):
        base = DY_LO[job.weight] + job.lo

        def product(cols, n):
            return mm_tn(b[s.xg][:, cols], b[s.dy][:, lanes(base + n * UNIT, UNIT)])

        def work():
            if job.weight == DOWN:

                @pl.loop(0, 4)
                def _(k):
                    b[s.total][...] = product(lanes(X_LO[DOWN] + net.z_of(k) * D, D), 0)
                    store_unit(net, b[s.total], b[job.own], job.r, job.axes, k, slice(0, UNIT), False)
            else:

                @pl.loop(0, job.width // UNIT)
                def _(n):
                    b[s.total][...] = product(slice(X_LO[job.weight], X_LO[job.weight] + D), n)
                    store_unit(net, b[s.total], b[job.own], job.r, job.axes, None, lanes(n * UNIT, UNIT), False)

            job.copies[0].start()

        net.on(0, work)

    def global_advance(job, i):
        net.on(0, lambda: advance(b, job, i))

    def global_sum(job):
        def work():
            value = last_sum(b, job)
            b[job.swap][0] = value[1].astype(BF16)
            job.swap_copy.start()
            outs[job.weight][:, lanes(net.z0 * HALF_OF[job.weight] + job.lo, job.width)] = value[0]

        net.on(0, work)

    def global_end(job):
        def work():
            job.swap_copy.wait_recv()
            cols = lanes((1 - net.z0) * HALF_OF[job.weight] + job.lo, job.width)
            outs[job.weight][:, cols] = b[job.swap][1].astype(F32)

        net.on(0, work)

    def wp_copy(j):
        slot = j % 2
        rows = pl.ds(pl.multiple_of(j * D, D), D)
        return pltpu.make_async_copy(wp_in.at[rows, :], b[s.wp].at[slot], wp_sem.at[slot])

    def input_grads():
        own = pl.ds(pl.multiple_of(core * PATCHES, PATCHES), PATCHES)
        for copy in dh_loads:
            copy.wait()

        @pl.loop(0, PATCH)
        def _(j):
            wp_copy(j).wait()

            @pl.when(j + 1 < PATCH)
            def _():
                wp_copy(j + 1).start()

            value = mm_nt(b[s.dpp][own, :], b[s.wp][j % 2])
            for i in range(LANES):
                places = (i, pl.ds(j, PATCHES, stride=PATCH), slice(None))
                b[s.acc][places] = b[s.acc][places] + value[:, i * 128 : i * 128 + 128]

        for i in range(LANES):
            out_mine[:, i * 128 : i * 128 + 128] = b[s.acc][i].astype(BF16)
        grad_copy.start()

    def first_wait():
        for copy in global_copies:
            copy.wait()
        dyn_copy.wait_recv()

    def spread_copy(i):
        return pltpu.make_async_copy(
            b[s.spread].at[i % 2], out_rows.at[pl.ds(pl.multiple_of(i * TILE, TILE), TILE), :], row_sem.at[i % 2]
        )

    def spread_rows():
        g_load.wait()
        matrix = spread_matrix()

        @pl.loop(0, MB * TILES)
        def _(i):
            @pl.when(i >= 2)
            def _():
                spread_copy(i - 2).wait()

            rows = pl.ds(pl.multiple_of(i * (TILE // PATCH), TILE // PATCH), TILE // PATCH)
            b[s.spread][i % 2] = mm(matrix, b[s.g][rows, :]).astype(BF16)
            spread_copy(i).start()

        for i in (MB * TILES - 2, MB * TILES - 1):
            spread_copy(i).wait()

    wp_copy(0).start()
    g_down, g_up0, g_up1, g_q0, g_q1, g_out = s.glob
    patch = s.patch
    for copy in rest:
        copy.wait()
    xt, xo, total = b[s.xt], b[s.xo], b[s.total]
    local_products(net, b, [q0], False, xt, total, b[s.a], b[s.dqkv])
    local_products(net, b, [q1], False, xt, total, None, b[s.dqkv])
    local_products(net, b, [proj], False, xo, total, b[s.o], b[s.dr])
    gain_step(0)
    net.on(0, dpp_load.wait)
    net.on(1, dpp_gives[0].wait_recv)
    input_grads()
    gain_step(1)
    forward_dpp()
    local_products(net, b, [q0], True, xt, total, None, b[s.dqkv])
    local_products(net, b, [q1], True, xt, total, None, b[s.dqkv])
    local_products(net, b, [proj], True, xo, total, None, b[s.dr])
    net.on(0, first_wait)
    gain_step(2)
    global_products(g_down)
    patch_products(patch)
    global_products(g_up0)
    advance(b, proj, 0)
    global_products(g_up1)
    advance(b, q0, 0)
    global_products(g_q0)
    global_products(g_q1)
    global_products(g_out)
    net.on(0, spread_rows)
    gain_step(3)
    advance(b, q1, 0)
    global_advance(g_down, 0)
    advance(b, patch, 0)
    global_advance(g_up0, 0)
    gain_step(4)
    global_advance(g_up1, 0)
    advance(b, proj, 1)
    advance(b, proj, 2)
    advance(b, q0, 1)
    global_advance(g_down, 1)
    gain_step(5)
    out_patch[...] = last_sum(b, patch)
    out_gains[...] = b[s.gains][0]

    def copy_first():
        out_up[...] = up_in[...]
        out_down[...] = down_in[...]

    net.on(1, copy_first)
    global_advance(g_up1, 1)
    local_sum(net, b, proj)
    global_advance(g_q0, 0)
    stage_four(net, b, proj, out_out)
    advance(b, q0, 2)
    global_advance(g_q1, 0)
    global_sum(g_down)
    global_advance(g_q0, 1)
    global_advance(g_out, 0)
    global_advance(g_q1, 1)
    global_sum(g_up1)
    advance(b, q1, 1)
    global_advance(g_out, 1)
    local_sum(net, b, q0)
    global_end(g_down)
    global_advance(g_up0, 1)
    stage_four(net, b, q0, out_qkv)
    global_sum(g_q0)
    global_end(g_up1)
    global_sum(g_q1)
    advance(b, q1, 2)
    global_sum(g_out)
    global_sum(g_up0)
    global_end(g_q0)
    global_end(g_q1)
    local_sum(net, b, q1)
    global_end(g_out)
    global_end(g_up0)
    stage_four(net, b, q1, out_qkv)
    for job in s.local + [patch]:
        end_job(job)
    grad_copy.wait()

    def end_rows():
        y_own.wait()
        y_copy.wait_recv()

    net.on(1, end_rows)

    def drain():
        for copy in dpp_gives + dpp_copies + [dyn_copy, y_copy]:
            copy.wait_send()
        for job in s.glob:
            end_job(job)
            job.swap_copy.wait_send()

    net.on(0, drain)


def second_part(*operands):
    plan = second_plan()
    outs = [((ROWS_OF[w], 2 * HALF_OF[w]), F32) for w in (QKV, OUT, UP, DOWN)] + [((192, D), F32), ((8, D), F32)]
    outs += [((SEQ, D), BF16)] * 2 + [((MB * SEQ, D), BF16)]
    vmem = pl.BlockSpec(memory_space=pltpu.VMEM)
    return pl.pallas_call(
        functools.partial(second_kernel, plan=plan),
        name="second_part",
        out_shape=[sds(*o) for o in outs],
        in_specs=[ANY] * (len(operands) - 2) + [vmem] * 2,
        out_specs=[vmem] * (len(outs) - 1) + [ANY],
        scratch_shapes=plan.specs + [
            pltpu.SemaphoreType.DMA((24,)), pltpu.SemaphoreType.DMA((2,)), pltpu.SemaphoreType.DMA((2,)),
            pltpu.SemaphoreType.DMA((64,)), pltpu.SemaphoreType.DMA((64,)),
        ],
        compiler_params=pltpu.CompilerParams(vmem_limit_bytes=63 * 2**20, collective_id=2, has_side_effects=True),
        cost_estimate=cost(15e9, 60e6),
    )(*operands)


def finish_kernel(*refs):
    own, peer = refs[:2]
    sources, grad_out = refs[2:8], refs[8]
    targets, refs = refs[9:15], refs[15:]
    held, wide, staged = refs[0], refs[1], refs[2:8]
    copy_sem, in_sem, out_sem = refs[8:]
    core = lax.axis_index("section")
    loads = [pltpu.make_async_copy(src, held.at[i], in_sem.at[i]) for i, src in enumerate((own, peer))]
    copies_in = [pltpu.make_async_copy(src, mid, copy_sem.at[0, i]) for i, (src, mid) in enumerate(zip(sources, staged))]
    copies_out = [pltpu.make_async_copy(mid, dst, copy_sem.at[1, i]) for i, (mid, dst) in enumerate(zip(staged, targets))]
    for copy in loads + copies_in:
        copy.start()

    def store(i, t):
        place = core if i == 0 else 1 - core
        rows = pl.ds(pl.multiple_of(place * SEQ + t * TILE, TILE), TILE)
        return pltpu.make_async_copy(wide.at[i * TILES + t], grad_out.at[rows, :], out_sem.at[i * TILES + t])

    for i in range(2):
        loads[i].wait()

        @pl.loop(0, TILES)
        def _(t, i=i):
            wide[i * TILES + t] = held[i, pl.ds(pl.multiple_of(t * TILE, TILE), TILE), :].astype(F32)
            store(i, t).start()

    for first, second in zip(copies_in, copies_out):
        first.wait()
        second.start()
    for i in range(2):
        @pl.loop(0, TILES)
        def _(t, i=i):
            store(i, t).wait()

    for copy in copies_out:
        copy.wait()


def finish(own_grad, peer_grad, others):
    outs = [((MB * SEQ, D), F32)] + [(v.shape, v.dtype) for v in others]
    return pl.pallas_call(
        finish_kernel,
        name="finish",
        out_shape=[sds(*o) for o in outs],
        in_specs=[ANY] * (2 + len(others)),
        out_specs=[ANY] * len(outs),
        scratch_shapes=[
            pltpu.VMEM((2, SEQ, D), BF16), pltpu.VMEM((2 * TILES, TILE, D), F32),
            *[pltpu.VMEM(v.shape, v.dtype) for v in others], pltpu.SemaphoreType.DMA((2, len(others))),
            pltpu.SemaphoreType.DMA((2,)), pltpu.SemaphoreType.DMA((2 * TILES,)),
        ],
        compiler_params=pltpu.CompilerParams(vmem_limit_bytes=VLIMIT),
        cost_estimate=cost(1e6, 20e6),
    )(own_grad, peer_grad, *others)


def swap_core(value):
    return lax.ppermute(value, "section", [(0, 1), (1, 0)])


def hop(value, mask, cores):
    size = lax.axis_size("dp")
    if cores == (0, 1):
        return lax.ppermute(value, "dp", [(i, i ^ mask) for i in range(size)])
    pairs = [(c * size + i, c * size + (i ^ mask)) for c in cores for i in range(size)]
    return lax.ppermute(value, ("section", "dp"), pairs)


HOPS = {"x": 1, "y": 2}


def body(states, lengths, patch_weight, w_qkv, w_out, w_up, w_down, gains, cotangent):
    size = lax.axis_size("dp")
    fast = size == 16
    core = lax.axis_index("section")
    at = lax.axis_index("dp")
    mx, my, mz = at % 2, (at // 2) % 2, (at // 4) % 4
    length = jnp.where(core == 0, lengths[0], lengths[1])
    scal = jnp.stack([core, mx, my, mz, length]).astype(jnp.int32)
    weights = (w_qkv, w_out, w_up, w_down)
    other = tuple(swap_core(w) for w in weights)
    gains_other = swap_core(gains)

    g_own, g_all, xg, start, qkv_g, p_g, mid_g, gp_g, pat = global_forward(states, gains, patch_weight, weights)
    y, dm, a, qkv, p, o, mid, c, u, gp = local_forward(
        scal, states, cotangent, g_own, gains, weights, gains_other, other
    )
    saved = (start, mid_g, qkv_g, p_g, gp_g)
    if fast:
        up_l, down_l, dr, dqkv, dh, dpp, dy_keep, dy_send, pat_next, xg_next, gain_parts = first_part(
            u, dm, c, gp, states, g_own, mid, qkv, p, gains, gains_other, weights, other, saved, pat, xg
        )
        *grads, patch_grad, gain_sums, own_grad, peer_grad, section_rows = second_part(
            pat, pat_next, dpp, o, dr, a, dqkv, xg, xg_next, dy_keep, dy_send, dh, patch_weight, g_all, y,
            gain_parts, up_l, down_l
        )
        input_grad, section_rows, patch_grad, *grads = finish(own_grad, peer_grad, (section_rows, patch_grad, *grads))
        outs = tuple(g[None] for g in grads)
    else:
        dz = local_dz(scal, dm, gp, w_down, other[3])
        dr, dqkv, dh, dg, dgain_l = local_backward(
            scal, dz, dm, states, g_own, mid, qkv, p, gains, weights[:3], gains_other, other[:3]
        )
        dpp, dy_keep, dy_send, dgain_g = global_backward(scal, (dg, swap_core(dg)), saved, gains, weights)
        gain_parts = jnp.concatenate([dgain_g[:2], dgain_l[:2], jnp.zeros((4, D), F32)], axis=0)
        dpp = jnp.where(core == 0, dpp, swap_core(dpp))
        own_grad = input_grad_part(jnp.where(core == 0, dpp[:PATCHES], dpp[PATCHES:]), dh, patch_weight)
        peer_grad = swap_core(own_grad)
        input_grad = jnp.where(
            core == 0, jnp.concatenate([own_grad, peer_grad]), jnp.concatenate([peer_grad, own_grad])
        ).astype(F32)
        g_rows = jnp.broadcast_to(g_all[:, None, :], (MB * PATCHES, PATCH, D)).reshape(MB * SEQ, D)
        section_rows = jnp.where(core == 0, g_rows, jnp.concatenate([swap_core(y), y], axis=0))
        gain_sums = lax.psum(gain_parts, ("section", "dp"))
        (patch_half,) = patch_weight_grad(scal, states, dpp, "xy", shards=False)
        patch_grad = lax.psum_scatter(patch_half, "dp", scatter_dimension=0, tiled=True)
        half = D // 2
        swap_halves = lambda keep, send, lo, width: jnp.where(
            mx == 0,
            jnp.concatenate([keep[:, lo : lo + width], send[:, lo : lo + width]], axis=1),
            jnp.concatenate([send[:, lo : lo + width], keep[:, lo : lo + width]], axis=1),
        )

        def whole_grad(x_lo, dy_lo, x, dy, rows, cols):
            dy_g = swap_halves(dy_keep, dy_send, dy_lo, cols // 2)
            glob = weight_grad(scal, [xg], x_lo, [dy_g], 0, rows, cols, 384, "xy", shards=False)
            loc = weight_grad(scal, [x], 0, [dy], 0, rows, cols, 384, "xy", shards=False)
            total = jnp.where(core == 0, glob, loc + swap_core(loc))
            return lax.psum_scatter(total, "dp", scatter_dimension=0, tiled=True)[None]

        outs = (
            whole_grad(0, 0, a, dqkv, D, 3 * D),
            whole_grad(D, 3 * half, o, dr, D, D),
            whole_grad(2 * D, 4 * half, c, dz, D, FF),
            whole_grad(3 * D, 8 * half, u, dm, FF, D),
        )
    share = D // size
    own_gains = jnp.where(core == 0, gain_sums[0:2], gain_sums[2:4])
    gain_grad = lax.dynamic_slice(own_gains, (0, at * share), (2, share))
    return (section_rows[None], input_grad, patch_grad, *outs, gain_grad[None])


def solution(mesh):
    return jax.shard_map(
        body,
        mesh=mesh,
        in_specs=(
            P("dp", None), P("dp"), P(), P("section", None, None), P("section", None, None),
            P("section", None, None), P("section", None, None), P("section", None, None), P("dp", None),
        ),
        out_specs=(
            P("section", "dp", None), P("dp", None), P(("section", "dp"), None), P("section", "dp", None),
            P("section", "dp", None), P("section", "dp", None), P("section", "dp", None), P("section", None, "dp"),
        ),
        check_vma=False,
    )
```

```python
import functools

import jax
import jax.numpy as jnp
from jax import lax
from jax.experimental import pallas as pl
from jax.experimental.pallas import tpu as pltpu
from jax.sharding import PartitionSpec as P

D = 768
HEADS = 12
HDIM = 64
FF = 3072
PATCH = 8
SEQ = 1024
PATCHES = SEQ // PATCH
TILE = 256
SUBS = TILE // 128
PAIRS = HEADS // 2
TILES = SEQ // TILE
MB = 2
XG = 3 * D + FF
F32 = jnp.float32
BF16 = jnp.bfloat16
ANY = pl.BlockSpec(memory_space=pl.ANY)
VLIMIT = 56 * 2**20


def sds(shape, dtype):
    return jax.ShapeDtypeStruct(shape, dtype)


def mm(a, b):
    return jnp.dot(a, b, preferred_element_type=F32)


def mm_nt(a, b):
    return lax.dot_general(a, b, (((1,), (1,)), ((), ())), preferred_element_type=F32)


def mm_tn(a, b):
    return lax.dot_general(a, b, (((0,), (0,)), ((), ())), preferred_element_type=F32)


def lanes(start, size):
    return pl.ds(pl.multiple_of(start, 128), size)


def normalized(v):
    centered = v - jnp.mean(v, axis=-1, keepdims=True)
    scale = lax.rsqrt(jnp.mean(centered * centered, axis=-1, keepdims=True) + 1e-5)
    return centered * scale, scale


def norm_backward(grad, gain, hat, scale):
    scaled = grad * gain
    inner = scaled - jnp.mean(scaled, axis=-1, keepdims=True)
    inner = inner - hat * jnp.mean(scaled * hat, axis=-1, keepdims=True)
    return inner * scale, jnp.sum(grad * hat, axis=0, keepdims=True)


def gelu_pair(z):
    cdf = 0.5 + 0.5 * lax.erf(z * 0.7071067811865476)
    bell = jnp.exp2(z * z * (-0.5 * 1.4426950408889634))
    return z * cdf, cdf + z * (bell * 0.3989422804014327)


def lane_masks():
    lane = lax.broadcasted_iota(jnp.int32, (128, 128), 1)
    first = jnp.where(lane < HDIM, 1.0, 0.0)
    return first.astype(BF16), (1.0 - first).astype(BF16), lane < HDIM


def split_heads(v, first, second):
    return jnp.concatenate([v * first, v * second], axis=0)


def attention_forward(qkv_ref, o_ref, p_ref, shift):
    first, second, _ = lane_masks()
    key = lax.broadcasted_iota(jnp.int32, (128, 128), 0)
    query = lax.broadcasted_iota(jnp.int32, (128, 128), 1)
    allowed = (key <= query) & ((key >> shift) == (query >> shift))

    @pl.loop(0, SUBS)
    def _(sub):
        rows = pl.ds(pl.multiple_of(sub * 128, 128), 128)
        scores, probs = [], []
        for lo in range(0, D, 128):
            k2 = split_heads(qkv_ref[rows, D + lo : D + lo + 128], first, second)
            scores.append(mm_nt(k2, qkv_ref[rows, lo : lo + 128]) * 0.125)
        for pair in range(PAIRS):
            parts = []
            for half in range(2):
                sh = jnp.where(allowed, scores[pair][half * 128 : half * 128 + 128], -1e30)
                e = jnp.exp(sh - jnp.max(sh, axis=0, keepdims=True))
                parts.append(e * (1.0 / jnp.sum(e, axis=0, keepdims=True)))
            probs.append(jnp.concatenate(parts, axis=0).astype(BF16))
            p_ref[sub, pair] = probs[pair]
        for pair in range(PAIRS):
            lo = pair * 128
            v2 = split_heads(qkv_ref[rows, 2 * D + lo : 2 * D + lo + 128], first, second)
            o_ref[rows, lo : lo + 128] = mm_tn(probs[pair], v2).astype(BF16)


def attention_backward(qkv_ref, p_ref, do_ref, dqkv_ref):
    first, second, is_first = lane_masks()

    @pl.loop(0, SUBS)
    def _(sub):
        rows = pl.ds(pl.multiple_of(sub * 128, 128), 128)
        dps, dss = [], []
        for lo in range(0, D, 128):
            v2 = split_heads(qkv_ref[rows, 2 * D + lo : 2 * D + lo + 128], first, second)
            dps.append(mm_nt(v2, do_ref[rows, lo : lo + 128]))
        for pair in range(PAIRS):
            pf = p_ref[sub, pair].astype(F32)
            weighted = pf * dps[pair]
            parts = []
            for half in range(2):
                keys = slice(half * 128, half * 128 + 128)
                parts.append(weighted[keys] - pf[keys] * jnp.sum(weighted[keys], axis=0, keepdims=True))
            dss.append(jnp.concatenate(parts, axis=0).astype(BF16))
        for pair in range(PAIRS):
            lo = pair * 128
            k2 = split_heads(qkv_ref[rows, D + lo : D + lo + 128], first, second)
            dq = mm_tn(dss[pair], k2) * 0.125
            dk2 = mm(dss[pair], qkv_ref[rows, lo : lo + 128]) * 0.125
            dv2 = mm(p_ref[sub, pair], do_ref[rows, lo : lo + 128])
            dqkv_ref[rows, lo : lo + 128] = dq.astype(BF16)
            dqkv_ref[rows, D + lo : D + lo + 128] = jnp.where(is_first, dk2[:128], dk2[128:]).astype(BF16)
            dqkv_ref[rows, 2 * D + lo : 2 * D + lo + 128] = jnp.where(is_first, dv2[:128], dv2[128:]).astype(BF16)


def block_forward(
    h, gains, w, wait, shift, a_ref, qkv_ref, p_ref, o_ref, mid_ref, c_ref, u_ref, gp_ref, done=lambda i: None
):
    wq, wo, wu, wd = w
    a_ref[...] = (normalized(h)[0] * gains[0:1, :]).astype(BF16)
    wait(0)

    @pl.loop(0, 3)
    def _(part):
        cols = lanes(part * D, D)
        qkv_ref[:, cols] = mm(a_ref[...], wq[:, cols]).astype(BF16)

    attention_forward(qkv_ref, o_ref, p_ref, shift)
    done(0)
    wait(1)
    mid = h + mm(o_ref[...], wo[...])
    mid_ref[...] = mid
    c_ref[...] = (normalized(mid)[0] * gains[1:2, :]).astype(BF16)
    done(1)
    wait(2)

    @pl.loop(0, FF // D)
    def _(part):
        cols = lanes(part * D, D)
        u, gp = gelu_pair(mm(c_ref[...], wu[:, cols]))
        u_ref[:, cols] = u.astype(BF16)
        gp_ref[:, cols] = gp.astype(BF16)

    done(2)
    wait(3)
    return mid_ref[...] + mm(u_ref[...], wd[...])


def dz_product(dm, wd, gp_ref, dz_ref):
    @pl.loop(0, FF // D)
    def _(part):
        cols = lanes(part * D, D)
        du = mm_nt(dm, wd[pl.ds(pl.multiple_of(part * D, D), D), :])
        dz_ref[:, cols] = (du * gp_ref[:, cols].astype(F32)).astype(BF16)


def backward_upper(dout, gains, wo, wu, dz_ref, mid_ref, dr_ref, do_ref, dmid_ref):
    hat, scale = normalized(mid_ref[...])
    dc = mm_nt(dz_ref[...], wu[...])
    back, dgain = norm_backward(dc, gains[1:2, :], hat, scale)
    dmid_ref[...] = dout + back
    dr_ref[...] = dmid_ref[...].astype(BF16)
    do_ref[...] = mm_nt(dr_ref[...], wo[...]).astype(BF16)
    return dgain


def backward_lower(h, gains, wq, qkv_ref, p_ref, do_ref, dqkv_ref, dmid_ref):
    attention_backward(qkv_ref, p_ref, do_ref, dqkv_ref)
    da = mm_nt(dqkv_ref[...], wq[...])
    hat, scale = normalized(h)
    back, dgain = norm_backward(da, gains[0:1, :], hat, scale)
    return dmid_ref[...] + back, dgain


def block_backward(dout, h, gains, w, wait, dz_ref, mid_ref, qkv_ref, p_ref, do_ref, dr_ref, dqkv_ref, dmid_ref):
    wq, wo, wu = w
    for i in (2, 1, 0):
        wait(i)
    dgain_two = backward_upper(dout, gains, wo, wu, dz_ref, mid_ref, dr_ref, do_ref, dmid_ref)
    dh, dgain_one = backward_lower(h, gains, wq, qkv_ref, p_ref, do_ref, dqkv_ref, dmid_ref)
    return dh, jnp.concatenate([dgain_one, dgain_two], axis=0)


LANES = D // 128


def fill_lanes(dst, src):
    for b in range(LANES):
        dst[b] = src[:, b * 128 : b * 128 + 128].astype(F32)


def strided_rows(ref, start, rows):
    picked = [ref[b, pl.ds(start, rows, stride=PATCH), :] for b in range(LANES)]
    return jnp.concatenate(picked, axis=1)


def spread_matrix():
    row = lax.broadcasted_iota(jnp.int32, (TILE, TILE // PATCH), 0) // PATCH
    col = lax.broadcasted_iota(jnp.int32, (TILE, TILE // PATCH), 1)
    return jnp.where(row == col, 1.0, 0.0).astype(BF16)


def add_low(a, b):
    return (a.astype(F32) + b.astype(F32)).astype(BF16)


def cost(flops, nbytes):
    return pl.CostEstimate(flops=int(flops), bytes_accessed=int(nbytes), transcendentals=0)


WSCRATCH = {
    "q": pltpu.VMEM((D, 3 * D), BF16),
    "o": pltpu.VMEM((D, D), BF16),
    "u": pltpu.VMEM((D, FF), BF16),
    "d": pltpu.VMEM((FF, D), BF16),
}


CORE, X, Y, ZN, ZF, XY = range(6)
QKV, OUT, UP, DOWN = range(4)
ROWS_OF = (D // 16, D // 16, D // 16, FF // 16)
HALF_OF = (3 * D // 2, D // 2, FF // 2, D // 2)
X_LO = (0, D, 2 * D, 3 * D)
DY_LO = (0, 3 * D // 2, 2 * D, 2 * D + FF // 2)
WIDTH_G = (3 * D + D + FF + D) // 2
ROWS_G = MB * PATCHES
UNIT = 384
MESH_ID = pl.DeviceIdType.MESH


class Net:
    def __init__(self, send, recv, local):
        self.send, self.recv, self.local, self.count, self.local_count = send, recv, local, 0, 0
        self.core = lax.axis_index("section")
        at = lax.axis_index("dp")
        self.x, self.y, self.z = at % 2, (at // 2) % 2, at // 4
        self.z0, self.z1 = self.z % 2, self.z // 2
        z0, z1 = self.z0, self.z1
        spot = lambda x, y, z: {"dp": z * 4 + y * 2 + x}
        self.partner = (
            {"section": 1 - self.core}, spot(1 - self.x, self.y, self.z), spot(self.x, 1 - self.y, self.z),
            spot(self.x, self.y, 1 - z0 + 2 * z1), spot(self.x, self.y, z0 + 2 - 2 * z1),
            spot(1 - self.x, 1 - self.y, self.z),
        )

    def meet(self):
        barrier = pltpu.get_barrier_semaphore()
        for device in self.partner:
            pl.semaphore_signal(barrier, inc=1, device_id=device, device_id_type=MESH_ID)
        pl.semaphore_wait(barrier, len(self.partner))

    def remote(self, src, dst, to):
        n = self.count
        self.count += 1
        return pltpu.make_async_remote_copy(
            src_ref=src, dst_ref=dst, send_sem=self.send.at[n], recv_sem=self.recv.at[n],
            device_id=self.partner[to], device_id_type=MESH_ID,
        )

    def load(self, src, dst):
        n = self.local_count
        self.local_count += 1
        return pltpu.make_async_copy(src, dst, self.local.at[n])

    def on(self, which, fn):
        pl.when(self.core == which)(fn)

    def z_of(self, k):
        return (self.z0 + k % 2) % 2 + 2 * ((self.z1 + k // 2) % 2)


def global_forward_kernel(
    bytes_ref, gains_ref, wp_hbm, wq_hbm, wo_hbm, wu_hbm, wd_hbm,
    own_out, g_out, x_out, start_out, qkv_out, p_out, mid_out, gp_out, pat_out,
    bytes_f32, wp, wq, wo, wu, wd, x_s, start_s, qkv_s, p_s, mid_s, gp_s, pat_s, g_s, psem, wsem, osem, send, recv,
):
    net = Net(send, recv, osem)
    core = net.core
    barrier = pltpu.get_barrier_semaphore()
    pl.semaphore_signal(barrier, inc=1, device_id=net.partner[CORE], device_id_type=MESH_ID)

    def wp_copy(j):
        rows = pl.ds(pl.multiple_of(j * D, D), D)
        return pltpu.make_async_copy(wp_hbm.at[rows, :], wp.at[rows, :], psem.at[j])

    wcopies = [
        pltpu.make_async_copy(src.at[0], dst, wsem.at[i])
        for i, (src, dst) in enumerate(((wq_hbm, wq), (wo_hbm, wo), (wu_hbm, wu), (wd_hbm, wd)))
    ]

    def start_weights():
        for j in range(PATCH):
            wp_copy(j).start()
        for copy in wcopies:
            copy.start()

    net.on(0, start_weights)
    fill_lanes(bytes_f32, bytes_ref)
    start_s[...] = jnp.zeros_like(start_s)

    @pl.loop(0, PATCH)
    def _(j):
        mine = j // (PATCH // 2) == core

        @pl.when((core == 0) | mine)
        def _():
            xj = strided_rows(bytes_f32, j, ROWS_G).astype(BF16)

            @pl.when(core == 0)
            def _():
                wp_copy(j).wait()
                start_s[...] = start_s[...] + mm(xj, wp[pl.ds(pl.multiple_of(j * D, D), D), :])

            @pl.when(mine)
            def _():
                for piece in range(4):
                    xr = 1 - net.x if piece % 2 else net.x
                    yr = 1 - net.y if piece // 2 else net.y
                    pat_s[yr * 2 + xr, j % (PATCH // 2)] = xj[:, piece * 192 : piece * 192 + 192]

    pat_copy = net.load(pat_s, pat_out)
    pat_copy.start()
    pl.semaphore_wait(barrier, 1)
    outs = [
        net.load(*pair) for pair in (
            (start_s, start_out), (qkv_s, qkv_out), (p_s, p_out), (mid_s, mid_out), (gp_s, gp_out), (x_s, x_out),
            (g_s, g_out), (g_s.at[0:PATCHES, :], own_out),
        )
    ]
    give = net.remote(g_s.at[PATCHES:ROWS_G, :], own_out, CORE)

    def work():
        moved = pltpu.roll(start_s[...], 1, 0)
        row = lax.broadcasted_iota(jnp.int32, (ROWS_G, D), 0)
        start_s[...] = jnp.where((row & (PATCHES - 1)) == 0, 0.0, moved)
        outs[0].start()

        def done(i):
            for copy in ((outs[1], outs[2]), (outs[3],), (outs[4], outs[5]))[i]:
                copy.start()

        out = block_forward(
            start_s[...], gains_ref[0], (wq, wo, wu, wd), lambda i: wcopies[i].wait(), 7,
            x_s.at[:, 0:D], qkv_s, p_s, x_s.at[:, D : 2 * D], mid_s,
            x_s.at[:, 2 * D : 3 * D], x_s.at[:, 3 * D : 3 * D + FF], gp_s, done,
        )
        g_s[...] = out.astype(BF16)
        give.start()
        outs[6].start()
        outs[7].start()
        for copy in outs:
            copy.wait()
        give.wait_send()

    net.on(0, work)
    net.on(1, give.wait_recv)
    pat_copy.wait()


def global_forward(states, gains, patch_weight, weights):
    outs = (
        ((PATCHES, D), BF16), ((ROWS_G, D), BF16), ((ROWS_G, XG), BF16), ((ROWS_G, D), F32), ((ROWS_G, 3 * D), BF16),
        ((SUBS, PAIRS, 256, 128), BF16), ((ROWS_G, D), F32), ((ROWS_G, FF), BF16), ((4, PATCH // 2, ROWS_G, 192), BF16),
    )
    vmem = pl.BlockSpec(memory_space=pltpu.VMEM)
    held = [pltpu.VMEM(*o) for o in outs[2:]] + [pltpu.VMEM((ROWS_G, D), BF16)]
    return pl.pallas_call(
        global_forward_kernel,
        name="global_forward",
        out_shape=[sds(*o) for o in outs],
        in_specs=[vmem] * 2 + [ANY] * 5,
        out_specs=[ANY] * len(outs),
        scratch_shapes=[
            pltpu.VMEM((LANES, MB * SEQ, 128), F32), pltpu.VMEM((PATCH * D, D), BF16),
            WSCRATCH["q"], WSCRATCH["o"], WSCRATCH["u"], WSCRATCH["d"], *held,
            pltpu.SemaphoreType.DMA((PATCH,)), pltpu.SemaphoreType.DMA((4,)), pltpu.SemaphoreType.DMA((9,)),
            pltpu.SemaphoreType.DMA((1,)), pltpu.SemaphoreType.DMA((1,)),
        ],
        compiler_params=pltpu.CompilerParams(vmem_limit_bytes=VLIMIT, collective_id=3, has_side_effects=True),
        cost_estimate=cost(6e9, 32e6),
    )(states, gains, patch_weight, *weights)


def global_backward_kernel(
    scal, dg0_ref, dg1_ref, start_ref, mid_ref, qkv_ref, p_ref, gp_ref, gains_ref, wq_hbm, wo_hbm, wu_hbm, wd_hbm,
    dpp_ref, keep_ref, send_ref, dgain_ref,
    dm_s, dz_s, do_s, dr_s, dqkv_s, dmid_s, wq, wo, wu, wd, wsem,
):
    @pl.when(scal[0] == 0)
    def _():
        rows = MB * PATCHES
        wcopies = [
            pltpu.make_async_copy(src.at[0], dst, wsem.at[i])
            for i, (src, dst) in enumerate(((wq_hbm, wq), (wo_hbm, wo), (wu_hbm, wu), (wd_hbm, wd)))
        ]
        for i in (3, 2, 1, 0):
            wcopies[i].start()
        dm_s[0:PATCHES, :] = dg0_ref[...]
        dm_s[PATCHES:, :] = dg1_ref[...]
        wcopies[3].wait()
        dz_product(dm_s[...], wd, gp_ref, dz_s)
        dh, dgain = block_backward(
            dm_s[...].astype(F32), start_ref[...], gains_ref[0], (wq, wo, wu), lambda i: wcopies[i].wait(),
            dz_s, mid_ref, qkv_ref, p_ref, do_s, dr_s, dqkv_s, dmid_s,
        )
        dgain_ref[...] = jnp.zeros_like(dgain_ref)
        dgain_ref[0:2, :] = dgain
        moved = pltpu.roll(dh, rows - 1, 0)
        row = lax.broadcasted_iota(jnp.int32, (rows, D), 0)
        dpp_ref[...] = jnp.where((row & (PATCHES - 1)) == PATCHES - 1, 0.0, moved).astype(BF16)
        for half in range(2):
            def fill(ref):
                lo = 0
                for src, width in ((dqkv_s, 3 * D // 2), (dr_s, D // 2), (dz_s, FF // 2), (dm_s, D // 2)):
                    ref[:, lo : lo + width] = src[:, half * width : half * width + width]
                    lo += width
            pl.when(scal[1] == half)(functools.partial(fill, keep_ref))
            pl.when(scal[1] != half)(functools.partial(fill, send_ref))

    @pl.when(scal[0] != 0)
    def _():
        dgain_ref[...] = jnp.zeros_like(dgain_ref)


def global_backward(scal, dgs, saved, gains, weights):
    rows = MB * PATCHES
    full = lambda *shape: pl.BlockSpec(shape, lambda i, s: (0,) * len(shape), pipeline_mode=pl.Buffered(1))
    width = (3 * D + D + FF + D) // 2
    outs = (((rows, D), BF16), ((rows, width), BF16), ((rows, width), BF16), ((8, D), F32))
    return pl.pallas_call(
        global_backward_kernel,
        name="global_backward",
        out_shape=[sds(*o) for o in outs],
        grid_spec=pltpu.PrefetchScalarGridSpec(
            num_scalar_prefetch=1,
            grid=(1,),
            in_specs=[full(PATCHES, D)] * 2 + [full(*v.shape) for v in saved] + [full(1, 2, D)] + [ANY] * 4,
            out_specs=[full(*o[0]) for o in outs],
            scratch_shapes=[
                pltpu.VMEM((rows, D), BF16), pltpu.VMEM((rows, FF), BF16), pltpu.VMEM((rows, D), BF16),
                pltpu.VMEM((rows, D), BF16), pltpu.VMEM((rows, 3 * D), BF16), pltpu.VMEM((rows, D), F32),
                WSCRATCH["q"], WSCRATCH["o"], WSCRATCH["u"], WSCRATCH["d"],
                pltpu.SemaphoreType.DMA((4,)),
            ],
        ),
        compiler_params=pltpu.CompilerParams(vmem_limit_bytes=VLIMIT),
        cost_estimate=cost(6e9, 24e6),
    )(scal, *dgs, *saved, gains, *weights)


def start_weights(scal, pairs, sems, order):
    step = pl.program_id(0)
    for i in order:
        own, recv, dst = pairs[i]

        @pl.when((step == 0) & (scal[0] == 1))
        def _(own=own, dst=dst, i=i):
            pltpu.make_async_copy(own.at[0], dst, sems.at[i]).start()

        @pl.when((step == 0) & (scal[0] == 0))
        def _(recv=recv, dst=dst, i=i):
            pltpu.make_async_copy(recv.at[0], dst, sems.at[i]).start()

    def wait(i):
        @pl.when(step == 0)
        def _():
            pltpu.make_async_copy(pairs[i][1].at[0], pairs[i][2], sems.at[i]).wait()

    return wait


def live_rows(scal):
    step = pl.program_id(0)
    row = lax.broadcasted_iota(jnp.int32, (TILE, D), 0) + step * TILE
    return row < scal[4]


def local_forward_kernel(
    scal, bytes_ref, cot_ref, g_ref, gains_ref, wq_a, wo_a, wu_a, wd_a, wq_b, wo_b, wu_b, wd_b, gains_b,
    y_ref, dm_ref, a_ref, qkv_ref, p_ref, o_ref, mid_ref, c_ref, u_ref, gp_ref,
    wq, wo, wu, wd, wsem,
):
    pairs = ((wq_a, wq_b, wq), (wo_a, wo_b, wo), (wu_a, wu_b, wu), (wd_a, wd_b, wd))
    wait = start_weights(scal, pairs, wsem, (0, 1, 2, 3))
    gains = jnp.where(scal[0] == 1, gains_ref[0], gains_b[0])
    h = bytes_ref[...].astype(F32) + mm(spread_matrix(), g_ref[...])
    out = block_forward(h, gains, (wq, wo, wu, wd), wait, 3, a_ref, qkv_ref, p_ref, o_ref, mid_ref, c_ref, u_ref, gp_ref)
    live = live_rows(scal)
    y_ref[...] = jnp.where(live, out, 0.0).astype(BF16)
    dm_ref[...] = jnp.where(live, cot_ref[...].astype(F32), 0.0).astype(BF16)


def row_block(*shape):
    return pl.BlockSpec(shape, lambda i, s: (i,) + (0,) * (len(shape) - 1))


def const_block(*shape):
    return pl.BlockSpec(shape, lambda i, s: (0,) * len(shape), pipeline_mode=pl.Buffered(1))


def seq_block():
    return pl.BlockSpec((TILE, D), lambda i, s: (s[0] * TILES + i, 0))


def local_forward(scal, states, cotangent, g_own, gains, weights, gains_b, weights_b):
    outs = (
        ((SEQ, D), BF16), ((SEQ, D), BF16), ((SEQ, D), BF16), ((SEQ, 3 * D), BF16),
        ((SEQ // 128, PAIRS, 256, 128), BF16), ((SEQ, D), BF16), ((SEQ, D), F32), ((SEQ, D), BF16),
        ((SEQ, FF), BF16), ((SEQ, FF), BF16),
    )
    return pl.pallas_call(
        local_forward_kernel,
        name="local_forward",
        out_shape=[sds(*o) for o in outs],
        grid_spec=pltpu.PrefetchScalarGridSpec(
            num_scalar_prefetch=1,
            grid=(TILES,),
            in_specs=[seq_block(), seq_block(), row_block(TILE // PATCH, D), const_block(1, 2, D)]
            + [pl.BlockSpec(memory_space=pltpu.HBM)] * 8 + [const_block(1, 2, D)],
            out_specs=[row_block(o[0][0] // TILES, *o[0][1:]) for o in outs],
            scratch_shapes=[
                WSCRATCH["q"], WSCRATCH["o"], WSCRATCH["u"], WSCRATCH["d"], pltpu.SemaphoreType.DMA((4,)),
            ],
        ),
        compiler_params=pltpu.CompilerParams(vmem_limit_bytes=VLIMIT),
        cost_estimate=cost(14.5e9, 60e6),
    )(scal, states, cotangent, g_own, gains, *weights, *weights_b, gains_b)


def local_dz_kernel(scal, dm_ref, gp_ref, wd_a, wd_b, dz_ref, wd, wsem):
    wait = start_weights(scal, ((wd_a, wd_b, wd),), wsem, (0,))
    wait(0)
    dz_product(dm_ref[...], wd, gp_ref, dz_ref)


def local_dz(scal, dm, gp, wd_a, wd_b):
    return pl.pallas_call(
        local_dz_kernel,
        name="local_dz",
        out_shape=sds((SEQ, FF), BF16),
        grid_spec=pltpu.PrefetchScalarGridSpec(
            num_scalar_prefetch=1,
            grid=(TILES,),
            in_specs=[row_block(TILE, D), row_block(TILE, FF), ANY, ANY],
            out_specs=row_block(TILE, FF),
            scratch_shapes=[WSCRATCH["d"], pltpu.SemaphoreType.DMA((1,))],
        ),
        compiler_params=pltpu.CompilerParams(vmem_limit_bytes=VLIMIT),
        cost_estimate=cost(4.8e9, 18e6),
    )(scal, dm, gp, wd_a, wd_b)


def local_backward_kernel(
    scal, dz_ref, dm_ref, bytes_ref, g_ref, mid_ref, qkv_ref, p_ref, gains_ref,
    wq_a, wo_a, wu_a, wq_b, wo_b, wu_b, gains_b,
    dr_ref, dqkv_ref, dh_ref, dg_ref, dgain_ref,
    do_s, wq, wo, wu, wsem,
):
    pairs = ((wq_a, wq_b, wq), (wo_a, wo_b, wo), (wu_a, wu_b, wu))
    wait = start_weights(scal, pairs, wsem, (2, 1, 0))
    gains = jnp.where(scal[0] == 1, gains_ref[0], gains_b[0])
    h = bytes_ref[...].astype(F32) + mm(spread_matrix(), g_ref[...])
    dh, dgain = block_backward(
        dm_ref[...].astype(F32), h, gains, (wq, wo, wu), wait, dz_ref, mid_ref, qkv_ref, p_ref, do_s, dr_ref, dqkv_ref,
        dh_ref,
    )
    dh_ref[...] = dh
    dg_ref[...] = jnp.sum(dh.reshape(TILE // PATCH, PATCH, D), axis=1).astype(BF16)

    @pl.when(pl.program_id(0) == 0)
    def _():
        dgain_ref[...] = jnp.zeros_like(dgain_ref)

    dgain_ref[0:2, :] += dgain


def local_backward(scal, dz, dm, states, g_own, mid, qkv, p, gains, weights, gains_b, weights_b):
    outs = (
        ((SEQ, D), BF16), ((SEQ, 3 * D), BF16), ((SEQ, D), F32), ((PATCHES, D), BF16), ((8, D), F32),
    )
    return pl.pallas_call(
        local_backward_kernel,
        name="local_backward",
        out_shape=[sds(*o) for o in outs],
        grid_spec=pltpu.PrefetchScalarGridSpec(
            num_scalar_prefetch=1,
            grid=(TILES,),
            in_specs=[
                row_block(TILE, FF), row_block(TILE, D), seq_block(), row_block(TILE // PATCH, D), row_block(TILE, D),
                row_block(TILE, 3 * D), row_block(SUBS, PAIRS, 256, 128), const_block(1, 2, D),
            ] + [ANY] * 6 + [const_block(1, 2, D)],
            out_specs=[row_block(o[0][0] // TILES, *o[0][1:]) for o in outs[:4]] + [const_block(8, D)],
            scratch_shapes=[
                pltpu.VMEM((TILE, D), BF16), WSCRATCH["q"], WSCRATCH["o"], WSCRATCH["u"], pltpu.SemaphoreType.DMA((3,)),
            ],
        ),
        compiler_params=pltpu.CompilerParams(vmem_limit_bytes=VLIMIT),
        cost_estimate=cost(10e9, 50e6),
    )(scal, dz, dm, states, g_own, mid, qkv, p, gains, *weights, *weights_b, gains_b)


def store_shards(scal, total, keep_ref, send_ref, add_refs, order, r, count, z):
    first, second = order
    position = {"x": scal[1], "y": scal[2]}
    for one in range(2):
        for two in range(2):
            at = {first: one ^ position[first], second: two ^ position[second]}
            for k in range(count // 4):
                level = (k ^ scal[3]) * 4 if count == 16 else 0
                shard = level + at["y"] * 2 + at["x"]
                value = total[pl.ds(pl.multiple_of(shard * r, 16), r), :]
                if add_refs is not None:
                    value = value + add_refs[one][two, k].astype(F32)
                (send_ref if one else keep_ref)[two, k] = value.astype(BF16)


def weight_grad_kernel(scal, *refs, parts, order, r, count, has_add, core_zero, shards):
    xs, dys, refs = refs[:parts], refs[parts : 2 * parts], refs[2 * parts :]
    adds = None
    if has_add:
        adds, refs = refs[:2], refs[2:]

    def work():
        value = mm_tn(xs[0][...], dys[0][...])
        for x, dy in zip(xs[1:], dys[1:]):
            value = value + mm_tn(x[...], dy[...])
        if not shards:
            refs[0][...] = value
            return
        keep_ref, send_ref, total = refs
        total[...] = value
        store_shards(scal, total, keep_ref, send_ref, adds, order, r, count, pl.program_id(0))

    if core_zero:
        pl.when(scal[0] == 0)(work)
    else:
        work()


def weight_grad(scal, xs, x_lo, dys, dy_lo, rows, cols, tn, order, add=None, half=None, core_zero=False, shards=True):
    mt, nt = rows // D, cols // tn
    r = rows // 16
    count = 16 if mt == 1 else 4
    depth = xs[0].shape[0]
    kz = 4 if mt == 1 else 1

    def dy_map(m, n, s):
        offset = 0 if half is None else (s[0] if half == "own" else 1 - s[0]) * nt
        return (0, dy_lo // tn + offset + n)

    shard_spec = pl.BlockSpec((2, kz, r, tn), lambda m, n, s: (0, 0 if mt == 1 else m ^ s[3], 0, n))
    if shards:
        out_shape = [sds((2, 4, r, cols), BF16)] * 2
        out_specs = [shard_spec] * 2
        scratch = [pltpu.VMEM((D, tn), F32)]
    else:
        out_shape = sds((rows, cols), F32)
        out_specs = pl.BlockSpec((D, tn), lambda m, n, s: (m, n))
        scratch = []
    return pl.pallas_call(
        functools.partial(
            weight_grad_kernel, parts=len(xs), order=order, r=r, count=count, has_add=add is not None,
            core_zero=core_zero, shards=shards,
        ),
        name="weight_grad",
        out_shape=out_shape,
        grid_spec=pltpu.PrefetchScalarGridSpec(
            num_scalar_prefetch=1,
            grid=(mt, nt),
            in_specs=[pl.BlockSpec((depth, D), lambda m, n, s: (0, x_lo // D + m))] * len(xs)
            + [pl.BlockSpec((depth, tn), dy_map)] * len(xs) + [shard_spec] * (0 if add is None else 2),
            out_specs=out_specs,
            scratch_shapes=scratch,
        ),
        compiler_params=pltpu.CompilerParams(vmem_limit_bytes=VLIMIT),
        cost_estimate=cost(2 * depth * len(xs) * rows * cols, 2 * (depth * (rows + cols) + rows * cols)),
    )(scal, *xs, *dys, *(add or ()))


def patch_grad_kernel(scal, bytes_ref, dpp_ref, *refs, order, shards):
    bytes_f32, total = refs[-2:]

    @pl.when(pl.program_id(0) == 0)
    def _():
        fill_lanes(bytes_f32, bytes_ref)

    byte = scal[0] * (PATCH // 2) + pl.program_id(0)
    x = strided_rows(bytes_f32, byte, MB * PATCHES).astype(BF16)
    value = mm_tn(x, dpp_ref[...])
    if not shards:
        refs[0][...] = value
        return
    total[...] = value
    store_shards(scal, total, refs[0], refs[1], None, order, 192, 4, pl.program_id(0))


def patch_weight_grad(scal, states, dpp, order, shards=True):
    if shards:
        out_shape = [sds((2, 4, 192, D), BF16)] * 2
        out_specs = [pl.BlockSpec((2, 1, 192, D), lambda i, s: (0, i ^ s[3], 0, 0))] * 2
    else:
        out_shape = [sds((PATCH // 2 * D, D), F32)]
        out_specs = [pl.BlockSpec((D, D), lambda i, s: (i, 0))]
    return pl.pallas_call(
        functools.partial(patch_grad_kernel, order=order, shards=shards),
        name="patch_weight_grad",
        out_shape=out_shape,
        grid_spec=pltpu.PrefetchScalarGridSpec(
            num_scalar_prefetch=1,
            grid=(PATCH // 2,),
            in_specs=[const_block(MB * SEQ, D), const_block(MB * PATCHES, D)],
            out_specs=out_specs,
            scratch_shapes=[pltpu.VMEM((LANES, MB * SEQ, 128), F32), pltpu.VMEM((D, D), F32)],
        ),
        compiler_params=pltpu.CompilerParams(vmem_limit_bytes=VLIMIT),
        cost_estimate=cost(1.2e9, 10e6),
    )(scal, states, dpp)


def input_grad_kernel(dpp_ref, dh_ref, wp_hbm, out_ref, acc, wp, psem):
    copies = [
        pltpu.make_async_copy(wp_hbm.at[pl.ds(j * D, D)], wp.at[pl.ds(j * D, D)], psem.at[j]) for j in range(PATCH)
    ]
    for copy in copies:
        copy.start()
    for j in range(PATCH):
        copies[j].wait()
        value = mm_nt(dpp_ref[...], wp[j * D : j * D + D, :])
        for b in range(LANES):
            acc[b, pl.ds(j, PATCHES, stride=PATCH), :] = value[:, b * 128 : b * 128 + 128]
    for b in range(LANES):
        cols = slice(b * 128, b * 128 + 128)
        out_ref[:, cols] = (dh_ref[:, cols] + acc[b]).astype(BF16)


def input_grad_part(dpp_own, dh, patch_weight):
    return pl.pallas_call(
        input_grad_kernel,
        name="input_grad",
        out_shape=sds((SEQ, D), BF16),
        in_specs=[pl.BlockSpec(memory_space=pltpu.VMEM)] * 2 + [ANY],
        out_specs=pl.BlockSpec(memory_space=pltpu.VMEM),
        scratch_shapes=[
            pltpu.VMEM((LANES, SEQ, 128), F32), pltpu.VMEM((PATCH * D, D), BF16), pltpu.SemaphoreType.DMA((PATCH,)),
        ],
        compiler_params=pltpu.CompilerParams(vmem_limit_bytes=VLIMIT),
        cost_estimate=cost(1.2e9, 15e6),
    )(dpp_own, dh, patch_weight)


class Job:
    def __init__(self, weight, lo, width, axes):
        self.weight, self.lo, self.width, self.axes = weight, lo, width, axes
        self.r = 192 if weight is None else ROWS_OF[weight]


class Alloc:
    def __init__(self):
        self.specs = []

    def __call__(self, shape, dtype):
        self.specs.append(pltpu.VMEM(shape, dtype))
        return len(self.specs) - 1


def store_unit(net, total, dst, r, axes, k_tile, cols, add):
    flip = lambda here, other: 1 - here if other else here
    for place in range(4 if k_tile is not None else 16):
        xr, yr = place % 2, place // 2 % 2
        k = place // 4 if k_tile is None else k_tile
        relative = {X: xr, Y: yr, ZN: k % 2, ZF: k // 2}
        shard = flip(net.y, yr) * 2 + flip(net.x, xr)
        if k_tile is None:
            shard = shard + 4 * (flip(net.z0, k % 2) + 2 * flip(net.z1, k // 2))
        index = 0
        for axis in axes:
            index = index * 2 + relative[axis]
        at_dst = (index,) if ZN in axes else (index, relative[ZN])
        at_dst += (slice(None), cols)
        value = total[pl.ds(pl.multiple_of(shard * r, 16), r), :]
        if add:
            value = value + dst[at_dst].astype(F32)
        dst[at_dst] = value.astype(BF16)


def job_buffers(alloc, job, local):
    block = (job.r, job.width) if ZN in job.axes else (2, job.r, job.width)
    count = 2 ** len(job.axes)
    job.own = alloc((count, *block), BF16)
    job.recv = []
    while count > 1:
        count //= 2
        job.recv.append(alloc((count, *block), BF16))
    if local:
        job.peer = alloc((16, *block), BF16)
        job.lf = alloc(block, F32)
        job.lr = alloc(block, F32)


def job_copies(net, b, job, local):
    job.copies = []
    count = 2 ** len(job.axes)
    for axis, recv in zip(job.axes, job.recv):
        job.copies.append(net.remote(b[job.own].at[count // 2 : count], b[recv], axis))
        count //= 2
    if local:
        job.cd = net.remote(b[job.peer], b[job.own], CORE)
        job.c4 = net.remote(b[job.lf], b[job.lr], CORE)


def advance(b, job, i):
    job.copies[i].wait_recv()
    own, recv = b[job.own], b[job.recv[i]]

    @pl.loop(0, 2 ** (len(job.axes) - 1 - i))
    def _(k):
        own[k] = add_low(own[k], recv[k])

    job.copies[i + 1].start()


def last_sum(b, job):
    job.copies[-1].wait_recv()
    return b[job.own][0].astype(F32) + b[job.recv[-1]][0].astype(F32)


def local_sum(net, b, job):
    b[job.lf][...] = last_sum(b, job)
    net.on(0, job.c4.start)


def stage_four(net, b, job, out):
    half = HALF_OF[job.weight]

    def finish():
        job.c4.wait_recv()
        out[:, job.lo : job.lo + job.width] = b[job.lr][...]
        out[:, half + job.lo : half + job.lo + job.width] = b[job.lf][...]

    net.on(1, finish)
    net.on(0, job.c4.wait_send)


def end_job(job):
    for copy in job.copies:
        copy.wait_send()


def local_products(net, b, jobs, mine, xt, total, x_ref, dy_ref):
    buffer = lambda job: b[job.own if mine else job.peer]
    job = jobs[0]
    base = (net.core if mine else 1 - net.core) * HALF_OF[job.weight] + job.lo
    if mine:
        for job in jobs:
            job.cd.wait_recv()
    if job.weight == DOWN:

        @pl.loop(0, 4)
        def _(k):
            xt[...] = x_ref[:, lanes(net.z_of(k) * D, D)].T
            total[...] = mm(xt[...], dy_ref[:, lanes(base, UNIT)])
            for job in jobs:
                part = total.at[:, job.lo : job.lo + job.width]
                store_unit(net, part, buffer(job), job.r, job.axes, k, slice(0, job.width), mine)
    else:
        if x_ref is not None:
            xt[...] = x_ref[...].T

        @pl.loop(0, job.width // UNIT)
        def _(n):
            total[...] = mm(xt[...], dy_ref[:, lanes(base + n * UNIT, UNIT)])
            store_unit(net, total, buffer(job), job.r, job.axes, None, lanes(n * UNIT, UNIT), mine)

    for job in jobs:
        if mine:
            job.copies[0].start()
            job.cd.wait_send()
        else:
            job.cd.start()


def first_plan():
    alloc = Alloc()
    jobs = [
        Job(DOWN, 0, 256, (X, Y, ZN, ZF)), Job(DOWN, 256, 128, (Y, X, ZN, ZF)),
        Job(UP, 0, 768, (X, Y, ZN, ZF)), Job(UP, 768, 768, (X, Y, ZN, ZF)),
    ]
    for job in jobs:
        job_buffers(alloc, job, True)
    s = lambda: None
    s.jobs = jobs
    s.ubuf, s.dz = alloc((SEQ, FF), BF16), alloc((SEQ, FF), BF16)
    s.dm = alloc((SEQ, D), BF16)
    s.xt, s.total = alloc((D, SEQ), BF16), alloc((D, UNIT), F32)
    s.wq, s.wo, s.wu, s.wd = (alloc(w, BF16) for w in ((D, 3 * D), (D, D), (D, FF), (FF, D)))
    s.gp = alloc((2, TILE, FF), BF16)
    s.bytes, s.mid = alloc((2, TILE, D), BF16), alloc((2, TILE, D), F32)
    s.qkv, s.p = alloc((2, TILE, 3 * D), BF16), alloc((2, SUBS, PAIRS, 256, 128), BF16)
    s.dr, s.dqkv, s.dh, s.do = alloc((TILE, D), BF16), alloc((TILE, 3 * D), BF16), alloc((TILE, D), F32), alloc((TILE, D), BF16)
    s.g, s.dg, s.dmg, s.dpp = (alloc((n, D), BF16) for n in (PATCHES, PATCHES, ROWS_G, ROWS_G))
    s.gains = alloc((2, 2, D), F32)
    s.specs = alloc.specs
    return s


def first_kernel(
    u_in, dm_in, c_in, gp_in, states, g_in, mid_in, qkv_in, p_in, gains_own, gains_other,
    wq_own, wo_own, wu_own, wd_own, wq_other, wo_other, wu_other, wd_other,
    start_g, mid_g, qkv_g, p_g, gp_g, pat_in, xg_in,
    out_up, out_down, dr_out, dqkv_out, dh_out, dpp_out, keep_out, send_out, pat_out, xn_out, gain_out,
    *refs, plan,
):
    b, (load_sem, tile_sem, send_sem, recv_sem) = refs[:-4], refs[-4:]
    net = Net(send_sem, recv_sem, load_sem)
    s = plan
    core = net.core
    down0, down1, up0, up1 = s.jobs
    net.meet()
    for job in s.jobs:
        job_copies(net, b, job, True)
    dg_copy = net.remote(b[s.dg], b[s.dmg].at[PATCHES:ROWS_G, :], CORE)
    pat_copies = [net.remote(pat_in.at[i], pat_out.at[i - 1], to) for i, to in ((1, X), (2, Y), (3, XY))]
    xg_copy = net.remote(xg_in, xn_out, ZN)
    net.on(0, xg_copy.start)

    def load(src, dst):
        copy = net.load(src, dst)
        copy.start()
        return copy

    def load_weight(own, other, dst, swap):
        copy = net.load(own.at[0], dst)
        net.on(0 if swap else 1, copy.start)
        if not swap:
            second = net.load(other.at[0], dst)
            net.on(0, second.start)

        def wait():
            if swap:
                net.on(0, copy.wait)
            else:
                net.on(1, copy.wait)
                net.on(0, second.wait)

        return wait

    u_load, dm_load = load(u_in, b[s.ubuf]), load(dm_in, b[s.dm])
    wd_wait = load_weight(wd_own, wd_other, b[s.wd], False)
    small = [load(g_in, b[s.g]), load(gains_own.at[0], b[s.gains].at[0]), load(gains_other.at[0], b[s.gains].at[1])]
    wu_wait = load_weight(wu_own, wu_other, b[s.wu], False)
    wo_wait = load_weight(wo_own, wo_other, b[s.wo], False)
    wq_wait = load_weight(wq_own, wq_other, b[s.wq], False)

    def tile_copies(t, slot, kinds):
        rows = pl.ds(pl.multiple_of(t * TILE, TILE), TILE)
        seq_rows = pl.ds(pl.multiple_of(core * SEQ + t * TILE, TILE), TILE)
        subs = pl.ds(t * SUBS, SUBS)
        table = (
            (gp_in.at[rows, :], b[s.gp].at[slot]), (states.at[seq_rows, :], b[s.bytes].at[slot]),
            (mid_in.at[rows, :], b[s.mid].at[slot]), (qkv_in.at[rows, :], b[s.qkv].at[slot]),
            (p_in.at[subs], b[s.p].at[slot]),
        )
        return [pltpu.make_async_copy(*table[i], tile_sem.at[slot, i]) for i in kinds]

    def store_copies(t):
        rows = pl.ds(pl.multiple_of(t * TILE, TILE), TILE)
        table = ((b[s.dr], dr_out), (b[s.dqkv], dqkv_out), (b[s.dh], dh_out))
        return [pltpu.make_async_copy(src, dst.at[rows, :], tile_sem.at[2, i]) for i, (src, dst) in enumerate(table)]

    for copy in tile_copies(0, 0, (0, 1, 2, 3, 4)):
        copy.start()
    u_load.wait()
    dm_load.wait()
    xt, total = b[s.xt], b[s.total]

    def dz_tiles(first, last):
        @pl.loop(first, last)
        def _(t):
            slot = t % 2
            tile_copies(t, slot, (0,))[0].wait()

            @pl.when(t + 1 < TILES)
            def _():
                tile_copies(t + 1, 1 - slot, (0,))[0].start()

            rows = pl.ds(pl.multiple_of(t * TILE, TILE), TILE)
            dz_product(b[s.dm][rows, :], b[s.wd], b[s.gp].at[slot], b[s.dz].at[rows, :])

    local_products(net, b, [down0, down1], False, xt, total, b[s.ubuf], b[s.dm])
    wd_wait()
    dz_tiles(0, 2)
    local_products(net, b, [down0, down1], True, xt, total, b[s.ubuf], b[s.dm])
    c_part = b[s.ubuf].at[:, 0:D]
    c_load = load(c_in, c_part)
    dz_tiles(2, TILES)
    wd_wait_g = load_weight(wd_own, wd_other, b[s.wd], True)
    c_load.wait()
    local_products(net, b, [up0], False, xt, total, c_part, b[s.dz])
    local_products(net, b, [up1], False, xt, total, None, b[s.dz])
    advance(b, down1, 0)
    local_products(net, b, [up0], True, xt, total, None, b[s.dz])
    local_products(net, b, [up1], True, xt, total, None, b[s.dz])
    for copy in small:
        copy.wait()
    wu_wait()
    wo_wait()
    wq_wait()
    gains = jnp.where(core == 1, b[s.gains][0], b[s.gains][1])
    gain_out[...] = jnp.zeros_like(gain_out)

    def global_loads():
        pairs = (
            (gp_g, b[s.gp].at[0]), (mid_g, b[s.mid].at[0]), (qkv_g, b[s.qkv].at[0]), (p_g, b[s.p].at[0]),
        )
        return [pltpu.make_async_copy(*pair, tile_sem.at[3, i]) for i, pair in enumerate(pairs)]

    @pl.loop(0, TILES)
    def _(t):
        slot = t % 2
        for copy in tile_copies(t, slot, (1, 2, 3, 4)):
            copy.wait()

        @pl.when(t + 1 < TILES)
        def _():
            for copy in tile_copies(t + 1, 1 - slot, (1, 2, 3, 4)):
                copy.start()

        @pl.when((t + 1 == TILES) & (core == 0))
        def _():
            for copy in global_loads():
                copy.start()

        @pl.when(t > 0)
        def _():
            for copy in store_copies(t - 1):
                copy.wait()

        rows = pl.ds(pl.multiple_of(t * TILE, TILE), TILE)
        patch_rows = pl.ds(pl.multiple_of(t * (TILE // PATCH), TILE // PATCH), TILE // PATCH)
        h = b[s.bytes][slot].astype(F32) + mm(spread_matrix(), b[s.g][patch_rows, :])
        dh, dgain = block_backward(
            b[s.dm][rows, :].astype(F32), h, gains, (b[s.wq], b[s.wo], b[s.wu]), lambda i: None,
            b[s.dz].at[rows, :], b[s.mid].at[slot], b[s.qkv].at[slot], b[s.p].at[slot], b[s.do], b[s.dr], b[s.dqkv],
            b[s.dh],
        )
        b[s.dh][...] = dh
        b[s.dg][patch_rows, :] = jnp.sum(dh.reshape(TILE // PATCH, PATCH, D), axis=1).astype(BF16)
        gain_out[2:4, :] += dgain
        for copy in store_copies(t):
            copy.start()

        @pl.when(t == 0)
        def _():
            advance(b, down1, 1)
            advance(b, down0, 0)

        @pl.when(t == 1)
        def _():
            for copy in pat_copies:
                copy.start()
            advance(b, down1, 2)

        @pl.when(t == 2)
        def _():
            local_sum(net, b, down1)
            advance(b, down0, 1)
            advance(b, up0, 0)

        @pl.when(t == 3)
        def _():
            advance(b, down0, 2)
            advance(b, up0, 1)
            advance(b, up1, 0)

    wu_wait_g = load_weight(wu_own, wu_other, b[s.wu], True)
    wo_wait_g = load_weight(wo_own, wo_other, b[s.wo], True)
    wq_wait_g = load_weight(wq_own, wq_other, b[s.wq], True)
    net.on(1, dg_copy.start)
    for copy in store_copies(TILES - 1):
        copy.wait()
    dz_g = b[s.ubuf].at[0:ROWS_G, :]
    wd_wait_g()
    wu_wait_g()
    wo_wait_g()
    wq_wait_g()

    start_load = pltpu.make_async_copy(start_g, b[s.mid].at[1], tile_sem.at[3, 4])

    def global_upper():
        start_load.start()
        for copy in global_loads():
            copy.wait()
        b[s.dmg][0:PATCHES, :] = b[s.dg][...]
        dg_copy.wait_recv()
        dz_product(b[s.dmg][...], b[s.wd], b[s.gp].at[0], dz_g)
        gain_out[1:2, :] = backward_upper(
            b[s.dmg][...].astype(F32), b[s.gains][0], b[s.wo], b[s.wu], dz_g, b[s.mid].at[0], b[s.dr], b[s.do], b[s.dh]
        )

    def global_lower():
        start_load.wait()
        dh, dgain = backward_lower(
            b[s.mid][1], b[s.gains][0], b[s.wq], b[s.qkv].at[0], b[s.p].at[0], b[s.do], b[s.dqkv], b[s.dh]
        )
        gain_out[0:1, :] = dgain
        moved = pltpu.roll(dh, ROWS_G - 1, 0)
        row = lax.broadcasted_iota(jnp.int32, (ROWS_G, D), 0)
        b[s.dpp][...] = jnp.where((row & (PATCHES - 1)) == PATCHES - 1, 0.0, moved).astype(BF16)
        for copy in global_stores():
            copy.start()

    def global_stores():
        copies = [pltpu.make_async_copy(b[s.dpp], dpp_out, tile_sem.at[4, 0])]
        lo, n = 0, 1
        for src, width in ((b[s.dqkv], 3 * D // 2), (b[s.dr], D // 2), (dz_g, FF // 2), (b[s.dmg], D // 2)):
            for out, half in ((keep_out, net.z0), (send_out, 1 - net.z0)):
                copies.append(
                    pltpu.make_async_copy(src.at[:, lanes(half * width, width)], out.at[:, lo : lo + width], tile_sem.at[4, n])
                )
                n += 1
            lo += width
        return copies

    net.on(0, global_upper)
    local_sum(net, b, down0)
    advance(b, up0, 2)
    advance(b, up1, 1)
    net.on(0, global_lower)
    stage_four(net, b, down1, out_down)
    stage_four(net, b, down0, out_down)
    local_sum(net, b, up0)
    advance(b, up1, 2)
    stage_four(net, b, up0, out_up)
    local_sum(net, b, up1)
    net.on(1, dg_copy.wait_send)
    stage_four(net, b, up1, out_up)
    for job in s.jobs:
        end_job(job)
    for copy in pat_copies:
        copy.wait()
    net.on(0, xg_copy.wait)

    def finish():
        for copy in global_stores():
            copy.wait()

    net.on(0, finish)


def first_part(u, dm, c, gp, states, g, mid, qkv, p, gains, gains_other, weights, other, saved, pat, xg):
    plan = first_plan()
    outs = [
        ((D // 16, FF), F32), ((FF // 16, D), F32), ((SEQ, D), BF16), ((SEQ, 3 * D), BF16), ((SEQ, D), F32),
        ((ROWS_G, D), BF16), ((ROWS_G, WIDTH_G), BF16), ((ROWS_G, WIDTH_G), BF16), ((3, PATCH // 2, ROWS_G, 192), BF16), ((ROWS_G, XG), BF16),
        ((8, D), F32),
    ]
    vmem = pl.BlockSpec(memory_space=pltpu.VMEM)
    operands = (u, dm, c, gp, states, g, mid, qkv, p, gains, gains_other, *weights, *other, *saved, pat, xg)
    return pl.pallas_call(
        functools.partial(first_kernel, plan=plan),
        name="first_part",
        out_shape=[sds(*o) for o in outs],
        in_specs=[ANY] * len(operands),
        out_specs=[vmem] * 2 + [ANY] * 8 + [vmem],
        scratch_shapes=plan.specs + [
            pltpu.SemaphoreType.DMA((32,)), pltpu.SemaphoreType.DMA((5, 9)), pltpu.SemaphoreType.DMA((40,)),
            pltpu.SemaphoreType.DMA((40,)),
        ],
        compiler_params=pltpu.CompilerParams(vmem_limit_bytes=63 * 2**20, collective_id=1, has_side_effects=True),
        cost_estimate=cost(35e9, 80e6),
    )(*operands)


def second_plan():
    alloc = Alloc()
    s = lambda: None
    s.local = [Job(QKV, 0, 768, (X, Y, ZN, ZF)), Job(QKV, 768, 384, (X, Y, ZN, ZF)), Job(OUT, 0, 384, (Y, X, ZN, ZF))]
    s.patch = Job(None, 0, D, (ZN, ZF))
    s.glob = [
        Job(DOWN, 0, 384, (Y, X, ZF)), Job(UP, 0, 768, (X, Y, ZF)), Job(UP, 768, 768, (Y, X, ZF)),
        Job(QKV, 0, 768, (Y, X, ZF)), Job(QKV, 768, 384, (Y, X, ZF)), Job(OUT, 0, 384, (Y, X, ZF)),
    ]
    for job in s.local:
        job_buffers(alloc, job, True)
    job_buffers(alloc, s.patch, False)
    for job in s.glob:
        job_buffers(alloc, job, False)
        job.swap = alloc((2, job.r, job.width), BF16)
    s.dqkv = alloc((SEQ, 3 * D), BF16)
    s.a, s.o, s.dr = (alloc((SEQ, D), BF16) for _ in range(3))
    s.xt, s.xo, s.total = alloc((D, SEQ), BF16), alloc((D, SEQ), BF16), alloc((D, UNIT), F32)
    s.pat, s.dpp = alloc((PATCH // 2, 4 * ROWS_G, 192), BF16), alloc((4 * ROWS_G, D), BF16)
    s.xg, s.dy = alloc((2 * ROWS_G, XG), BF16), alloc((2 * ROWS_G, WIDTH_G), BF16)
    s.gains = alloc((11, 8, D), F32)
    s.g, s.spread = alloc((ROWS_G, D), BF16), alloc((2, TILE, D), BF16)
    s.wp, s.acc = alloc((2, D, D), BF16), alloc((LANES, SEQ, 128), F32)
    s.specs = alloc.specs
    return s


def second_kernel(
    pat_own, pat_in, dpp_in, o_in, dr_in, a_in, dqkv_in, xg_in, xn_in, keep_in, send_in, dh_in, wp_in, g_in, y_in,
    gains_in, up_in, down_in,
    out_qkv, out_out, out_up, out_down, out_patch, out_gains, out_mine, out_peer, out_rows, *refs, plan,
):
    b, (load_sem, wp_sem, row_sem, send_sem, recv_sem) = refs[:-5], refs[-5:]
    net = Net(send_sem, recv_sem, load_sem)
    s = plan
    core = net.core
    q0, q1, proj = s.local
    outs = (out_qkv, out_out, out_up, out_down)
    net.meet()
    for job in s.local:
        job_copies(net, b, job, True)
    job_copies(net, b, s.patch, False)
    for job in s.glob:
        job_copies(net, b, job, False)
        job.swap_copy = net.remote(b[job.swap].at[0], b[job.swap].at[1], ZN)
    gain_copies = [
        net.remote(b[s.gains].at[i], b[s.gains].at[i + 6], to) for i, to in enumerate((CORE, X, Y, ZN, ZF))
    ]
    dpp_slots = [b[s.dpp].at[i * ROWS_G : i * ROWS_G + ROWS_G, :] for i in range(4)]
    dpp_gives = [net.remote(dpp_in, dpp_slots[0], CORE)] + [net.remote(slot, slot, CORE) for slot in dpp_slots[1:]]
    dpp_copies = [net.remote(dpp_in, dpp_slots[i], to) for i, to in ((1, X), (2, Y), (3, XY))]
    own_part, next_part = slice(0, ROWS_G), slice(ROWS_G, 2 * ROWS_G)
    dyn_copy = net.remote(send_in, b[s.dy].at[next_part, :], ZN)
    grad_copy = net.remote(out_mine, out_peer, CORE)
    y_copy = net.remote(y_in, out_rows.at[0:SEQ, :], CORE)
    y_own = net.load(y_in, out_rows.at[SEQ : MB * SEQ, :])
    g_load = net.load(g_in, b[s.g])
    dpp_load = net.load(dpp_in, dpp_slots[0])
    global_copies = [net.load(*pair) for pair in (
        (xg_in, b[s.xg].at[own_part, :]), (xn_in, b[s.xg].at[next_part, :]), (keep_in, b[s.dy].at[own_part, :]),
    )]

    def give():
        dpp_gives[0].start()
        for copy in dpp_copies:
            copy.start()
        dyn_copy.start()
        dpp_load.start()
        g_load.start()
        y_copy.start()

    net.on(0, give)
    net.on(1, y_own.start)
    rest = [net.load(*pair) for pair in ((dqkv_in, b[s.dqkv]), (a_in, b[s.a]), (o_in, b[s.o]), (dr_in, b[s.dr]))]
    pat_parts = [pat_own.at[0]] + [pat_in.at[i] for i in range(3)]
    pat_loads = [
        net.load(part, b[s.pat].at[:, i * ROWS_G : i * ROWS_G + ROWS_G, :]) for i, part in enumerate(pat_parts)
    ]
    gain_load = net.load(gains_in, b[s.gains].at[0])
    dh_loads = [net.load(dh_in.at[:, i * 128 : i * 128 + 128], b[s.acc].at[i]) for i in range(LANES)]
    for copy in rest + [gain_load] + pat_loads + dh_loads:
        copy.start()
    net.on(0, lambda: [copy.start() for copy in global_copies] and None)

    def gain_step(i):
        if i == 0:
            gain_load.wait()
        else:
            gain_copies[i - 1].wait_recv()
            b[s.gains][i] = b[s.gains][i - 1] + b[s.gains][i + 5]
        if i < 5:
            gain_copies[i].start()

    def forward_dpp():
        def work():
            for copy, give_copy in zip(dpp_copies, dpp_gives[1:]):
                copy.wait_recv()
                give_copy.start()

        net.on(0, work)

    def patch_products(job):
        for copy in pat_loads:
            copy.wait()
        for i in range(PATCH // 2):
            b[s.xt][i * 192 : i * 192 + 192, :] = b[s.pat][i].T
        net.on(1, lambda: [copy.wait_recv() for copy in dpp_gives[1:]] and None)

        @pl.loop(0, D // UNIT)
        def _(n):
            cols = lanes(n * UNIT, UNIT)
            b[s.total][...] = mm(b[s.xt][...], b[s.dpp][:, cols])
            for k in range(4):
                z = (1 - net.z0 if k // 2 else net.z0) + 2 * (1 - net.z1 if k % 2 else net.z1)
                b[job.own][k, :, cols] = b[s.total][pl.ds(pl.multiple_of(z * 192, 16), 192), :].astype(BF16)
        job.copies[0].start()

    def global_products(job):
        base = DY_LO[job.weight] + job.lo

        def product(cols, n):
            return mm_tn(b[s.xg][:, cols], b[s.dy][:, lanes(base + n * UNIT, UNIT)])

        def work():
            if job.weight == DOWN:

                @pl.loop(0, 4)
                def _(k):
                    b[s.total][...] = product(lanes(X_LO[DOWN] + net.z_of(k) * D, D), 0)
                    store_unit(net, b[s.total], b[job.own], job.r, job.axes, k, slice(0, UNIT), False)
            else:

                @pl.loop(0, job.width // UNIT)
                def _(n):
                    b[s.total][...] = product(slice(X_LO[job.weight], X_LO[job.weight] + D), n)
                    store_unit(net, b[s.total], b[job.own], job.r, job.axes, None, lanes(n * UNIT, UNIT), False)

            job.copies[0].start()

        net.on(0, work)

    def global_advance(job, i):
        net.on(0, lambda: advance(b, job, i))

    def global_sum(job):
        def work():
            value = last_sum(b, job)
            b[job.swap][0] = value[1].astype(BF16)
            job.swap_copy.start()
            outs[job.weight][:, lanes(net.z0 * HALF_OF[job.weight] + job.lo, job.width)] = value[0]

        net.on(0, work)

    def global_end(job):
        def work():
            job.swap_copy.wait_recv()
            cols = lanes((1 - net.z0) * HALF_OF[job.weight] + job.lo, job.width)
            outs[job.weight][:, cols] = b[job.swap][1].astype(F32)

        net.on(0, work)

    def wp_copy(j):
        slot = j % 2
        rows = pl.ds(pl.multiple_of(j * D, D), D)
        return pltpu.make_async_copy(wp_in.at[rows, :], b[s.wp].at[slot], wp_sem.at[slot])

    def input_grads():
        own = pl.ds(pl.multiple_of(core * PATCHES, PATCHES), PATCHES)
        for copy in dh_loads:
            copy.wait()

        @pl.loop(0, PATCH)
        def _(j):
            wp_copy(j).wait()

            @pl.when(j + 1 < PATCH)
            def _():
                wp_copy(j + 1).start()

            value = mm_nt(b[s.dpp][own, :], b[s.wp][j % 2])
            for i in range(LANES):
                places = (i, pl.ds(j, PATCHES, stride=PATCH), slice(None))
                b[s.acc][places] = b[s.acc][places] + value[:, i * 128 : i * 128 + 128]

        for i in range(LANES):
            out_mine[:, i * 128 : i * 128 + 128] = b[s.acc][i].astype(BF16)
        grad_copy.start()

    def first_wait():
        for copy in global_copies:
            copy.wait()
        dyn_copy.wait_recv()

    def spread_copy(i):
        return pltpu.make_async_copy(
            b[s.spread].at[i % 2], out_rows.at[pl.ds(pl.multiple_of(i * TILE, TILE), TILE), :], row_sem.at[i % 2]
        )

    def spread_rows():
        g_load.wait()
        matrix = spread_matrix()

        @pl.loop(0, MB * TILES)
        def _(i):
            @pl.when(i >= 2)
            def _():
                spread_copy(i - 2).wait()

            rows = pl.ds(pl.multiple_of(i * (TILE // PATCH), TILE // PATCH), TILE // PATCH)
            b[s.spread][i % 2] = mm(matrix, b[s.g][rows, :]).astype(BF16)
            spread_copy(i).start()

        for i in (MB * TILES - 2, MB * TILES - 1):
            spread_copy(i).wait()

    wp_copy(0).start()
    gain_step(0)
    g_down, g_up0, g_up1, g_q0, g_q1, g_out = s.glob
    patch = s.patch
    for copy in rest:
        copy.wait()
    xt, xo, total = b[s.xt], b[s.xo], b[s.total]
    local_products(net, b, [q0], False, xt, total, b[s.a], b[s.dqkv])
    local_products(net, b, [q1], False, xt, total, None, b[s.dqkv])
    local_products(net, b, [proj], False, xo, total, b[s.o], b[s.dr])
    net.on(0, dpp_load.wait)
    net.on(1, dpp_gives[0].wait_recv)
    gain_step(1)
    forward_dpp()
    local_products(net, b, [q0], True, xt, total, None, b[s.dqkv])
    local_products(net, b, [q1], True, xt, total, None, b[s.dqkv])
    local_products(net, b, [proj], True, xo, total, None, b[s.dr])
    net.on(0, first_wait)
    global_products(g_down)
    patch_products(patch)
    global_products(g_up0)
    advance(b, proj, 0)
    global_products(g_up1)
    advance(b, q0, 0)
    gain_step(2)
    global_products(g_q0)
    global_products(g_q1)
    global_products(g_out)
    input_grads()
    net.on(0, spread_rows)
    advance(b, q1, 0)
    global_advance(g_down, 0)
    gain_step(3)
    advance(b, patch, 0)
    global_advance(g_up0, 0)
    global_advance(g_up1, 0)
    advance(b, proj, 1)
    advance(b, proj, 2)
    gain_step(4)
    advance(b, q0, 1)
    global_advance(g_down, 1)
    out_patch[...] = last_sum(b, patch)

    def copy_first():
        out_up[...] = up_in[...]
        out_down[...] = down_in[...]

    net.on(1, copy_first)
    global_advance(g_up1, 1)
    local_sum(net, b, proj)
    global_advance(g_q0, 0)
    stage_four(net, b, proj, out_out)
    advance(b, q0, 2)
    global_advance(g_q1, 0)
    global_sum(g_down)
    global_advance(g_q0, 1)
    global_advance(g_out, 0)
    global_advance(g_q1, 1)
    global_sum(g_up1)
    advance(b, q1, 1)
    global_advance(g_out, 1)
    local_sum(net, b, q0)
    global_end(g_down)
    global_advance(g_up0, 1)
    stage_four(net, b, q0, out_qkv)
    global_sum(g_q0)
    gain_step(5)
    out_gains[...] = b[s.gains][5]
    global_end(g_up1)
    global_sum(g_q1)
    advance(b, q1, 2)
    global_sum(g_out)
    global_sum(g_up0)
    global_end(g_q0)
    global_end(g_q1)
    local_sum(net, b, q1)
    global_end(g_out)
    global_end(g_up0)
    stage_four(net, b, q1, out_qkv)
    for job in s.local + [patch]:
        end_job(job)
    grad_copy.wait()

    def end_rows():
        y_own.wait()
        y_copy.wait_recv()

    net.on(1, end_rows)

    for copy in gain_copies:
        copy.wait_send()

    def drain():
        for copy in dpp_gives + dpp_copies + [dyn_copy, y_copy]:
            copy.wait_send()
        for job in s.glob:
            end_job(job)
            job.swap_copy.wait_send()

    net.on(0, drain)


def second_part(*operands):
    plan = second_plan()
    outs = [((ROWS_OF[w], 2 * HALF_OF[w]), F32) for w in (QKV, OUT, UP, DOWN)] + [((192, D), F32), ((8, D), F32)]
    outs += [((SEQ, D), BF16)] * 2 + [((MB * SEQ, D), BF16)]
    vmem = pl.BlockSpec(memory_space=pltpu.VMEM)
    return pl.pallas_call(
        functools.partial(second_kernel, plan=plan),
        name="second_part",
        out_shape=[sds(*o) for o in outs],
        in_specs=[ANY] * (len(operands) - 2) + [vmem] * 2,
        out_specs=[vmem] * (len(outs) - 1) + [ANY],
        scratch_shapes=plan.specs + [
            pltpu.SemaphoreType.DMA((24,)), pltpu.SemaphoreType.DMA((2,)), pltpu.SemaphoreType.DMA((2,)),
            pltpu.SemaphoreType.DMA((64,)), pltpu.SemaphoreType.DMA((64,)),
        ],
        compiler_params=pltpu.CompilerParams(vmem_limit_bytes=63 * 2**20, collective_id=2, has_side_effects=True),
        cost_estimate=cost(15e9, 60e6),
    )(*operands)


def finish_kernel(*refs):
    own, peer = refs[:2]
    sources, grad_out = refs[2:8], refs[8]
    targets, refs = refs[9:15], refs[15:]
    held, wide, staged = refs[0], refs[1], refs[2:8]
    copy_sem, in_sem, out_sem = refs[8:]
    core = lax.axis_index("section")
    loads = [pltpu.make_async_copy(src, held.at[i], in_sem.at[i]) for i, src in enumerate((own, peer))]
    copies_in = [pltpu.make_async_copy(src, mid, copy_sem.at[0, i]) for i, (src, mid) in enumerate(zip(sources, staged))]
    copies_out = [pltpu.make_async_copy(mid, dst, copy_sem.at[1, i]) for i, (mid, dst) in enumerate(zip(staged, targets))]
    for copy in loads + copies_in:
        copy.start()

    def store(i, t):
        place = core if i == 0 else 1 - core
        rows = pl.ds(pl.multiple_of(place * SEQ + t * TILE, TILE), TILE)
        return pltpu.make_async_copy(wide.at[i * TILES + t], grad_out.at[rows, :], out_sem.at[i * TILES + t])

    for i in range(2):
        loads[i].wait()

        @pl.loop(0, TILES)
        def _(t, i=i):
            wide[i * TILES + t] = held[i, pl.ds(pl.multiple_of(t * TILE, TILE), TILE), :].astype(F32)
            store(i, t).start()

    for first, second in zip(copies_in, copies_out):
        first.wait()
        second.start()
    for i in range(2):
        @pl.loop(0, TILES)
        def _(t, i=i):
            store(i, t).wait()

    for copy in copies_out:
        copy.wait()


def finish(own_grad, peer_grad, others):
    outs = [((MB * SEQ, D), F32)] + [(v.shape, v.dtype) for v in others]
    return pl.pallas_call(
        finish_kernel,
        name="finish",
        out_shape=[sds(*o) for o in outs],
        in_specs=[ANY] * (2 + len(others)),
        out_specs=[ANY] * len(outs),
        scratch_shapes=[
            pltpu.VMEM((2, SEQ, D), BF16), pltpu.VMEM((2 * TILES, TILE, D), F32),
            *[pltpu.VMEM(v.shape, v.dtype) for v in others], pltpu.SemaphoreType.DMA((2, len(others))),
            pltpu.SemaphoreType.DMA((2,)), pltpu.SemaphoreType.DMA((2 * TILES,)),
        ],
        compiler_params=pltpu.CompilerParams(vmem_limit_bytes=VLIMIT),
        cost_estimate=cost(1e6, 20e6),
    )(own_grad, peer_grad, *others)


def swap_core(value):
    return lax.ppermute(value, "section", [(0, 1), (1, 0)])


def hop(value, mask, cores):
    size = lax.axis_size("dp")
    if cores == (0, 1):
        return lax.ppermute(value, "dp", [(i, i ^ mask) for i in range(size)])
    pairs = [(c * size + i, c * size + (i ^ mask)) for c in cores for i in range(size)]
    return lax.ppermute(value, ("section", "dp"), pairs)


HOPS = {"x": 1, "y": 2}


def body(states, lengths, patch_weight, w_qkv, w_out, w_up, w_down, gains, cotangent):
    size = lax.axis_size("dp")
    fast = size == 16
    core = lax.axis_index("section")
    at = lax.axis_index("dp")
    mx, my, mz = at % 2, (at // 2) % 2, (at // 4) % 4
    length = jnp.where(core == 0, lengths[0], lengths[1])
    scal = jnp.stack([core, mx, my, mz, length]).astype(jnp.int32)
    weights = (w_qkv, w_out, w_up, w_down)
    other = tuple(swap_core(w) for w in weights)
    gains_other = swap_core(gains)

    g_own, g_all, xg, start, qkv_g, p_g, mid_g, gp_g, pat = global_forward(states, gains, patch_weight, weights)
    y, dm, a, qkv, p, o, mid, c, u, gp = local_forward(
        scal, states, cotangent, g_own, gains, weights, gains_other, other
    )
    saved = (start, mid_g, qkv_g, p_g, gp_g)
    if fast:
        up_l, down_l, dr, dqkv, dh, dpp, dy_keep, dy_send, pat_next, xg_next, gain_parts = first_part(
            u, dm, c, gp, states, g_own, mid, qkv, p, gains, gains_other, weights, other, saved, pat, xg
        )
        *grads, patch_grad, gain_sums, own_grad, peer_grad, section_rows = second_part(
            pat, pat_next, dpp, o, dr, a, dqkv, xg, xg_next, dy_keep, dy_send, dh, patch_weight, g_all, y,
            gain_parts, up_l, down_l
        )
        input_grad, section_rows, patch_grad, *grads = finish(own_grad, peer_grad, (section_rows, patch_grad, *grads))
        outs = tuple(g[None] for g in grads)
    else:
        dz = local_dz(scal, dm, gp, w_down, other[3])
        dr, dqkv, dh, dg, dgain_l = local_backward(
            scal, dz, dm, states, g_own, mid, qkv, p, gains, weights[:3], gains_other, other[:3]
        )
        dpp, dy_keep, dy_send, dgain_g = global_backward(scal, (dg, swap_core(dg)), saved, gains, weights)
        gain_parts = jnp.concatenate([dgain_g[:2], dgain_l[:2], jnp.zeros((4, D), F32)], axis=0)
        dpp = jnp.where(core == 0, dpp, swap_core(dpp))
        own_grad = input_grad_part(jnp.where(core == 0, dpp[:PATCHES], dpp[PATCHES:]), dh, patch_weight)
        peer_grad = swap_core(own_grad)
        input_grad = jnp.where(
            core == 0, jnp.concatenate([own_grad, peer_grad]), jnp.concatenate([peer_grad, own_grad])
        ).astype(F32)
        g_rows = jnp.broadcast_to(g_all[:, None, :], (MB * PATCHES, PATCH, D)).reshape(MB * SEQ, D)
        section_rows = jnp.where(core == 0, g_rows, jnp.concatenate([swap_core(y), y], axis=0))
        gain_sums = lax.psum(gain_parts, ("section", "dp"))
        (patch_half,) = patch_weight_grad(scal, states, dpp, "xy", shards=False)
        patch_grad = lax.psum_scatter(patch_half, "dp", scatter_dimension=0, tiled=True)
        half = D // 2
        swap_halves = lambda keep, send, lo, width: jnp.where(
            mx == 0,
            jnp.concatenate([keep[:, lo : lo + width], send[:, lo : lo + width]], axis=1),
            jnp.concatenate([send[:, lo : lo + width], keep[:, lo : lo + width]], axis=1),
        )

        def whole_grad(x_lo, dy_lo, x, dy, rows, cols):
            dy_g = swap_halves(dy_keep, dy_send, dy_lo, cols // 2)
            glob = weight_grad(scal, [xg], x_lo, [dy_g], 0, rows, cols, 384, "xy", shards=False)
            loc = weight_grad(scal, [x], 0, [dy], 0, rows, cols, 384, "xy", shards=False)
            total = jnp.where(core == 0, glob, loc + swap_core(loc))
            return lax.psum_scatter(total, "dp", scatter_dimension=0, tiled=True)[None]

        outs = (
            whole_grad(0, 0, a, dqkv, D, 3 * D),
            whole_grad(D, 3 * half, o, dr, D, D),
            whole_grad(2 * D, 4 * half, c, dz, D, FF),
            whole_grad(3 * D, 8 * half, u, dm, FF, D),
        )
    share = D // size
    own_gains = jnp.where(core == 0, gain_sums[0:2], gain_sums[2:4])
    gain_grad = lax.dynamic_slice(own_gains, (0, at * share), (2, share))
    return (section_rows[None], input_grad, patch_grad, *outs, gain_grad[None])


def solution(mesh):
    return jax.shard_map(
        body,
        mesh=mesh,
        in_specs=(
            P("dp", None), P("dp"), P(), P("section", None, None), P("section", None, None),
            P("section", None, None), P("section", None, None), P("section", None, None), P("dp", None),
        ),
        out_specs=(
            P("section", "dp", None), P("dp", None), P(("section", "dp"), None), P("section", "dp", None),
            P("section", "dp", None), P("section", "dp", None), P("section", "dp", None), P("section", None, "dp"),
        ),
        check_vma=False,
    )
```
